32 devices in a mesh: fsdp: 2 (over core), ctx: 4 (over y, x), tp: 4 (over z).
Axes of the slice: x: 2, y: 2, z: 4, core: 2. Of those that a mesh axis runs over, the one named last changes fastest.
Arguments:
- x_prompt: bfloat16 [2, 1024, 1024], P('fsdp', 'ctx'), may hold values from -6 to 6
- x_cont: bfloat16 [2, 12, 256, 1024], P('fsdp', 'ctx'), may hold values from -6 to 6
- cont_start: int32 [2, 12], P('fsdp', 'ctx'), may hold values from 512 to 1024
- w_qkv: bfloat16 [1024, 3, 1024], P(('fsdp', 'ctx'), None, 'tp'), may hold values from -0.1875 to 0.1875
- qkv_bias: bfloat16 [3, 1024], P(None, 'tp'), may hold values from -3 to 3
- w_dense: bfloat16 [1024, 1024], P('tp', ('fsdp', 'ctx')), may hold values from -0.75 to 0.75
- dense_bias: bfloat16 [1024], P(('fsdp', 'ctx')), may hold values from -3 to 3
- w_fc1: bfloat16 [1024, 4096], P(('fsdp', 'ctx'), 'tp'), may hold values from -0.1875 to 0.1875
- fc1_bias: bfloat16 [4096], P('tp'), may hold values from -3 to 3
- w_fc2: bfloat16 [4096, 1024], P('tp', ('fsdp', 'ctx')), may hold values from -0.09375 to 0.09375
- fc2_bias: bfloat16 [1024], P(('fsdp', 'ctx')), may hold values from -3 to 3
- ln1_gain: bfloat16 [1024], P(('fsdp', 'ctx')), may hold values from 0.099609375 to 1.8984375
- ln1_bias: bfloat16 [1024], P(('fsdp', 'ctx')), may hold values from -2 to 2
- ln2_gain: bfloat16 [1024], P(('fsdp', 'ctx')), may hold values from 0.099609375 to 1.8984375
- ln2_bias: bfloat16 [1024], P(('fsdp', 'ctx')), may hold values from -2 to 2
- dy_prompt: bfloat16 [2, 1024, 1024], P('fsdp', 'ctx'), may hold values from -6 to 6
- dy_cont: bfloat16 [2, 12, 256, 1024], P('fsdp', 'ctx'), may hold values from -6 to 6
Outputs:
- y_prompt: float32 [2, 1024, 1024], P('fsdp', 'ctx')
- y_cont: float32 [2, 12, 256, 1024], P('fsdp', 'ctx')
- dx_prompt: float32 [2, 1024, 1024], P('fsdp', 'ctx')
- dx_cont: float32 [2, 12, 256, 1024], P('fsdp', 'ctx')
- d_w_qkv: float32 [1024, 3, 1024], P(('fsdp', 'ctx'), None, 'tp')
- d_qkv_bias: float32 [3, 1024], P(None, 'tp')
- d_w_dense: float32 [1024, 1024], P('tp', ('fsdp', 'ctx'))
- d_dense_bias: float32 [1024], P(('fsdp', 'ctx'))
- d_w_fc1: float32 [1024, 4096], P(('fsdp', 'ctx'), 'tp')
- d_fc1_bias: float32 [4096], P('tp')
- d_w_fc2: float32 [4096, 1024], P('tp', ('fsdp', 'ctx'))
- d_fc2_bias: float32 [1024], P(('fsdp', 'ctx'))
- d_ln1_gain: float32 [1024], P(('fsdp', 'ctx'))
- d_ln1_bias: float32 [1024], P(('fsdp', 'ctx'))
- d_ln2_gain: float32 [1024], P(('fsdp', 'ctx'))
- d_ln2_bias: float32 [1024], P(('fsdp', 'ctx'))
The draws below stay inside these ranges and needn't reach their ends.
Inputs may be any that keep to these rules, and one draw needn't show every extreme that they name: `cont_start`: a continuation follows the prompt tokens before its first position.
All inputs are finite; a program needn't handle non-finite values.
Results may differ from the reference program's by a relative error of at most 0.012.
Values may be sent and summed in bfloat16 or wider, within the bound.
A program may use at most 192 MiB of HBM per device.

```python
import math
import jax
import jax.numpy as jnp
from jax import lax

D = 1024
H = 16
HD = 64
ROT = 16
FF = 4096
CONT_LEN = 256
GROUPS = 2
PROMPT = 1024
CONTS = 12


def with_ends(array, key, smallest, high):
    dims = array.shape
    index_at = [jax.random.randint(jax.random.fold_in(key, axis), (), 0, dims[axis]) for axis in range(len(dims))]
    array = array.at[tuple(index_at)].set(smallest)
    longest = dims.index(max(dims))
    index_at[longest] = (index_at[longest] + 1) % dims[longest]
    return array.at[tuple(index_at)].set(high)


def levels(own_key, dims, cuts, low, high):
    def one(position, shards_of):
        heights = jax.random.uniform(jax.random.fold_in(jax.random.fold_in(own_key, 6), position), (shards_of,), jnp.float32, low / len(cuts), high / len(cuts))
        return jnp.repeat(jnp.exp(heights), dims[position] // shards_of).reshape((-1,) + (1,) * (len(dims) - position - 1))

    factor_of = one(*cuts[0])
    for cut in cuts[1:]:
        factor_of = factor_of * one(*cut)
    return factor_of


def noise(stream_key, extent, width, limit, cuts=(), kind=jnp.bfloat16):
    values = width * jax.random.normal(stream_key, extent, jnp.float32)
    if cuts:
        values = values * levels(stream_key, extent, cuts, -0.22, 0.18)
    return jnp.clip(values, -limit, limit).astype(kind)


def setup_inputs(seed: int = 0) -> dict:
    arg_keys = jax.random.split(jax.random.key(seed), 18)
    return {
        "x_prompt": noise(arg_keys[0], (GROUPS, PROMPT, D), 1.0, 6.0, ((0, 2), (1, 4))),
        "x_cont": noise(arg_keys[1], (GROUPS, CONTS, CONT_LEN, D), 1.0, 6.0, ((0, 2), (1, 4))),
        "cont_start": with_ends(jax.random.randint(arg_keys[2], (GROUPS, CONTS), PROMPT // 2, PROMPT + 1), jax.random.fold_in(arg_keys[2], 1), PROMPT // 2, PROMPT).astype(jnp.int32),
        "w_qkv": noise(arg_keys[3], (D, 3, D), D ** -0.5, 0.1875, ((0, 8), (2, 4))),
        "qkv_bias": noise(arg_keys[4], (3, D), 0.5, 3.0, ((1, 4),)),
        "w_dense": noise(arg_keys[5], (D, D), (D // 16) ** -0.5, 0.75, ((0, 4), (1, 8))),
        "dense_bias": noise(arg_keys[6], (D,), 0.5, 3.0, ((0, 8),)),
        "w_fc1": noise(arg_keys[7], (D, FF), D ** -0.5, 0.1875, ((0, 8), (1, 4))),
        "fc1_bias": noise(arg_keys[8], (FF,), 0.5, 3.0, ((0, 4),)),
        "w_fc2": noise(arg_keys[9], (FF, D), FF ** -0.5, 0.09375, ((0, 4), (1, 8))),
        "fc2_bias": noise(arg_keys[10], (D,), 0.5, 3.0, ((0, 8),)),
        "ln1_gain": jnp.clip(1.0 + 0.18 * jax.random.normal(arg_keys[11], (D,), jnp.float32), 0.099609375, 1.8984375).astype(jnp.bfloat16),
        "ln1_bias": noise(arg_keys[12], (D,), 0.3, 2.0, ((0, 8),)),
        "ln2_gain": jnp.clip(1.0 + 0.18 * jax.random.normal(arg_keys[13], (D,), jnp.float32), 0.099609375, 1.8984375).astype(jnp.bfloat16),
        "ln2_bias": noise(arg_keys[14], (D,), 0.3, 2.0, ((0, 8),)),
        "dy_prompt": noise(arg_keys[15], (GROUPS, PROMPT, D), 1.0, 6.0, ((0, 2), (1, 4))),
        "dy_cont": noise(arg_keys[16], (GROUPS, CONTS, CONT_LEN, D), 1.0, 6.0, ((0, 2), (1, 4))),
    }


@jax.custom_vjp
def low(v):
    return lax.optimization_barrier(v.astype(jnp.bfloat16)).astype(jnp.float32)

@jax.custom_vjp
def low_back(v):
    return v

def low_keep(v):
    return (low(v), None)

def low_pass(kept, grad):
    return (grad,)

def back_keep(v):
    return (v, None)

def back_low(kept, grad):
    return (low(grad),)
low.defvjp(low_keep, low_pass)
low_back.defvjp(back_keep, back_low)
EPS = 1e-05
PRECISE = lax.Precision.HIGHEST

def product(left, right):
    return jnp.dot(left, right, precision=PRECISE, preferred_element_type=jnp.float32)

def layer_norm(inputs, norm_gain, norm_shift):
    row_mean = lax.optimization_barrier(jnp.mean(inputs, axis=-1, keepdims=True))
    centered = inputs - row_mean
    variance = lax.optimization_barrier(jnp.mean(centered * centered, axis=-1, keepdims=True))
    return centered * lax.rsqrt(variance + EPS) * norm_gain + norm_shift

def rotary_tables(positions):
    freq_index = jnp.arange(ROT // 2).astype(jnp.float32)
    inverse = jnp.power(10000.0, -2.0 * freq_index / ROT)
    phase = positions.astype(jnp.float32)[..., None] * inverse
    cos_half = jnp.cos(phase)
    sin_half = jnp.sin(phase)
    return (jnp.concatenate([cos_half, cos_half], axis=-1), jnp.concatenate([sin_half, sin_half], axis=-1))

def rotate(inputs, cos_t, sin_t):
    leading = inputs[..., :ROT]
    half_rot = ROT // 2
    turned = jnp.concatenate([-leading[..., half_rot:], leading[..., :half_rot]], axis=-1)
    return jnp.concatenate([leading * cos_t + turned * sin_t, inputs[..., ROT:]], axis=-1)

def attend_block(q_blk, all_keys, values, limit_blk, slot_blk, offs_blk, key_slot, key_offs):
    raw_scores = jnp.einsum('qhd,khd->hqk', q_blk, all_keys, precision=PRECISE)
    scores = low_back(raw_scores * 0.125)
    key_index = jnp.arange(all_keys.shape[0], dtype=jnp.int32)
    near_keys = key_index[None, :] < limit_blk[:, None]
    own_keys = (key_slot[None, :] == slot_blk[:, None]) & (key_offs[None, :] <= offs_blk[:, None])
    allowed = jnp.where((key_index < PROMPT)[None, :], near_keys, own_keys)
    scores = jnp.where(allowed[None], scores, -1e+30)
    highest = lax.optimization_barrier(jnp.max(scores, axis=-1, keepdims=True))
    log_total = highest + jnp.log(lax.optimization_barrier(jnp.sum(jnp.exp(scores - highest), axis=-1, keepdims=True)))
    probs = jnp.exp(scores - log_total)
    return jnp.einsum('hqk,khd->qhd', low(probs), values, precision=PRECISE)

def reference(x_prompt, x_cont, cont_start, w_qkv, qkv_bias, w_dense, dense_bias, w_fc1, fc1_bias, w_fc2, fc2_bias, ln1_gain, ln1_bias, ln2_gain, ln2_bias, dy_prompt, dy_cont):
    groups = x_prompt.shape[0]
    seq_len = PROMPT + CONTS * CONT_LEN
    offsets = jnp.arange(CONT_LEN, dtype=jnp.int32)
    prompt_index = jnp.arange(PROMPT, dtype=jnp.int32)
    slot_ids = jnp.concatenate([jnp.full((PROMPT,), -1, jnp.int32), jnp.repeat(jnp.arange(CONTS, dtype=jnp.int32), CONT_LEN)])
    slot_offs = jnp.concatenate([jnp.zeros((PROMPT,), jnp.int32), jnp.tile(offsets, CONTS)])
    key_limit = jnp.concatenate([jnp.broadcast_to(prompt_index + 1, (groups, PROMPT)), jnp.repeat(cont_start, CONT_LEN, axis=1)], axis=1)
    positions = jnp.concatenate([jnp.broadcast_to(prompt_index, (groups, PROMPT)), (cont_start[:, :, None] + offsets[None, None, :]).reshape(groups, CONTS * CONT_LEN)], axis=1)
    cos_t, sin_t = rotary_tables(positions)
    cos_t = cos_t[:, :, None, :]
    sin_t = sin_t[:, :, None, :]
    block_rows = math.gcd(seq_len, 512)
    blocks = seq_len // block_rows

    def attend_group(group_item):
        queries, all_keys, values, limit_row = group_item

        def one_block(block_item):
            q_blk, limit_blk, slot_blk, offs_blk = block_item
            return jax.checkpoint(attend_block)(q_blk, all_keys, values, limit_blk, slot_blk, offs_blk, slot_ids, slot_offs)
        attended = lax.map(one_block, (queries.reshape(blocks, block_rows, H, HD), limit_row.reshape(blocks, block_rows), slot_ids.reshape(blocks, block_rows), slot_offs.reshape(blocks, block_rows)))
        return attended.reshape(seq_len, H, HD)

    def forward(xp_in, xc_in, wq_in, bq_in, wd_in, bd_in, wu_in, bu_in, wo_in, bo_in, gain_one, shift_one, gain_two, shift_two):
        inputs = jnp.concatenate([xp_in, xc_in.reshape(groups, CONTS * CONT_LEN, D)], axis=1).reshape(groups * seq_len, D)
        norm_one = low(layer_norm(inputs, gain_one, shift_one))
        norm_two = low(layer_norm(inputs, gain_two, shift_two))
        projected = low_back(product(norm_one, wq_in.reshape(D, 3 * D)) + bq_in.reshape(3 * D))
        projected = projected.reshape(groups, seq_len, 3, H, HD)
        queries = low(rotate(projected[:, :, 0], cos_t, sin_t))
        all_keys = low(rotate(projected[:, :, 1], cos_t, sin_t))
        values = low(projected[:, :, 2])
        attended = lax.map(attend_group, (queries, all_keys, values, key_limit))
        attended = low(low_back(attended.reshape(groups * seq_len, D)))
        hidden = low_back(product(norm_two, wu_in) + bu_in)
        active = low(jax.nn.gelu(hidden, approximate=False))
        output = inputs + product(attended, wd_in) + bd_in + product(active, wo_in) + bo_in
        output = output.reshape(groups, seq_len, D)
        return (output[:, :PROMPT], output[:, PROMPT:].reshape(groups, CONTS, CONT_LEN, D))
    float_args = (x_prompt, x_cont, w_qkv, qkv_bias, w_dense, dense_bias, w_fc1, fc1_bias, w_fc2, fc2_bias, ln1_gain, ln1_bias, ln2_gain, ln2_bias)
    float_args = tuple((piece.astype(jnp.float32) for piece in float_args))
    results, pullback = jax.vjp(forward, *float_args)
    gradients = pullback((dy_prompt.astype(jnp.float32), dy_cont.astype(jnp.float32)))
    return (results[0], results[1], gradients[0], gradients[1], gradients[2], gradients[3], gradients[4], gradients[5], gradients[6], gradients[7], gradients[8], gradients[9], gradients[10], gradients[11], gradients[12], gradients[13])
```

```python
import jax
import jax.numpy as jnp
from jax import lax
from jax.sharding import PartitionSpec as P

HD = 64
ROT = 16


EPS = 1e-05


def exact_gelu(values):
    return jax.nn.gelu(values, approximate=False)


def rotary_tables(positions):
    freq_index = jnp.arange(ROT // 2).astype(jnp.float32)
    inverse = jnp.power(10000.0, -2.0 * freq_index / ROT)
    phase = positions.astype(jnp.float32)[..., None] * inverse
    cos_half = jnp.cos(phase)
    sin_half = jnp.sin(phase)
    return (
        jnp.concatenate([cos_half, cos_half], axis=-1),
        jnp.concatenate([sin_half, sin_half], axis=-1),
    )


def rotate(inputs, cos_t, sin_t):
    leading = inputs[..., :ROT]
    half_rot = ROT // 2
    turned = jnp.concatenate([-leading[..., half_rot:], leading[..., :half_rot]], axis=-1)
    return jnp.concatenate([leading * cos_t + turned * sin_t, inputs[..., ROT:]], axis=-1)


def masked_scores(
    queries, all_keys, key_limit, query_slot, query_offs, prompt_len, key_slot, key_offs
):
    raw_scores = jnp.einsum("qhd,khd->hqk", queries, all_keys, preferred_element_type=jnp.float32)
    key_index = jnp.arange(all_keys.shape[0], dtype=jnp.int32)
    near_keys = key_index[None, :] < key_limit[:, None]
    own_keys = (key_slot[None, :] == query_slot[:, None]) & (
        key_offs[None, :] <= query_offs[:, None]
    )
    allowed = jnp.where((key_index < prompt_len)[None, :], near_keys, own_keys)
    return jnp.where(allowed[None], raw_scores * 0.125, -1e30)


def on_device(
    x_prompt,
    x_cont,
    cont_start,
    w_qkv,
    qkv_bias,
    w_dense,
    dense_bias,
    w_fc1,
    fc1_bias,
    w_fc2,
    fc2_bias,
    ln1_gain,
    ln1_bias,
    ln2_gain,
    ln2_bias,
    dy_prompt,
    dy_cont,
):
    gathered = (
        lax.all_gather(w_qkv, ("fsdp", "ctx"), axis=0, tiled=True),
        lax.all_gather(w_dense, ("fsdp", "ctx"), axis=1, tiled=True),
        lax.all_gather(w_fc1, ("fsdp", "ctx"), axis=0, tiled=True),
        lax.all_gather(w_fc2, ("fsdp", "ctx"), axis=1, tiled=True),
        lax.all_gather(dense_bias, ("fsdp", "ctx"), axis=0, tiled=True),
        lax.all_gather(fc2_bias, ("fsdp", "ctx"), axis=0, tiled=True),
        lax.all_gather(ln1_gain, ("fsdp", "ctx"), axis=0, tiled=True),
        lax.all_gather(ln1_bias, ("fsdp", "ctx"), axis=0, tiled=True),
        lax.all_gather(ln2_gain, ("fsdp", "ctx"), axis=0, tiled=True),
        lax.all_gather(ln2_bias, ("fsdp", "ctx"), axis=0, tiled=True),
    )
    qkv_full, dense_full, up_full, down_full = (gathered[0], gathered[1], gathered[2], gathered[3])
    dense_shift = gathered[4].astype(jnp.float32)
    down_shift = gathered[5].astype(jnp.float32)
    gain_one = gathered[6].astype(jnp.float32)
    shift_one = gathered[7].astype(jnp.float32)
    gain_two = gathered[8].astype(jnp.float32)
    shift_two = gathered[9].astype(jnp.float32)
    p_rows = x_prompt.shape[1]
    cont_count = x_cont.shape[1]
    cont_len = x_cont.shape[2]
    model_width = x_prompt.shape[2]
    row_count = p_rows + cont_count * cont_len
    prompt_len = p_rows * lax.axis_size("ctx")
    local_cols = qkv_full.shape[2]
    head_count = local_cols // HD
    piece_index = lax.axis_index("ctx")
    inputs = jnp.concatenate(
        [x_prompt[0], x_cont[0].reshape(cont_count * cont_len, model_width)], axis=0
    ).astype(jnp.float32)
    offsets = jnp.arange(cont_len, dtype=jnp.int32)
    prompt_pos = piece_index * p_rows + jnp.arange(p_rows, dtype=jnp.int32)
    starts = cont_start[0]
    cont_pos = (starts[:, None] + offsets[None, :]).reshape(cont_count * cont_len)
    positions = jnp.concatenate([prompt_pos, cont_pos])
    key_limit = jnp.concatenate([prompt_pos + 1, jnp.repeat(starts, cont_len)])
    own_slot = jnp.repeat(jnp.arange(cont_count, dtype=jnp.int32), cont_len)
    own_offs = jnp.tile(offsets, cont_count)
    query_slot = jnp.concatenate([jnp.full((p_rows,), -1, jnp.int32), own_slot])
    query_offs = jnp.concatenate([jnp.zeros((p_rows,), jnp.int32), own_offs])
    key_slot = jnp.concatenate([jnp.full((prompt_len,), -1, jnp.int32), own_slot])
    key_offs = jnp.concatenate([jnp.zeros((prompt_len,), jnp.int32), own_offs])
    cos_t, sin_t = rotary_tables(positions)
    cos_t = cos_t[:, None, :]
    sin_t = sin_t[:, None, :]
    row_mean = jnp.mean(inputs, axis=-1, keepdims=True)
    centered = inputs - row_mean
    scale = lax.rsqrt(jnp.mean(centered * centered, axis=-1, keepdims=True) + EPS)
    unit = centered * scale
    norm_one = unit * gain_one + shift_one
    norm_two = unit * gain_two + shift_two
    unit_low = unit.astype(jnp.bfloat16)
    ln_one = norm_one.astype(jnp.bfloat16)
    ln_two = norm_two.astype(jnp.bfloat16)
    qkv_flat = qkv_full.reshape(model_width, 3 * local_cols)
    projected = jnp.dot(ln_one, qkv_flat, preferred_element_type=jnp.float32) + qkv_bias.reshape(
        3 * local_cols
    ).astype(jnp.float32)
    projected = projected.reshape(row_count, 3, head_count, HD)
    queries = rotate(projected[:, 0], cos_t, sin_t).astype(jnp.bfloat16)
    keys_own = rotate(projected[:, 1], cos_t, sin_t).astype(jnp.bfloat16)
    values_own = projected[:, 2].astype(jnp.bfloat16)
    prompt_keys, prompt_values = (
        lax.all_gather(keys_own[:p_rows].reshape(p_rows, local_cols), "ctx", axis=0, tiled=True),
        lax.all_gather(values_own[:p_rows].reshape(p_rows, local_cols), "ctx", axis=0, tiled=True),
    )
    all_keys = jnp.concatenate(
        [prompt_keys.reshape(prompt_len, head_count, HD), keys_own[p_rows:]], axis=0
    )
    all_values = jnp.concatenate(
        [prompt_values.reshape(prompt_len, head_count, HD), values_own[p_rows:]], axis=0
    )
    scores = masked_scores(
        queries, all_keys, key_limit, query_slot, query_offs, prompt_len, key_slot, key_offs
    )
    highest = jnp.max(scores, axis=-1, keepdims=True)
    log_total = highest + jnp.log(jnp.sum(jnp.exp(scores - highest), axis=-1, keepdims=True))
    probs_low = jnp.exp(scores - log_total).astype(jnp.bfloat16)
    attended = jnp.einsum("hqk,khd->qhd", probs_low, all_values, preferred_element_type=jnp.float32)
    attended_low = attended.reshape(row_count, local_cols).astype(jnp.bfloat16)
    attn_part = jnp.dot(attended_low, dense_full, preferred_element_type=jnp.float32)
    hidden = jnp.dot(ln_two, up_full, preferred_element_type=jnp.float32) + fc1_bias.astype(
        jnp.float32
    )
    active_low = exact_gelu(hidden).astype(jnp.bfloat16)
    mlp_part = jnp.dot(active_low, down_full, preferred_element_type=jnp.float32)
    mixed = lax.psum((attn_part + mlp_part).astype(jnp.bfloat16), "tp").astype(jnp.float32)
    output = inputs + mixed + dense_shift + down_shift
    grad_out = jnp.concatenate(
        [dy_prompt[0], dy_cont[0].reshape(cont_count * cont_len, model_width)], axis=0
    )
    grad_dense = jnp.dot(attended_low.T, grad_out, preferred_element_type=jnp.float32)
    grad_down = jnp.dot(active_low.T, grad_out, preferred_element_type=jnp.float32)
    grad_shift = jnp.sum(grad_out.astype(jnp.float32), axis=0)
    grad_attended = (
        jnp.dot(grad_out, dense_full.T, preferred_element_type=jnp.float32)
        .astype(jnp.bfloat16)
        .reshape(row_count, head_count, HD)
    )
    scores = masked_scores(
        queries, all_keys, key_limit, query_slot, query_offs, prompt_len, key_slot, key_offs
    )
    probs = jnp.exp(scores - log_total)
    probs_low = probs.astype(jnp.bfloat16)
    grad_probs = jnp.einsum(
        "qhd,khd->hqk", grad_attended, all_values, preferred_element_type=jnp.float32
    )
    inner = jnp.sum(probs * grad_probs, axis=-1, keepdims=True)
    grad_scores = (probs * (grad_probs - inner)).astype(jnp.bfloat16)
    grad_queries = (
        jnp.einsum("hqk,khd->qhd", grad_scores, all_keys, preferred_element_type=jnp.float32)
        * 0.125
    )
    grad_keys = (
        jnp.einsum("hqk,qhd->khd", grad_scores, queries, preferred_element_type=jnp.float32) * 0.125
    )
    grad_values = jnp.einsum(
        "hqk,qhd->khd", probs_low, grad_attended, preferred_element_type=jnp.float32
    )
    prompt_key_grads, prompt_value_grads = (
        lax.psum_scatter(
            grad_keys[:prompt_len].reshape(prompt_len, local_cols).astype(jnp.bfloat16),
            "ctx",
            scatter_dimension=0,
            tiled=True,
        ),
        lax.psum_scatter(
            grad_values[:prompt_len].reshape(prompt_len, local_cols).astype(jnp.bfloat16),
            "ctx",
            scatter_dimension=0,
            tiled=True,
        ),
    )
    grad_keys = jnp.concatenate(
        [prompt_key_grads.reshape(p_rows, head_count, HD).astype(jnp.float32), grad_keys[prompt_len:]], axis=0
    )
    grad_values = jnp.concatenate(
        [prompt_value_grads.reshape(p_rows, head_count, HD).astype(jnp.float32), grad_values[prompt_len:]], axis=0
    )
    grad_projected = jnp.stack(
        [rotate(grad_queries, cos_t, -sin_t), rotate(grad_keys, cos_t, -sin_t), grad_values], axis=1
    )
    grad_proj_low = grad_projected.reshape(row_count, 3 * local_cols).astype(jnp.bfloat16)
    moment_one = jnp.dot(unit_low.T, grad_proj_low, preferred_element_type=jnp.float32)
    grad_qkv_bias = jnp.sum(grad_proj_low.astype(jnp.float32), axis=0)
    grad_norm_one = jnp.dot(grad_proj_low, qkv_flat.T, preferred_element_type=jnp.float32)
    grad_active = jnp.dot(grad_out, down_full.T, preferred_element_type=jnp.float32)
    gelu_back = jax.vjp(exact_gelu, hidden)[1]
    grad_hidden_low = gelu_back(grad_active)[0].astype(jnp.bfloat16)
    moment_two = jnp.dot(unit_low.T, grad_hidden_low, preferred_element_type=jnp.float32)
    grad_up_bias = jnp.sum(grad_hidden_low.astype(jnp.float32), axis=0)
    grad_norm_two = jnp.dot(grad_hidden_low, up_full.T, preferred_element_type=jnp.float32)
    turned = (grad_norm_one * gain_one + grad_norm_two * gain_two).astype(jnp.bfloat16)
    turned = lax.psum(turned, "tp").astype(jnp.float32)
    grad_inputs = grad_out.astype(jnp.float32) + scale * (
        turned
        - jnp.mean(turned, axis=-1, keepdims=True)
        - unit * jnp.mean(turned * unit, axis=-1, keepdims=True)
    )
    both = ("fsdp", "ctx")

    def scatter(array, axis):
        return lax.psum_scatter(
            array.astype(jnp.bfloat16), both, scatter_dimension=axis, tiled=True
        ).astype(jnp.float32)

    own_one = scatter(moment_one, 0)
    own_two = scatter(moment_two, 0)
    d_dense = scatter(grad_dense, 1)
    d_down = scatter(grad_down, 1)
    bias_qkv_total, bias_up_total, shift_total = lax.psum(
        (grad_qkv_bias, grad_up_bias, grad_shift), both
    )
    own_rows = w_qkv.shape[0]
    own_place = (lax.axis_index("fsdp") * lax.axis_size("ctx") + piece_index) * own_rows
    d_shift = lax.dynamic_slice_in_dim(shift_total, own_place, own_rows)
    own_qkv = w_qkv.reshape(own_rows, 3 * local_cols).astype(jnp.float32)
    own_up = w_fc1.astype(jnp.float32)
    small = lax.psum(
        jnp.stack(
            [
                jnp.sum(own_one * own_qkv, axis=1),
                jnp.sum(own_qkv * bias_qkv_total, axis=1),
                jnp.sum(own_two * own_up, axis=1),
                jnp.sum(own_up * bias_up_total, axis=1),
            ]
        ),
        "tp",
    )
    d_qkv = (
        own_one * ln1_gain.astype(jnp.float32)[:, None]
        + ln1_bias.astype(jnp.float32)[:, None] * bias_qkv_total
    ).reshape(own_rows, 3, local_cols)
    d_up = (
        own_two * ln2_gain.astype(jnp.float32)[:, None]
        + ln2_bias.astype(jnp.float32)[:, None] * bias_up_total
    )
    y_prompt = output[:p_rows][None]
    y_cont = output[p_rows:].reshape(1, cont_count, cont_len, model_width)
    dx_prompt = grad_inputs[:p_rows][None]
    dx_cont = grad_inputs[p_rows:].reshape(1, cont_count, cont_len, model_width)
    return (
        y_prompt,
        y_cont,
        dx_prompt,
        dx_cont,
        d_qkv,
        bias_qkv_total.reshape(3, local_cols),
        d_dense,
        d_shift,
        d_up,
        bias_up_total,
        d_down,
        d_shift,
        small[0],
        small[1],
        small[2],
        small[3],
    )


def solution(mesh):
    placed = (
        P("fsdp", "ctx", None),
        P("fsdp", "ctx", None, None),
        P("fsdp", "ctx"),
        P(("fsdp", "ctx"), None, "tp"),
        P(None, "tp"),
        P("tp", ("fsdp", "ctx")),
        P(("fsdp", "ctx")),
        P(("fsdp", "ctx"), "tp"),
        P("tp"),
        P("tp", ("fsdp", "ctx")),
        P(("fsdp", "ctx")),
        P(("fsdp", "ctx")),
        P(("fsdp", "ctx")),
        P(("fsdp", "ctx")),
        P(("fsdp", "ctx")),
        P("fsdp", "ctx", None),
        P("fsdp", "ctx", None, None),
    )
    return jax.shard_map(
        on_device,
        mesh=mesh,
        in_specs=placed,
        out_specs=(
            P("fsdp", "ctx", None),
            P("fsdp", "ctx", None, None),
            P("fsdp", "ctx", None),
            P("fsdp", "ctx", None, None),
            P(("fsdp", "ctx"), None, "tp"),
            P(None, "tp"),
            P("tp", ("fsdp", "ctx")),
            P(("fsdp", "ctx")),
            P(("fsdp", "ctx"), "tp"),
            P("tp"),
            P("tp", ("fsdp", "ctx")),
            P(("fsdp", "ctx")),
            P(("fsdp", "ctx")),
            P(("fsdp", "ctx")),
            P(("fsdp", "ctx")),
            P(("fsdp", "ctx")),
        ),
        check_vma=False,
    )
```

```python
import functools

import jax
import jax.numpy as jnp
import numpy as np
from jax import lax
from jax.experimental import pallas as pl
from jax.experimental.pallas import tpu as pltpu
from jax.sharding import PartitionSpec as P

HD = 64
ROT = 16
EPS = 1e-05
MASKED = -1e30
F32 = jnp.float32
BF16 = jnp.bfloat16
MESH = pl.DeviceIdType.MESH
CHUNK = 128
ERF = (0.254829592, -0.284496736, 1.421413741, -1.453152027, 1.061405429)


def nn(left, right):
    return jnp.dot(left, right, preferred_element_type=F32)


def nt(left, right):
    return lax.dot_general(left, right, (((1,), (1,)), ((), ())), preferred_element_type=F32)


def remote(src, dst, send_sem, recv_sem, device):
    return pltpu.make_async_remote_copy(
        src_ref=src,
        dst_ref=dst,
        send_sem=send_sem,
        recv_sem=recv_sem,
        device_id=device,
        device_id_type=MESH,
    )


def turn(values, cos_t, sin_t):
    lane = lax.broadcasted_iota(jnp.int32, cos_t.shape, 1)
    low_half = lax.rem(lane, HD) < ROT // 2
    pieces = []
    for start in range(0, values.shape[1], 128):
        piece = values[:, start : start + 128]
        up = pltpu.roll(piece, 128 - ROT // 2, 1)
        down = pltpu.roll(piece, ROT // 2, 1)
        pieces.append(piece * cos_t + jnp.where(low_half, up, down) * sin_t)
    return jnp.concatenate(pieces, axis=1) if len(pieces) > 1 else pieces[0]


def layer_kernel(sizes, *refs):
    nf, nc, nt_axis = sizes["nf"], sizes["nc"], sizes["tp"]
    own, cols, ff, width = sizes["own"], sizes["cols"], sizes["ff"], sizes["width"]
    length, slots, total = sizes["length"], sizes["slots"], sizes["total"]
    part, pieces_one, pieces_two = sizes["part"], sizes["pieces_one"], sizes["pieces_two"]
    (
        starts, freq, x_prompt, x_cont, dy_prompt, dy_cont, w_q, w_d, w_u, w_o,
        small, bias_q, bias_u,
        y_out, u_out, dw_out, sums_out, norms_out, small_out,
        xv, dyv, n_t, dy_t, wall, wsh, wd_tmp, wo_tmp, mean_s, scale_s, cos_s, sin_s,
        smallg, qb, kvb, kvp, k_t, v_t, ko_t, vo_t, qm, gm, o_t, dq_t, p_own, ds_own,
        ga, oa, gd, acc, kv_send, kv_recv,
        yb, ya, yt, ub, ua, ut, half_send, half_recv, piece_recv, dw_acc,
        sum_own, sum_f, sum_c, norm_own, norm_in,
        in_sem, small_sem, ws, wr, fs, fr, ls, kvs, kvr, gks, gkr,
        zs, za, zbs, zb, zo, hs, hr, ps, pr, ss, sr, ns, nr, os,
    ) = refs
    f, c, t = lax.axis_index("fsdp"), lax.axis_index("ctx"), lax.axis_index("tp")
    heads = cols // HD
    rows_all = slots * length
    prompt = nc * length
    first = 3 * cols
    edge = first + ff
    shard = f * nc + c
    own_rows = pl.ds(pl.multiple_of(shard * own, own), own)

    def ctx_to(step):
        return (f, lax.rem(c + step, nc), t)

    def ctx_from(step):
        return lax.rem(c + nc - step, nc)

    def mate_to(step):
        return (lax.rem(f + step, nf), c, t)

    def mate_from(step):
        return lax.rem(f + nf - step, nf)

    def tp_to(step):
        return (f, c, lax.rem(t + step, nt_axis))

    upper = lax.div(t, nt_axis // 2)
    inward = (f, c, t + 1 - 2 * upper)
    outward = (f, c, lax.rem(t - 1 + 2 * upper + nt_axis, nt_axis))
    at_end = (t == 0) | (t == nt_axis - 1)
    not_end = (t != 0) & (t != nt_axis - 1)
    in_middle = (t == nt_axis // 2 - 1) | (t == nt_axis // 2)
    not_middle = (t != nt_axis // 2 - 1) & (t != nt_axis // 2)

    loads = [
        (x_prompt, xv.at[pl.ds(0, length)]),
        (x_cont, xv.at[pl.ds(length, rows_all - length)]),
        (dy_prompt, dyv.at[pl.ds(0, length)]),
        (dy_cont, dyv.at[pl.ds(length, rows_all - length)]),
        (w_q.at[0], wsh.at[:, pl.ds(0, cols)]),
        (w_q.at[1], wsh.at[:, pl.ds(cols, cols)]),
        (w_q.at[2], wsh.at[:, pl.ds(2 * cols, cols)]),
        (w_u, wsh.at[:, pl.ds(first, ff)]),
    ]
    turned_in = sizes["turned"]
    if turned_in:
        loads += [(w_d, wsh.at[:, pl.ds(edge, cols)]), (w_o, wsh.at[:, pl.ds(edge + cols, ff)])]
    else:
        loads += [(w_d, wd_tmp), (w_o, wo_tmp)]
    loads = [pltpu.make_async_copy(src, dst, in_sem.at[i]) for i, (src, dst) in enumerate(loads)]
    for i in (4, 5, 6, 0, 1, 8, 7, 9, 2, 3):
        loads[i].start()

    barrier = pltpu.get_barrier_semaphore()
    greeted = [ctx_to(k) for k in range(1, nc)]
    greeted += [mate_to(g) for g in range(1, nf)]
    greeted += [tp_to(k) for k in range(1, nt_axis)]
    for device in greeted:
        pl.semaphore_signal(barrier, inc=1, device_id=device, device_id_type=MESH)
    pl.semaphore_wait(barrier, len(greeted))

    spans = (
        (0, first),
        (edge, cols),
        (first, ff),
        (edge + cols, ff),
    )

    def gather_copy(p, step, g):
        lanes = pl.ds(spans[p][0], spans[p][1])
        if g == 0:
            return remote(
                wsh.at[:, lanes],
                wall.at[own_rows, lanes],
                ws.at[p, step - 1],
                wr.at[p, step - 1],
                ctx_to(step),
            )
        held = f * nc + ctx_from(step)
        rows = pl.ds(pl.multiple_of(held * own, own), own)
        src = wsh.at[:, lanes] if step == 0 else wall.at[rows, lanes]
        return remote(
            src, wall.at[rows, lanes], fs.at[p, step, g - 1], fr.at[p, step, g - 1], mate_to(g)
        )

    def gather_local(p):
        lanes = pl.ds(spans[p][0], spans[p][1])
        return pltpu.make_async_copy(wsh.at[:, lanes], wall.at[own_rows, lanes], ls.at[p])

    def gather_start(p):
        for step in range(1, nc):
            gather_copy(p, step, 0).start()
        for g in range(1, nf):
            gather_copy(p, 0, g).start()
        gather_local(p).start()

    def gather_pass(p):
        for step in range(1, nc):
            gather_copy(p, step, 0).wait_recv()
            for g in range(1, nf):
                gather_copy(p, step, g).start()

    def gather_finish(p):
        gather_local(p).wait()
        for step in range(nc):
            for g in range(1, nf):
                gather_copy(p, step, g).wait_recv()

    def gather_sent(p):
        for step in range(1, nc):
            gather_copy(p, step, 0).wait_send()
        for step in range(nc):
            for g in range(1, nf):
                gather_copy(p, step, g).wait_send()

    def small_copy(step, g):
        if g == 0:
            return remote(
                small, smallg.at[shard], small_sem.at[0, step, 0], small_sem.at[1, step, 0], ctx_to(step)
            )
        held = f * nc + ctx_from(step)
        src = small if step == 0 else smallg.at[held]
        return remote(
            src, smallg.at[held], small_sem.at[0, step, g], small_sem.at[1, step, g], mate_to(g)
        )

    for step in range(1, nc):
        small_copy(step, 0).start()
    for g in range(1, nf):
        small_copy(0, g).start()
    for i in (4, 5, 6):
        loads[i].wait()
    gather_start(0)
    if not turned_in:
        loads[8].wait()
        wsh[:, edge : edge + cols] = wd_tmp[...].astype(F32).T.astype(BF16)
    else:
        loads[8].wait()
    gather_start(1)
    smallg[shard] = small[...]

    loads[0].wait()
    loads[1].wait()

    def statistics(slot, carry):
        rows = pl.ds(pl.multiple_of(slot * length, length), length)
        block = xv[rows, :].astype(F32)
        mean = jnp.mean(block, axis=1, keepdims=True)
        block = block - mean
        scale = lax.rsqrt(jnp.mean(block * block, axis=1, keepdims=True) + EPS)
        mean_s[rows, :] = mean
        scale_s[rows, :] = scale
        n_t[:, rows] = (block * scale).T.astype(BF16)
        before = starts[0, jnp.maximum(slot - 1, 0)]
        base = jnp.where(slot == 0, c * length, before)
        place = base + lax.broadcasted_iota(jnp.int32, (length, 128), 0)
        phase = place.astype(F32) * freq[0:1, :]
        cos_s[rows, :] = jnp.cos(phase)
        sin_s[rows, :] = jnp.sin(phase) * freq[1:2, :]
        return carry

    lax.fori_loop(0, slots, statistics, 0)

    for step in range(1, nc):
        small_copy(step, 0).wait_recv()
        for g in range(1, nf):
            small_copy(step, g).start()
    for step in range(nc):
        for g in range(1, nf):
            small_copy(step, g).wait_recv()
    parts = [smallg[i] for i in range(nf * nc)]
    whole = jnp.concatenate(parts, axis=1)
    small_out[...] = whole
    gain_one, shift_one = small_out[2:3, :], small_out[3:4, :]
    gain_two, shift_two = small_out[4:5, :], small_out[5:6, :]

    def normed(rows, gain, shift):
        block = (xv[rows, :].astype(F32) - mean_s[rows, :]) * scale_s[rows, :]
        return (block * gain + shift).astype(BF16)

    gather_pass(0)
    gather_finish(0)

    def project(slot):
        rows = pl.ds(pl.multiple_of(slot * length, length), length)
        both = nn(normed(rows, gain_one, shift_one), wall[:, 0:first])
        cos_t, sin_t = cos_s[rows, :], sin_s[rows, :]
        query = both[:, 0:cols] + bias_q[0:1, :].astype(F32)
        key = both[:, cols : 2 * cols] + bias_q[1:2, :].astype(F32)
        value = both[:, 2 * cols : first] + bias_q[2:3, :].astype(F32)
        qb[rows, :] = (turn(query, cos_t, sin_t) * 0.125).astype(BF16)
        kvb[rows, 0:cols] = turn(key, cos_t, sin_t).astype(BF16)
        kvb[rows, cols : 2 * cols] = value.astype(BF16)

    project(0)
    mine = pl.ds(pl.multiple_of(c * length, length), length)
    kvp[mine, :] = kvb[0:length, :]

    def kv_copy(step):
        return remote(
            kvb.at[pl.ds(0, length)], kvp.at[mine], kvs.at[step - 1], kvr.at[step - 1], ctx_to(step)
        )

    for step in range(1, nc):
        kv_copy(step).start()
    loads[7].wait()
    gather_start(2)
    loads[9].wait()
    if not turned_in:
        wsh[:, edge + cols : total] = wo_tmp[...].astype(F32).T.astype(BF16)
    gather_start(3)

    lax.fori_loop(1, slots, lambda slot, carry: (project(slot), carry)[1], 0)

    gather_pass(1)
    gather_finish(1)
    loads[2].wait()
    loads[3].wait()

    def back_dense(slot, carry):
        rows = pl.ds(pl.multiple_of(slot * length, length), length)
        block = dyv[rows, :]
        ga[rows, :] = nn(block, wall[:, edge : edge + cols]).astype(BF16)
        dy_t[:, rows] = block.astype(F32).T.astype(BF16)
        return carry

    lax.fori_loop(0, slots, back_dense, 0)

    for step in range(1, nc):
        kv_copy(step).wait_recv()
    k_t[...] = kvp[:, 0:cols].astype(F32).T.astype(BF16)
    v_t[...] = kvp[:, cols : 2 * cols].astype(F32).T.astype(BF16)

    def attend(slot, is_prompt):
        rows = pl.ds(pl.multiple_of(slot * length, length), length)
        head_of = lax.div(lax.broadcasted_iota(jnp.int32, (length, cols), 1), HD)
        query, grad = qb[rows, :], ga[rows, :]
        zero = jnp.zeros_like(query)
        for h in range(heads):
            qm[h * length : (h + 1) * length, :] = jnp.where(head_of == h, query, zero)
            gm[h * length : (h + 1) * length, :] = jnp.where(head_of == h, grad, zero)
        if not is_prompt:
            ko_t[...] = kvb[rows, 0:cols].astype(F32).T.astype(BF16)
            vo_t[...] = kvb[rows, cols : 2 * cols].astype(F32).T.astype(BF16)
            limit = starts[0, slot - 1]

        def one_head(h, carry):
            lanes = pl.ds(pl.multiple_of(h * length, length), length)
            lines = pl.ds(pl.multiple_of(h * HD, HD), HD)
            q_h, g_h = qm[lanes, :], gm[lanes, :]
            scores = nt(kvp[:, 0:cols], q_h)
            key_at = lax.broadcasted_iota(jnp.int32, scores.shape, 0)
            query_at = lax.broadcasted_iota(jnp.int32, scores.shape, 1)
            if is_prompt:
                seen = key_at <= query_at + c * length
            else:
                seen = key_at < limit
            scores = jnp.where(seen, scores, MASKED)
            highest = jnp.max(scores, axis=0, keepdims=True)
            if not is_prompt:
                scores_own = nt(kvb[rows, 0:cols], q_h)
                own_key = lax.broadcasted_iota(jnp.int32, scores_own.shape, 0)
                own_query = lax.broadcasted_iota(jnp.int32, scores_own.shape, 1)
                scores_own = jnp.where(own_key <= own_query, scores_own, MASKED)
                highest = jnp.maximum(highest, jnp.max(scores_own, axis=0, keepdims=True))
            probs = jnp.exp(scores - highest)
            norm = jnp.sum(probs, axis=0, keepdims=True)
            if not is_prompt:
                probs_own = jnp.exp(scores_own - highest)
                norm = norm + jnp.sum(probs_own, axis=0, keepdims=True)
            share = 1.0 / norm
            probs = probs * share
            probs_low = probs.astype(BF16)
            yb[0:prompt, lanes] = probs_low
            grads = nt(kvp[:, cols : 2 * cols], g_h)
            inner = jnp.sum(probs * grads, axis=0, keepdims=True)
            if not is_prompt:
                probs_own = probs_own * share
                own_low = probs_own.astype(BF16)
                p_own[:, lanes] = own_low
                grads_own = nt(kvb[rows, cols : 2 * cols], g_h)
                inner = inner + jnp.sum(probs_own * grads_own, axis=0, keepdims=True)
            back_low = (probs * (grads - inner)).astype(BF16)
            ub[0:prompt, lanes] = back_low
            out_t = nn(v_t[lines, :], probs_low)
            back_q = nn(k_t[lines, :], back_low)
            if not is_prompt:
                back_own = (probs_own * (grads_own - inner)).astype(BF16)
                ds_own[:, lanes] = back_own
                out_t = out_t + nn(vo_t[lines, :], own_low)
                back_q = back_q + nn(ko_t[lines, :], back_own)
            o_t[lines, :] = out_t
            dq_t[lines, :] = back_q
            return carry

        lax.fori_loop(0, heads, one_head, 0)
        cos_t, sin_t = cos_s[rows, :], -sin_s[rows, :]
        oa[rows, 0:cols] = o_t[...].T.astype(BF16)
        gd[rows, 0:cols] = turn(dq_t[...].T * 0.125, cos_t, sin_t).astype(BF16)
        stacked = heads * length
        back_k = nn(ub[0:prompt, 0:stacked], qm[...])
        back_v = nn(yb[0:prompt, 0:stacked], gm[...])
        if is_prompt:
            acc[:, 0:cols] = back_k
            acc[:, cols : 2 * cols] = back_v
        else:
            acc[:, 0:cols] += back_k
            acc[:, cols : 2 * cols] += back_v
            gd[rows, cols : 2 * cols] = turn(nn(ds_own[...], qm[...]), cos_t, sin_t).astype(BF16)
            gd[rows, 2 * cols : first] = nn(p_own[...], gm[...]).astype(BF16)

    attend(0, True)
    lax.fori_loop(1, slots, lambda slot, carry: (attend(slot, False), carry)[1], 0)

    def back_kv_copy(step):
        return remote(
            kv_send.at[step - 1], kv_recv.at[step - 1], gks.at[step - 1], gkr.at[step - 1], ctx_to(step)
        )

    for step in range(1, nc):
        there = pl.ds(pl.multiple_of(lax.rem(c + step, nc) * length, length), length)
        kv_send[step - 1] = acc[there, :].astype(BF16)
        back_kv_copy(step).start()

    chunks = rows_all // CHUNK
    sums = ((yb, ya, yt, y_out), (ub, ua, ut, u_out))

    def line(which, i):
        return sums[which], pl.ds(pl.multiple_of(i * CHUNK, CHUNK), CHUNK)

    def line_out(which, i, middle):
        (mine_ref, from_out, from_in, _), rows = line(which, i)
        target = from_in if middle else from_out
        landed = zb if middle else za
        return remote(
            mine_ref.at[rows], target.at[rows], zs.at[which, i], landed.at[which, i], inward
        )

    def line_home(which, i, middle):
        (_, from_out, from_in, _), rows = line(which, i)
        src = from_out if middle else from_in
        return remote(
            src.at[rows], from_in.at[rows], zbs.at[which, i], zb.at[which, i], outward
        )

    def line_store(which, i, middle):
        (_, from_out, from_in, out), rows = line(which, i)
        src = from_out if middle else from_in
        return pltpu.make_async_copy(src.at[rows], out.at[rows], zo.at[which, i])

    def line_send(which, i):
        @pl.when(in_middle)
        def _():
            line_out(which, i, True).start()

        @pl.when(not_middle)
        def _():
            line_out(which, i, False).start()

    def line_first(which, i):
        @pl.when(at_end)
        def _():
            line_send(which, i)

    def line_add(which, i):
        (mine_ref, from_out, _, _), rows = line(which, i)

        @pl.when(not_end)
        def _():
            line_out(which, i, False).wait_recv()
            mine_ref[rows, :] = (
                mine_ref[rows, :].astype(F32) + from_out[rows, :].astype(F32)
            ).astype(BF16)
            line_send(which, i)

    def line_back(which, i):
        (mine_ref, from_out, from_in, _), rows = line(which, i)

        @pl.when(in_middle)
        def _():
            line_out(which, i, True).wait_recv()
            from_out[rows, :] = (
                mine_ref[rows, :].astype(F32) + from_in[rows, :].astype(F32)
            ).astype(BF16)

            @pl.when(not_end)
            def _():
                line_home(which, i, True).start()

            line_store(which, i, True).start()

        @pl.when(not_middle)
        def _():
            line_home(which, i, False).wait_recv()

            @pl.when(not_end)
            def _():
                line_home(which, i, False).start()

            line_store(which, i, False).start()

    def line_done(which, i):
        line_out(which, i, True).wait_send()
        line_store(which, i, True).wait()

        @pl.when(not_end)
        def _():
            line_home(which, i, True).wait_send()

    for p in (2, 3):
        gather_pass(p)
    for p in (2, 3):
        gather_finish(p)

    def feed(slot, carry):
        rows = pl.ds(pl.multiple_of(slot * length, length), length)
        hidden = nn(normed(rows, gain_two, shift_two), wall[:, first:edge]) + bias_u[...].astype(F32)
        depth = jnp.abs(hidden) * np.float32(0.5**0.5)
        step = 1.0 / (1.0 + np.float32(0.3275911) * depth)
        poly = np.float32(ERF[4])
        for factor in ERF[3::-1]:
            poly = poly * step + np.float32(factor)
        bell = jnp.exp(-(depth * depth))
        tail = 0.5 * (poly * step) * bell
        below = jnp.where(hidden >= 0.0, 1.0 - tail, tail)
        oa[rows, cols : cols + ff] = (hidden * below).astype(BF16)
        slope = below + hidden * (bell * np.float32((2.0 * np.pi) ** -0.5))
        back = nn(dyv[rows, :], wall[:, edge + cols : total])
        gd[rows, first:edge] = (back * slope).astype(BF16)
        yb[rows, :] = nt(oa[rows, :], wall[:, edge:total]).astype(BF16)
        for i in range(length // CHUNK):
            line_first(0, slot * (length // CHUNK) + i)
        return carry

    lax.fori_loop(0, slots, feed, 0)

    grad_kv = acc[mine, :]
    for step in range(1, nc):
        back_kv_copy(step).wait_recv()
        grad_kv = grad_kv + kv_recv[step - 1].astype(F32)
    gd[0:length, cols : 2 * cols] = turn(
        grad_kv[:, 0:cols], cos_s[0:length, :], -sin_s[0:length, :]
    ).astype(BF16)
    gd[0:length, 2 * cols : first] = grad_kv[:, cols : 2 * cols].astype(BF16)

    def back_norms(slot, carry):
        rows = pl.ds(pl.multiple_of(slot * length, length), length)
        toward_x = nt(gd[rows, 0:first], wall[:, 0:first]) * gain_one
        toward_x = toward_x + nt(gd[rows, first:edge], wall[:, first:edge]) * gain_two
        ub[rows, :] = toward_x.astype(BF16)
        for i in range(length // CHUNK):
            line_first(1, slot * (length // CHUNK) + i)
        line_add(0, slot)
        return carry

    lax.fori_loop(0, slots, back_norms, 0)

    ones = jnp.ones((16, rows_all), BF16)
    sum_own[:, 0:edge] = nn(ones, gd[...])[0:8, :]
    sum_own[:, edge : edge + width] = nn(ones, dyv[...])[0:8, :]

    def sum_copy(step, g):
        if g:
            return remote(
                sum_own, sum_f.at[f], ss.at[0, g - 1], sr.at[0, g - 1], mate_to(g)
            )
        return remote(
            sum_own, sum_c.at[c], ss.at[1, step - 1], sr.at[1, step - 1], ctx_to(step)
        )

    sum_f[f] = sum_own[...]
    for g in range(1, nf):
        sum_copy(0, g).start()

    group = nc * own
    split = pieces_one + pieces_two

    def product(p, rows, second):
        lanes = pl.ds(pl.multiple_of(p * part, part), part)
        if second:
            return nn(dy_t[rows, :], oa[:, lanes])
        return nn(n_t[rows, :], gd[:, lanes])

    def half_copy(p, g):
        return remote(
            half_send.at[g - 1, p], half_recv.at[g - 1, p], hs.at[g - 1, p], hr.at[g - 1, p], mate_to(g)
        )

    def piece_copy(p, step):
        rows = pl.ds(pl.multiple_of(lax.rem(c + step, nc) * own, own), own)
        return remote(
            half_recv.at[0, p, rows],
            piece_recv.at[step - 1, p],
            ps.at[step - 1, p],
            pr.at[step - 1, p],
            ctx_to(step),
        )

    def give_half(p, base, second):
        for g in range(1, nf):
            rows = pl.ds(pl.multiple_of(lax.rem(f + g, nf) * group, group), group)
            half_send[g - 1, p] = product(p - base, rows, second).astype(BF16)
            half_copy(p, g).start()

    def keep_half(p, base, second):
        rows = pl.ds(pl.multiple_of(f * group, group), group)
        kept = product(p - base, rows, second)
        for g in range(1, nf):
            half_copy(p, g).wait_recv()
            kept = kept + half_recv[g - 1, p].astype(F32)
        half_recv[0, p] = kept.astype(BF16)
        for step in range(1, nc):
            piece_copy(p, step).start()

    def loop(low, high, body):
        lax.fori_loop(low, high, lambda i, carry: (body(i), carry)[1], 0)

    loop(0, pieces_one, lambda p: give_half(p, 0, False))
    loop(pieces_one, split, lambda p: give_half(p, pieces_one, True))
    loop(slots, chunks, lambda i: line_add(0, i))
    loop(0, chunks // 2, lambda i: line_back(0, i))
    loop(0, pieces_one, lambda p: keep_half(p, 0, False))
    loop(pieces_one, split, lambda p: keep_half(p, pieces_one, True))

    for g in range(1, nf):
        sum_copy(0, g).wait_recv()
        sum_copy(0, g).wait_send()
    held = sum_f[0]
    for i in range(1, nf):
        held = held + sum_f[i]
    sum_own[...] = held
    sum_c[c] = held
    for step in range(1, nc):
        sum_copy(step, 0).start()

    loop(0, chunks // 2, lambda i: line_add(1, i))
    loop(chunks // 2, chunks, lambda i: line_back(0, i))
    loop(chunks // 2, chunks, lambda i: line_add(1, i))

    for step in range(1, nc):
        sum_copy(step, 0).wait_recv()
        sum_copy(step, 0).wait_send()
    held = sum_c[0]
    for i in range(1, nc):
        held = held + sum_c[i]
    sums_out[...] = held

    def settle(p):
        rows = pl.ds(pl.multiple_of(c * own, own), own)
        kept = half_recv[0, p, rows, :].astype(F32)
        for step in range(1, nc):
            piece_copy(p, step).wait_recv()
            kept = kept + piece_recv[step - 1, p].astype(F32)
        dw_acc[:, pl.ds(pl.multiple_of(p * part, part), part)] = kept

    loop(0, split, settle)
    dw_store = pltpu.make_async_copy(dw_acc, dw_out, os.at[0])
    dw_store.start()

    loads_w = wsh[:, 0:edge].astype(F32)
    moment = dw_acc[:, 0:edge] * loads_w
    against = loads_w * sums_out[0:1, 0:edge]
    four = [
        jnp.sum(moment[:, 0:first], axis=1, keepdims=True),
        jnp.sum(against[:, 0:first], axis=1, keepdims=True),
        jnp.sum(moment[:, first:edge], axis=1, keepdims=True),
        jnp.sum(against[:, first:edge], axis=1, keepdims=True),
    ]
    lane = lax.broadcasted_iota(jnp.int32, (own, 128), 1)
    packed = jnp.zeros((own, 128), F32)
    for i, column in enumerate(four):
        packed = jnp.where(lane == i, column, packed)
    norm_own[...] = packed
    norm_in[t] = packed

    def norm_copy(k):
        return remote(norm_own, norm_in.at[t], ns.at[k - 1], nr.at[k - 1], tp_to(k))

    for k in range(1, nt_axis):
        norm_copy(k).start()

    loop(0, chunks, lambda i: line_back(1, i))

    for k in range(1, nt_axis):
        norm_copy(k).wait_recv()
        norm_copy(k).wait_send()
    held = norm_in[0]
    for i in range(1, nt_axis):
        held = held + norm_in[i]
    norms_out[...] = held

    for which in range(2):
        loop(0, chunks, functools.partial(line_done, which))
    for p in range(4):
        gather_sent(p)
    for step in range(1, nc):
        small_copy(step, 0).wait_send()
        kv_copy(step).wait_send()
        back_kv_copy(step).wait_send()
    for step in range(nc):
        for g in range(1, nf):
            small_copy(step, g).wait_send()

    def sent(p):
        for g in range(1, nf):
            half_copy(p, g).wait_send()
        for step in range(1, nc):
            piece_copy(p, step).wait_send()

    loop(0, split, sent)
    dw_store.wait()


def run_layer(sizes, *operands):
    nf, nc, tp = sizes["nf"], sizes["nc"], sizes["tp"]
    own, cols, ff, width = sizes["own"], sizes["cols"], sizes["ff"], sizes["width"]
    length, slots, total = sizes["length"], sizes["slots"], sizes["total"]
    part, split = sizes["part"], sizes["pieces_one"] + sizes["pieces_two"]
    rows = slots * length
    prompt = nc * length
    stacked = cols // HD * length
    edge = 3 * cols + ff
    chunks = rows // CHUNK
    sums = edge + width
    anywhere = pl.BlockSpec(memory_space=pl.ANY)
    vmem = pl.BlockSpec(memory_space=pltpu.VMEM)
    smem = pl.BlockSpec(memory_space=pltpu.SMEM)
    dma = pltpu.SemaphoreType.DMA
    shapes = (
        jax.ShapeDtypeStruct((rows, width), BF16),
        jax.ShapeDtypeStruct((rows, width), BF16),
        jax.ShapeDtypeStruct((own, total), F32),
        jax.ShapeDtypeStruct((8, sums), F32),
        jax.ShapeDtypeStruct((own, 128), F32),
        jax.ShapeDtypeStruct((8, width), F32),
    )
    half = nf - 1
    tmp = (8, 128)
    scratch = [
        pltpu.VMEM((rows, width), BF16),
        pltpu.VMEM((rows, width), BF16),
        pltpu.VMEM((width, rows), BF16),
        pltpu.VMEM((width, rows), BF16),
        pltpu.VMEM((width, total), BF16),
        pltpu.VMEM((own, total), BF16),
        pltpu.VMEM(tmp if sizes["turned"] else (cols, own), BF16),
        pltpu.VMEM(tmp if sizes["turned"] else (ff, own), BF16),
        pltpu.VMEM((rows, 1), F32),
        pltpu.VMEM((rows, 1), F32),
        pltpu.VMEM((rows, 128), F32),
        pltpu.VMEM((rows, 128), F32),
        pltpu.VMEM((nf * nc, 8, own), F32),
        pltpu.VMEM((rows, cols), BF16),
        pltpu.VMEM((rows, 2 * cols), BF16),
        pltpu.VMEM((prompt, 2 * cols), BF16),
        pltpu.VMEM((cols, prompt), BF16),
        pltpu.VMEM((cols, prompt), BF16),
        pltpu.VMEM((cols, length), BF16),
        pltpu.VMEM((cols, length), BF16),
        pltpu.VMEM((stacked, cols), BF16),
        pltpu.VMEM((stacked, cols), BF16),
        pltpu.VMEM((cols, length), F32),
        pltpu.VMEM((cols, length), F32),
        pltpu.VMEM((length, stacked), BF16),
        pltpu.VMEM((length, stacked), BF16),
        pltpu.VMEM((rows, cols), BF16),
        pltpu.VMEM((rows, cols + ff), BF16),
        pltpu.VMEM((rows, edge), BF16),
        pltpu.VMEM((prompt, 2 * cols), F32),
        pltpu.VMEM((nc - 1, length, 2 * cols), BF16),
        pltpu.VMEM((nc - 1, length, 2 * cols), BF16),
    ]
    scratch += [pltpu.VMEM((rows, width), BF16)] * 6
    scratch += [
        pltpu.VMEM((half, split, nc * own, part), BF16),
        pltpu.VMEM((half, split, nc * own, part), BF16),
        pltpu.VMEM((nc - 1, split, own, part), BF16),
        pltpu.VMEM((own, total), F32),
        pltpu.VMEM((8, sums), F32),
        pltpu.VMEM((nf, 8, sums), F32),
        pltpu.VMEM((nc, 8, sums), F32),
        pltpu.VMEM((own, 128), F32),
        pltpu.VMEM((tp, own, 128), F32),
        dma((10,)),
        dma((2, nc, nf)),
        dma((4, nc - 1)),
        dma((4, nc - 1)),
        dma((4, nc, half)),
        dma((4, nc, half)),
        dma((4,)),
        dma((nc - 1,)),
        dma((nc - 1,)),
        dma((nc - 1,)),
        dma((nc - 1,)),
        dma((2, chunks)),
        dma((2, chunks)),
        dma((2, chunks)),
        dma((2, chunks)),
        dma((2, chunks)),
        dma((half, split)),
        dma((half, split)),
        dma((nc - 1, split)),
        dma((nc - 1, split)),
        dma((2, max(half, nc - 1))),
        dma((2, max(half, nc - 1))),
        dma((tp - 1,)),
        dma((tp - 1,)),
        dma((1,)),
    ]
    return pl.pallas_call(
        functools.partial(layer_kernel, sizes),
        out_shape=shapes,
        in_specs=[smem, vmem] + [anywhere] * 8 + [vmem] * 3,
        out_specs=(anywhere, anywhere, anywhere, vmem, vmem, vmem),
        scratch_shapes=scratch,
        compiler_params=pltpu.CompilerParams(
            collective_id=0, has_side_effects=True, vmem_limit_bytes=62 * 1024 * 1024
        ),
        name="layer",
    )(*operands)


def on_device(
    x_prompt,
    x_cont,
    cont_start,
    w_qkv,
    qkv_bias,
    w_dense,
    dense_bias,
    w_fc1,
    fc1_bias,
    w_fc2,
    fc2_bias,
    ln1_gain,
    ln1_bias,
    ln2_gain,
    ln2_bias,
    dy_prompt,
    dy_cont,
):
    length = x_prompt.shape[1]
    conts, cont_len, width = x_cont.shape[1:]
    own, _, cols = w_qkv.shape
    ff = w_fc1.shape[1]
    nf, nc, tp = (lax.axis_size(name) for name in ("fsdp", "ctx", "tp"))
    edge = 3 * cols + ff
    part = 256 if edge % 256 == 0 and (cols + ff) % 256 == 0 else 128
    sizes = {
        "nf": nf,
        "nc": nc,
        "tp": tp,
        "own": own,
        "cols": cols,
        "ff": ff,
        "width": width,
        "length": length,
        "slots": 1 + conts,
        "total": 4 * cols + 2 * ff,
        "part": part,
        "pieces_one": edge // part,
        "pieces_two": (cols + ff) // part,
        "turned": own % 128 != 0,
    }
    turned = [w_dense.T, w_fc2.T] if sizes["turned"] else [w_dense, w_fc2]
    lane = np.arange(128) % HD
    inverse = 10000.0 ** (-2.0 * (lane % (ROT // 2)) / ROT)
    freq = np.zeros((8, 128), np.float32)
    freq[0] = np.where(lane < ROT, inverse, 0.0)
    freq[1] = np.where(lane < ROT // 2, -1.0, 1.0)
    small = jnp.stack([dense_bias, fc2_bias, ln1_gain, ln1_bias, ln2_gain, ln2_bias])
    small = jnp.pad(small.astype(F32), ((0, 2), (0, 0)))
    y_sum, u_sum, dw, sums, norms, small_full = run_layer(
        sizes,
        cont_start,
        jnp.asarray(freq),
        x_prompt[0],
        x_cont.reshape(conts * cont_len, width),
        dy_prompt[0],
        dy_cont.reshape(conts * cont_len, width),
        w_qkv.transpose(1, 0, 2),
        turned[0],
        w_fc1,
        turned[1],
        small,
        qkv_bias,
        fc1_bias.reshape(1, ff),
    )
    shift = small_full[0:1] + small_full[1:2]

    def finish(x, dy, y_rows, u_rows):
        x = x.astype(F32)
        centered = x - jnp.mean(x, axis=-1, keepdims=True)
        scale = lax.rsqrt(jnp.mean(centered * centered, axis=-1, keepdims=True) + EPS)
        unit = centered * scale
        u = u_rows.astype(F32)
        u = u - jnp.mean(u, axis=-1, keepdims=True) - unit * jnp.mean(u * unit, -1, keepdims=True)
        return x + y_rows.astype(F32) + shift, dy.astype(F32) + scale * u

    y_prompt, dx_prompt = finish(x_prompt[0], dy_prompt[0], y_sum[:length], u_sum[:length])
    tokens = conts * cont_len
    y_cont, dx_cont = finish(
        x_cont.reshape(tokens, width), dy_cont.reshape(tokens, width), y_sum[length:], u_sum[length:]
    )
    shape = x_cont.shape
    first = 3 * cols
    bias_q, bias_u = sums[0, :first], sums[0, first:edge]
    gain_one, shift_one = ln1_gain.astype(F32)[:, None], ln1_bias.astype(F32)[:, None]
    gain_two, shift_two = ln2_gain.astype(F32)[:, None], ln2_bias.astype(F32)[:, None]
    d_qkv = (dw[:, :first] * gain_one + shift_one * bias_q).reshape(own, 3, cols)
    d_fc1 = dw[:, first:edge] * gain_two + shift_two * bias_u
    d_dense = dw[:, edge : edge + cols].T
    d_fc2 = dw[:, edge + cols :].T
    place = (lax.axis_index("fsdp") * nc + lax.axis_index("ctx")) * own
    d_shift = lax.dynamic_slice_in_dim(sums[0, edge:], place, own)
    four = norms[:, 0:4].T
    return (
        y_prompt[None],
        y_cont.reshape(shape),
        dx_prompt[None],
        dx_cont.reshape(shape),
        d_qkv,
        bias_q.reshape(3, cols),
        d_dense,
        d_shift,
        d_fc1,
        bias_u,
        d_fc2,
        d_shift,
        four[0],
        four[1],
        four[2],
        four[3],
    )


def solution(mesh):
    both = ("fsdp", "ctx")
    rows = P("fsdp", "ctx", None)
    conts = P("fsdp", "ctx", None, None)
    vector = P(both)
    return jax.shard_map(
        on_device,
        mesh=mesh,
        in_specs=(
            rows,
            conts,
            P("fsdp", "ctx"),
            P(both, None, "tp"),
            P(None, "tp"),
            P("tp", both),
            vector,
            P(both, "tp"),
            P("tp"),
            P("tp", both),
            vector,
            vector,
            vector,
            vector,
            vector,
            rows,
            conts,
        ),
        out_specs=(
            rows,
            conts,
            rows,
            conts,
            P(both, None, "tp"),
            P(None, "tp"),
            P("tp", both),
            vector,
            P(both, "tp"),
            P("tp"),
            P("tp", both),
            vector,
            vector,
            vector,
            vector,
            vector,
        ),
        check_vma=False,
    )
```

```python
import functools

import jax
import jax.numpy as jnp
import numpy as np
from jax import lax
from jax.experimental import pallas as pl
from jax.experimental.pallas import tpu as pltpu
from jax.sharding import PartitionSpec as P

HD = 64
ROT = 16
EPS = 1e-05
MASKED = -1e30
F32 = jnp.float32
BF16 = jnp.bfloat16
MESH = pl.DeviceIdType.MESH
CHUNK = 128
BLOCK = 128
LAG = 2
ERF = (0.254829592, -0.284496736, 1.421413741, -1.453152027, 1.061405429)


def nn(left, right):
    return jnp.dot(left, right, preferred_element_type=F32)


def nt(left, right):
    return lax.dot_general(left, right, (((1,), (1,)), ((), ())), preferred_element_type=F32)


def remote(src, dst, send_sem, recv_sem, device):
    return pltpu.make_async_remote_copy(
        src_ref=src,
        dst_ref=dst,
        send_sem=send_sem,
        recv_sem=recv_sem,
        device_id=device,
        device_id_type=MESH,
    )


def turn(values, cos_t, sin_t):
    lane = lax.broadcasted_iota(jnp.int32, cos_t.shape, 1)
    low_half = lax.rem(lane, HD) < ROT // 2
    pieces = []
    for start in range(0, values.shape[1], 128):
        piece = values[:, start : start + 128]
        up = pltpu.roll(piece, 128 - ROT // 2, 1)
        down = pltpu.roll(piece, ROT // 2, 1)
        pieces.append(piece * cos_t + jnp.where(low_half, up, down) * sin_t)
    return jnp.concatenate(pieces, axis=1) if len(pieces) > 1 else pieces[0]


def layer_kernel(sizes, *refs):
    nf, nc, nt_axis = sizes["nf"], sizes["nc"], sizes["tp"]
    own, cols, ff, width = sizes["own"], sizes["cols"], sizes["ff"], sizes["width"]
    length, slots, total = sizes["length"], sizes["slots"], sizes["total"]
    part, pieces_one, pieces_two = sizes["part"], sizes["pieces_one"], sizes["pieces_two"]
    turned_in = sizes["turned"]
    refs = list(refs)

    def take(count):
        taken = refs[:count]
        del refs[:count]
        return taken

    starts, freq, x_prompt, x_cont, dy_prompt, dy_cont, w_q, w_d, w_u, w_o = take(10)
    vectors = take(1 if turned_in else 6)
    bias_q, bias_up = take(2)
    tot_out, dw_out, sums_out, norms_out, small_out = take(5)
    xv, dyv, n_t, wall, wsh, wd_tmp, wo_tmp = take(7)
    stat_s, cos_s, sin_s, small, smallg, bias_u = take(6)
    qb, kvb, kvp, k_t, v_t, ko_t, vo_t, qm, gm, o_t, dq_t, p_own, ds_own, p_all = take(14)
    ga, oa, gd, acc, kv_recv = take(5)
    part_sum, from_out, from_in, half_send, half_recv, piece_recv, dw_acc = take(7)
    sum_own, sum_f, sum_c, norm_own, norm_in = take(5)
    in_sem, small_sem, ws, wr, fs, fr, ls, kvs, kvr, gks, gkr = take(11)
    zs, za, zbs, zb, zo, hs, hr, ps, pr, ss, sr, ns, nr, os = take(14)
    f, c, t = lax.axis_index("fsdp"), lax.axis_index("ctx"), lax.axis_index("tp")
    heads = cols // HD
    rows_all = slots * length
    prompt = nc * length
    first = 3 * cols
    edge = first + ff
    shard = f * nc + c
    own_rows = pl.ds(pl.multiple_of(shard * own, own), own)

    def ctx_to(step):
        return (f, lax.rem(c + step, nc), t)

    def ctx_from(step):
        return lax.rem(c + nc - step, nc)

    across_x = c + 1 - 2 * lax.rem(c, 2)
    across_y = lax.rem(c + 2, nc)
    corner = lax.rem(across_x + 2, nc)
    peers = (c, across_x, across_y, corner)

    def mate_to(step):
        return (lax.rem(f + step, nf), c, t)

    def mate_from(step):
        return lax.rem(f + nf - step, nf)

    def tp_to(step):
        return (f, c, lax.rem(t + step, nt_axis))

    upper = lax.div(t, nt_axis // 2)
    inward = (f, c, t + 1 - 2 * upper)
    outward = (f, c, lax.rem(t - 1 + 2 * upper + nt_axis, nt_axis))
    at_end = (t == 0) | (t == nt_axis - 1)
    not_end = (t != 0) & (t != nt_axis - 1)
    in_middle = (t == nt_axis // 2 - 1) | (t == nt_axis // 2)
    not_middle = (t != nt_axis // 2 - 1) & (t != nt_axis // 2)

    loads = [
        (x_prompt, xv.at[pl.ds(0, length)]),
        (x_cont, xv.at[pl.ds(length, rows_all - length)]),
        (dy_prompt, dyv.at[pl.ds(0, length)]),
        (dy_cont, dyv.at[pl.ds(length, rows_all - length)]),
        (w_q.at[0], wsh.at[:, pl.ds(0, cols)]),
        (w_q.at[1], wsh.at[:, pl.ds(cols, cols)]),
        (w_q.at[2], wsh.at[:, pl.ds(2 * cols, cols)]),
        (w_u, wsh.at[:, pl.ds(first, ff)]),
    ]
    if turned_in:
        loads += [(w_d, wsh.at[:, pl.ds(edge, cols)]), (w_o, wsh.at[:, pl.ds(edge + cols, ff)])]
    else:
        loads += [(w_d, wd_tmp), (w_o, wo_tmp)]
    loads = [pltpu.make_async_copy(src, dst, in_sem.at[i]) for i, (src, dst) in enumerate(loads)]
    for i in (4, 5, 6, 0, 1, 8, 7, 9, 2, 3):
        loads[i].start()

    barrier = pltpu.get_barrier_semaphore()
    greeted = [ctx_to(k) for k in range(1, nc)]
    greeted += [mate_to(g) for g in range(1, nf)]
    greeted += [tp_to(k) for k in range(1, nt_axis)]
    for device in greeted:
        pl.semaphore_signal(barrier, inc=1, device_id=device, device_id_type=MESH)
    pl.semaphore_wait(barrier, len(greeted))

    spans = (
        (0, first),
        (edge, cols),
        (first, ff),
        (edge + cols, ff),
    )

    half_own = own // 2

    def block(owner, side, size):
        base = owner * size
        if side is None:
            return pl.ds(pl.multiple_of(base, size), size)
        return pl.ds(pl.multiple_of(base + side * (size // 2), size // 2), size // 2)

    routes = ((0, 0, 1), (0, 1, 2), (0, 1, 1), (0, 0, 2), (1, 0, 2), (2, 1, 1))
    lands = ((1, 0), (2, 1), (1, 1), (2, 0), (3, 0), (3, 1))

    def ctx_copy(route, source, target, size, send_sem, recv_sem):
        owner, side, to = routes[route]
        rows = block(peers[owner], side, size)
        src = source(owner, side, rows)
        return remote(src, target(rows), send_sem, recv_sem, (f, peers[to], t))

    def lanes_of(p):
        return pl.ds(spans[p][0], spans[p][1])

    def gather_copy(p, route):
        def source(owner, side, rows):
            if owner == 0:
                return wsh.at[pl.ds(side * half_own, half_own), lanes_of(p)]
            return wall.at[pl.ds(rows.start + f * nc * own, half_own), lanes_of(p)]

        def target(rows):
            return wall.at[pl.ds(rows.start + f * nc * own, half_own), lanes_of(p)]

        return ctx_copy(route, source, target, own, ws.at[p, route], wr.at[p, route])

    def mate_copy(p, peer, g):
        rows = block(f * nc + peers[peer], None, own)
        src = wsh.at[:, lanes_of(p)] if peer == 0 else wall.at[rows, lanes_of(p)]
        return remote(
            src,
            wall.at[rows, lanes_of(p)],
            fs.at[p, peer, g - 1],
            fr.at[p, peer, g - 1],
            mate_to(g),
        )

    def gather_local(p):
        return pltpu.make_async_copy(
            wsh.at[:, lanes_of(p)], wall.at[own_rows, lanes_of(p)], ls.at[p]
        )

    def gather_start(p):
        for route in range(4):
            gather_copy(p, route).start()
        for g in range(1, nf):
            mate_copy(p, 0, g).start()
        gather_local(p).start()

    def gather_relay(p):
        for arrived, route in ((0, 4), (1, 5)):
            gather_copy(p, arrived).wait_recv()
            gather_copy(p, route).start()

    def gather_pass(p):
        for peer, rest in ((1, (2,)), (2, (3,)), (3, (4, 5))):
            for route in rest:
                gather_copy(p, route).wait_recv()
            for g in range(1, nf):
                mate_copy(p, peer, g).start()

    def gather_finish(p):
        gather_local(p).wait()
        for peer in range(nc):
            for g in range(1, nf):
                mate_copy(p, peer, g).wait_recv()

    def gather_sent(p):
        for route in range(6):
            gather_copy(p, route).wait_send()
        for peer in range(nc):
            for g in range(1, nf):
                mate_copy(p, peer, g).wait_send()

    def small_copy(step, g):
        if g == 0:
            return remote(
                small, smallg.at[shard], small_sem.at[0, step, 0], small_sem.at[1, step, 0], ctx_to(step)
            )
        held = f * nc + ctx_from(step)
        src = small if step == 0 else smallg.at[held]
        return remote(
            src, smallg.at[held], small_sem.at[0, step, g], small_sem.at[1, step, g], mate_to(g)
        )

    if turned_in:
        small[...] = vectors[0][...]
    else:
        small[...] = jnp.zeros_like(small)
        for i, vector in enumerate(vectors):
            small[i : i + 1, :] = vector[...].astype(F32).reshape(1, own)
    bias_u[...] = bias_up[...].astype(F32).reshape(1, ff)
    for step in range(1, nc):
        small_copy(step, 0).start()
    for g in range(1, nf):
        small_copy(0, g).start()
    for i in (4, 5, 6):
        loads[i].wait()
    gather_start(0)
    if not turned_in:
        loads[8].wait()
        wsh[:, edge : edge + cols] = wd_tmp[...].astype(F32).T.astype(BF16)
    else:
        loads[8].wait()
    gather_start(1)
    smallg[shard] = small[...]

    loads[0].wait()
    loads[1].wait()

    def statistics(slot):
        rows = pl.ds(pl.multiple_of(slot * length, length), length)
        block_x = xv[rows, :].astype(F32)
        mean = jnp.mean(block_x, axis=1, keepdims=True)
        block_x = block_x - mean
        scale = lax.rsqrt(jnp.mean(block_x * block_x, axis=1, keepdims=True) + EPS)
        stat_s[rows, 0:1] = mean
        stat_s[rows, 1:2] = scale
        n_t[:, rows] = (block_x * scale).T.astype(BF16)
        before = starts[0, jnp.maximum(slot - 1, 0)]
        base = jnp.where(slot == 0, c * length, before)
        place = base + lax.broadcasted_iota(jnp.int32, (length, 128), 0)
        phase = place.astype(F32) * freq[0:1, :]
        cos_s[rows, :] = jnp.cos(phase)
        sin_s[rows, :] = jnp.sin(phase) * freq[1:2, :]

    def loop(low, high, body):
        lax.fori_loop(low, high, lambda i, carry: (body(i), carry)[1], 0)

    statistics(0)
    gather_relay(0)
    for step in range(1, nc):
        small_copy(step, 0).wait_recv()
        for g in range(1, nf):
            small_copy(step, g).start()
    gather_relay(1)
    gather_pass(0)
    for step in range(nc):
        for g in range(1, nf):
            small_copy(step, g).wait_recv()
    parts = [smallg[i] for i in range(nf * nc)]
    small_out[...] = jnp.concatenate(parts, axis=1)
    gain_one, shift_one = small_out[2:3, :], small_out[3:4, :]
    gain_two, shift_two = small_out[4:5, :], small_out[5:6, :]

    def normed(rows, gain, shift):
        block = (xv[rows, :].astype(F32) - stat_s[rows, 0:1]) * stat_s[rows, 1:2]
        return (block * gain + shift).astype(BF16)

    gather_finish(0)

    def project(slot):
        rows = pl.ds(pl.multiple_of(slot * length, length), length)
        both = nn(normed(rows, gain_one, shift_one), wall[:, 0:first])
        cos_t, sin_t = cos_s[rows, :], sin_s[rows, :]
        query = both[:, 0:cols] + bias_q[0:1, :].astype(F32)
        key = both[:, cols : 2 * cols] + bias_q[1:2, :].astype(F32)
        value = both[:, 2 * cols : first] + bias_q[2:3, :].astype(F32)
        qb[rows, :] = (turn(query, cos_t, sin_t) * 0.125).astype(BF16)
        kvb[rows, 0:cols] = turn(key, cos_t, sin_t).astype(BF16)
        kvb[rows, cols : 2 * cols] = value.astype(BF16)

    project(0)
    mine = pl.ds(pl.multiple_of(c * length, length), length)
    kvp[mine, :] = kvb[0:length, :]

    def kv_copy(route):
        def source(owner, side, rows):
            if owner == 0:
                return kvb.at[pl.ds(side * (length // 2), length // 2)]
            return kvp.at[rows]

        return ctx_copy(
            route, source, lambda rows: kvp.at[rows], length, kvs.at[route], kvr.at[route]
        )

    for route in range(4):
        kv_copy(route).start()
    gather_pass(1)
    loads[7].wait()
    loads[9].wait()
    if not turned_in:
        wsh[:, edge + cols : total] = wo_tmp[...].astype(F32).T.astype(BF16)
    loop(1, slots // 2 + 1, statistics)
    for arrived, route in ((0, 4), (1, 5)):
        kv_copy(arrived).wait_recv()
        kv_copy(route).start()
    gather_start(2)
    gather_start(3)
    loop(slots // 2 + 1, slots, statistics)
    loop(1, slots, project)
    gather_finish(1)
    loads[2].wait()
    loads[3].wait()
    gather_relay(2)

    def back_dense(slot):
        rows = pl.ds(pl.multiple_of(slot * length, length), length)
        block_dy = dyv[rows, :]
        ga[rows, :] = nn(block_dy, wall[:, edge : edge + cols]).astype(BF16)

    loop(0, slots, back_dense)

    for route in range(2, 6):
        kv_copy(route).wait_recv()
    k_t[...] = kvp[:, 0:cols].astype(F32).T.astype(BF16)
    v_t[...] = kvp[:, cols : 2 * cols].astype(F32).T.astype(BF16)

    def attend(slot, is_prompt, between=()):
        rows = pl.ds(pl.multiple_of(slot * length, length), length)
        head_of = lax.div(lax.broadcasted_iota(jnp.int32, (length, cols), 1), HD)
        query, grad = qb[rows, :], ga[rows, :]
        zero = jnp.zeros_like(query)
        for h in range(heads):
            qm[h * length : (h + 1) * length, :] = jnp.where(head_of == h, query, zero)
            gm[h * length : (h + 1) * length, :] = jnp.where(head_of == h, grad, zero)
        if not is_prompt:
            ko_t[...] = kvb[rows, 0:cols].astype(F32).T.astype(BF16)
            vo_t[...] = kvb[rows, cols : 2 * cols].astype(F32).T.astype(BF16)
            limit = starts[0, slot - 1]

        def one_head(h, carry):
            lanes = pl.ds(pl.multiple_of(h * length, length), length)
            lines = pl.ds(pl.multiple_of(h * HD, HD), HD)
            q_h, g_h = qm[lanes, :], gm[lanes, :]
            scores = nt(kvp[:, 0:cols], q_h)
            key_at = lax.broadcasted_iota(jnp.int32, scores.shape, 0)
            query_at = lax.broadcasted_iota(jnp.int32, scores.shape, 1)
            if is_prompt:
                seen = key_at <= query_at + c * length
            else:
                seen = key_at < limit
            scores = jnp.where(seen, scores, MASKED)
            highest = jnp.max(scores, axis=0, keepdims=True)
            if not is_prompt:
                scores_own = nt(kvb[rows, 0:cols], q_h)
                own_key = lax.broadcasted_iota(jnp.int32, scores_own.shape, 0)
                own_query = lax.broadcasted_iota(jnp.int32, scores_own.shape, 1)
                scores_own = jnp.where(own_key <= own_query, scores_own, MASKED)
                highest = jnp.maximum(highest, jnp.max(scores_own, axis=0, keepdims=True))
            probs = jnp.exp(scores - highest)
            norm = jnp.sum(probs, axis=0, keepdims=True)
            if not is_prompt:
                probs_own = jnp.exp(scores_own - highest)
                norm = norm + jnp.sum(probs_own, axis=0, keepdims=True)
            share = 1.0 / norm
            probs = probs * share
            probs_low = probs.astype(BF16)
            p_all[0, 0:prompt, lanes] = probs_low
            grads = nt(kvp[:, cols : 2 * cols], g_h)
            inner = jnp.sum(probs * grads, axis=0, keepdims=True)
            if not is_prompt:
                probs_own = probs_own * share
                own_low = probs_own.astype(BF16)
                p_own[:, lanes] = own_low
                grads_own = nt(kvb[rows, cols : 2 * cols], g_h)
                inner = inner + jnp.sum(probs_own * grads_own, axis=0, keepdims=True)
            back_low = (probs * (grads - inner)).astype(BF16)
            p_all[1, 0:prompt, lanes] = back_low
            out_t = nn(v_t[lines, :], probs_low)
            back_q = nn(k_t[lines, :], back_low)
            if not is_prompt:
                back_own = (probs_own * (grads_own - inner)).astype(BF16)
                ds_own[:, lanes] = back_own
                out_t = out_t + nn(vo_t[lines, :], own_low)
                back_q = back_q + nn(ko_t[lines, :], back_own)
            o_t[lines, :] = out_t
            dq_t[lines, :] = back_q
            for at, action in between:
                pl.when(h == at)(action)
            return carry

        lax.fori_loop(0, heads, one_head, 0)
        cos_t, sin_t = cos_s[rows, :], -sin_s[rows, :]
        oa[rows, 0:cols] = o_t[...].T.astype(BF16)
        gd[rows, 0:cols] = turn(dq_t[...].T * 0.125, cos_t, sin_t).astype(BF16)
        stacked = heads * length
        back_k = nn(p_all[1, 0:prompt, 0:stacked], qm[...])
        back_v = nn(p_all[0, 0:prompt, 0:stacked], gm[...])
        acc[:, 0:cols] += back_k
        acc[:, cols : 2 * cols] += back_v
        if not is_prompt:
            gd[rows, cols : 2 * cols] = turn(nn(ds_own[...], qm[...]), cos_t, sin_t).astype(BF16)
            gd[rows, 2 * cols : first] = nn(p_own[...], gm[...]).astype(BF16)

    def kv_send(step):
        return p_all.at[1, pl.ds((step - 1) * length, length), pl.ds(0, 2 * cols)]

    def back_kv_copy(step):
        return remote(
            kv_send(step), kv_recv.at[step - 1], gks.at[step - 1], gkr.at[step - 1], ctx_to(step)
        )

    chunks = rows_all // CHUNK
    per_slot = length // CHUNK
    pair = slots // 2

    def line(q):
        group, inner = lax.div(q, per_slot), lax.rem(q, per_slot)
        which = lax.rem(lax.div(group, pair), 2)
        slot = lax.rem(lax.div(group, 2 * pair) * pair + lax.rem(group, pair) + 1, slots)
        return which, pl.ds(pl.multiple_of((slot * per_slot + inner) * CHUNK, CHUNK), CHUNK)

    def line_out(q, middle):
        which, rows = line(q)
        target = from_in if middle else from_out
        landed = zb if middle else za
        return remote(
            part_sum.at[which, rows], target.at[which, rows], zs.at[q], landed.at[q], inward
        )

    def line_home(q, middle):
        which, rows = line(q)
        src = from_out if middle else from_in
        return remote(
            src.at[which, rows], from_in.at[which, rows], zbs.at[q], zb.at[q], outward
        )

    def line_store(q, middle):
        which, rows = line(q)
        src = from_out if middle else from_in
        return pltpu.make_async_copy(src.at[which, rows], tot_out.at[which, rows], zo.at[q])

    def line_send(q):
        @pl.when(in_middle)
        def _():
            line_out(q, True).start()

        @pl.when(not_middle)
        def _():
            line_out(q, False).start()

    def line_first(q):
        @pl.when(at_end)
        def _():
            line_send(q)

    def line_add(q):
        which, rows = line(q)

        @pl.when(not_end)
        def _():
            line_out(q, False).wait_recv()
            part_sum[which, rows, :] = (
                part_sum[which, rows, :].astype(F32) + from_out[which, rows, :].astype(F32)
            ).astype(BF16)
            line_send(q)

    def line_back(q):
        which, rows = line(q)

        @pl.when(in_middle)
        def _():
            line_out(q, True).wait_recv()
            from_out[which, rows, :] = (
                part_sum[which, rows, :].astype(F32) + from_in[which, rows, :].astype(F32)
            ).astype(BF16)

            @pl.when(not_end)
            def _():
                line_home(q, True).start()

            line_store(q, True).start()

        @pl.when(not_middle)
        def _():
            line_home(q, False).wait_recv()

            @pl.when(not_end)
            def _():
                line_home(q, False).start()

            line_store(q, False).start()

    def line_done(q):
        line_out(q, True).wait_send()
        line_store(q, True).wait()

        @pl.when(not_end)
        def _():
            line_home(q, True).wait_send()

    def tick(q):
        @pl.when(q < 2 * chunks)
        def _():
            line_add(q)

        @pl.when((q >= LAG) & not_end)
        def _():
            line_back(q - LAG)

    def first_chunks(position, which):
        half_at, inner = divmod(position, pair)
        group = half_at * 2 * pair + which * pair + inner
        return group * per_slot

    def feed(position):
        slot = (position + 1) % slots
        rows = pl.ds(slot * length, length)
        hidden = nn(normed(rows, gain_two, shift_two), wall[:, first:edge]) + bias_u[...]
        depth = jnp.abs(hidden) * np.float32(0.5**0.5)
        step = 1.0 / (1.0 + np.float32(0.3275911) * depth)
        poly = np.float32(ERF[4])
        for factor in ERF[3::-1]:
            poly = poly * step + np.float32(factor)
        bell = jnp.exp(-(depth * depth))
        tail = 0.5 * (poly * step) * bell
        below = jnp.where(hidden >= 0.0, 1.0 - tail, tail)
        oa[rows, cols : cols + ff] = (hidden * below).astype(BF16)
        slope = below + hidden * (bell * np.float32((2.0 * np.pi) ** -0.5))
        back = nn(dyv[rows, :], wall[:, edge + cols : total])
        gd[rows, first:edge] = (back * slope).astype(BF16)
        part_sum[0, rows, :] = nt(oa[rows, :], wall[:, edge:total]).astype(BF16)
        for i in range(per_slot):
            line_first(first_chunks(position, 0) + i)

    def back_norms(position):
        slot = (position + 1) % slots
        rows = pl.ds(slot * length, length)
        toward_x = nt(gd[rows, 0:first], wall[:, 0:first]) * gain_one
        toward_x = toward_x + nt(gd[rows, first:edge], wall[:, first:edge]) * gain_two
        part_sum[1, rows, :] = toward_x.astype(BF16)
        for i in range(per_slot):
            line_first(first_chunks(position, 1) + i)

    acc[...] = jnp.zeros_like(acc)
    loop(1, pair + 1, lambda slot: attend(slot, False))
    gather_relay(3)
    for p in (2, 3):
        gather_pass(p)
    for p in (2, 3):
        gather_finish(p)
    for position in range(pair):
        feed(position)
    for position in range(pair):
        back_norms(position)
    for slot in range(pair + 1, slots):
        attend(slot, False, ((heads - 1, lambda: tick(0)),))
    attend(0, True, ((0, lambda: tick(1)), (heads - 1, lambda: tick(2))))

    for step in range(1, nc):
        there = pl.ds(pl.multiple_of(lax.rem(c + step, nc) * length, length), length)
        kv_send(step)[...] = acc[there, :].astype(BF16)
        back_kv_copy(step).start()

    for position in range(pair, slots):
        feed(position)
    tick(3)

    def turn_dy(slot):
        rows = pl.ds(pl.multiple_of(slot * length, length), length)
        p_all[0, :, rows] = dyv[rows, :].astype(F32).T.astype(BF16)

    loop(0, slots, turn_dy)
    for position in range(pair, slots - 1):
        back_norms(position)

    tick(4)
    grad_kv = acc[mine, :]
    for step in range(1, nc):
        back_kv_copy(step).wait_recv()
        grad_kv = grad_kv + kv_recv[step - 1].astype(F32)
    gd[0:length, cols : 2 * cols] = turn(
        grad_kv[:, 0:cols], cos_s[0:length, :], -sin_s[0:length, :]
    ).astype(BF16)
    gd[0:length, 2 * cols : first] = grad_kv[:, cols : 2 * cols].astype(BF16)
    back_norms(slots - 1)

    ones = jnp.ones((16, rows_all), BF16)
    sum_own[:, 0:edge] = nn(ones, gd[...])[0:8, :]
    sum_own[:, edge : edge + width] = nn(ones, dyv[...])[0:8, :]

    def sum_copy(step, g):
        if g:
            return remote(
                sum_own, sum_f.at[f], ss.at[0, g - 1], sr.at[0, g - 1], mate_to(g)
            )
        return remote(
            sum_own, sum_c.at[c], ss.at[1, step - 1], sr.at[1, step - 1], ctx_to(step)
        )

    sum_f[f] = sum_own[...]
    for g in range(1, nf):
        sum_copy(0, g).start()

    group = nc * own
    split = pieces_one + pieces_two

    def product(p, rows, second):
        lanes = pl.ds(pl.multiple_of(p * part, part), part)
        if second:
            return nn(p_all[0, rows, :], oa[:, lanes])
        return nn(n_t[rows, :], gd[:, lanes])

    def half_copy(p, g):
        return remote(
            half_send.at[g - 1, p], half_recv.at[g - 1, p], hs.at[g - 1, p], hr.at[g - 1, p], mate_to(g)
        )

    def piece_copy(p, step):
        rows = pl.ds(pl.multiple_of(lax.rem(c + step, nc) * own, own), own)
        return remote(
            half_recv.at[0, p, rows],
            piece_recv.at[step - 1, p],
            ps.at[step - 1, p],
            pr.at[step - 1, p],
            ctx_to(step),
        )

    def give_half(p, base, second):
        for g in range(1, nf):
            rows = pl.ds(pl.multiple_of(lax.rem(f + g, nf) * group, group), group)
            half_send[g - 1, p] = product(p - base, rows, second).astype(BF16)
            half_copy(p, g).start()

    def keep_half(p, base, second):
        rows = pl.ds(pl.multiple_of(f * group, group), group)
        kept = product(p - base, rows, second)
        for g in range(1, nf):
            half_copy(p, g).wait_recv()
            kept = kept + half_recv[g - 1, p].astype(F32)
        half_recv[0, p] = kept.astype(BF16)
        for step in range(1, nc):
            piece_copy(p, step).start()

    loop(0, pieces_one, lambda p: give_half(p, 0, False))
    loop(pieces_one, split, lambda p: give_half(p, pieces_one, True))
    tick(5)

    def keep_and_tick(p, base, second):
        keep_half(p, base, second)

        @pl.when(lax.rem(p, 2) == 1)
        def _():
            tick(6 + lax.div(p, 2))

    loop(0, pieces_one, lambda p: keep_and_tick(p, 0, False))
    loop(pieces_one, split, lambda p: keep_and_tick(p, pieces_one, True))
    ticked = 6 + split // 2

    for g in range(1, nf):
        sum_copy(0, g).wait_recv()
        sum_copy(0, g).wait_send()
    held = sum_f[0]
    for i in range(1, nf):
        held = held + sum_f[i]
    sum_own[...] = held
    sum_c[c] = held
    for step in range(1, nc):
        sum_copy(step, 0).start()

    loop(ticked, ticked + 2, tick)

    for step in range(1, nc):
        sum_copy(step, 0).wait_recv()
        sum_copy(step, 0).wait_send()
    held = sum_c[0]
    for i in range(1, nc):
        held = held + sum_c[i]
    sums_out[...] = held

    def settle(p):
        rows = pl.ds(pl.multiple_of(c * own, own), own)
        kept = half_recv[0, p, rows, :].astype(F32)
        for step in range(1, nc):
            piece_copy(p, step).wait_recv()
            kept = kept + piece_recv[step - 1, p].astype(F32)
        dw_acc[:, pl.ds(pl.multiple_of(p * part, part), part)] = kept

    loop(0, split, settle)
    dw_store = pltpu.make_async_copy(dw_acc, dw_out, os.at[0])
    dw_store.start()

    loads_w = wsh[:, 0:edge].astype(F32)
    moment = dw_acc[:, 0:edge] * loads_w
    against = loads_w * sums_out[0:1, 0:edge]
    four = [
        jnp.sum(moment[:, 0:first], axis=1, keepdims=True),
        jnp.sum(against[:, 0:first], axis=1, keepdims=True),
        jnp.sum(moment[:, first:edge], axis=1, keepdims=True),
        jnp.sum(against[:, first:edge], axis=1, keepdims=True),
    ]
    lane = lax.broadcasted_iota(jnp.int32, (own, 128), 1)
    packed = jnp.zeros((own, 128), F32)
    for i, column in enumerate(four):
        packed = jnp.where(lane == i, column, packed)
    norm_own[...] = packed
    norm_in[t] = packed

    def norm_copy(k):
        return remote(norm_own, norm_in.at[t], ns.at[k - 1], nr.at[k - 1], tp_to(k))

    for k in range(1, nt_axis):
        norm_copy(k).start()

    def finish_line(q):
        tick(q)

        @pl.when(at_end)
        def _():
            line_back(q - LAG)

    @pl.when(at_end)
    def _():
        loop(0, ticked + 2 - LAG, line_back)

    loop(ticked + 2, 2 * chunks + LAG, finish_line)

    for k in range(1, nt_axis):
        norm_copy(k).wait_recv()
        norm_copy(k).wait_send()
    held = norm_in[0]
    for i in range(1, nt_axis):
        held = held + norm_in[i]
    norms_out[...] = held

    loop(0, 2 * chunks, line_done)
    for p in range(4):
        gather_sent(p)
    for step in range(1, nc):
        small_copy(step, 0).wait_send()
        back_kv_copy(step).wait_send()
    for route in range(6):
        kv_copy(route).wait_send()
    for step in range(nc):
        for g in range(1, nf):
            small_copy(step, g).wait_send()

    def sent(p):
        for g in range(1, nf):
            half_copy(p, g).wait_send()
        for step in range(1, nc):
            piece_copy(p, step).wait_send()

    loop(0, split, sent)
    dw_store.wait()


def run_layer(sizes, *operands):
    nf, nc, tp = sizes["nf"], sizes["nc"], sizes["tp"]
    own, cols, ff, width = sizes["own"], sizes["cols"], sizes["ff"], sizes["width"]
    length, slots, total = sizes["length"], sizes["slots"], sizes["total"]
    part, split = sizes["part"], sizes["pieces_one"] + sizes["pieces_two"]
    rows = slots * length
    prompt = nc * length
    stacked = cols // HD * length
    edge = 3 * cols + ff
    chunks = rows // CHUNK
    sums = edge + width
    anywhere = pl.BlockSpec(memory_space=pl.ANY)
    vmem = pl.BlockSpec(memory_space=pltpu.VMEM)
    smem = pl.BlockSpec(memory_space=pltpu.SMEM)
    dma = pltpu.SemaphoreType.DMA
    shapes = (
        jax.ShapeDtypeStruct((2, rows, width), BF16),
        jax.ShapeDtypeStruct((own, total), F32),
        jax.ShapeDtypeStruct((8, sums), F32),
        jax.ShapeDtypeStruct((own, 128), F32),
        jax.ShapeDtypeStruct((8, width), F32),
    )
    half = nf - 1
    tmp = (8, 128)
    scratch = [
        pltpu.VMEM((rows, width), BF16),
        pltpu.VMEM((rows, width), BF16),
        pltpu.VMEM((width, rows), BF16),
        pltpu.VMEM((width, total), BF16),
        pltpu.VMEM((own, total), BF16),
        pltpu.VMEM(tmp if sizes["turned"] else (cols, own), BF16),
        pltpu.VMEM(tmp if sizes["turned"] else (ff, own), BF16),
        pltpu.VMEM((rows, 2), F32),
        pltpu.VMEM((rows, 128), F32),
        pltpu.VMEM((rows, 128), F32),
        pltpu.VMEM((8, own), F32),
        pltpu.VMEM((nf * nc, 8, own), F32),
        pltpu.VMEM((1, ff), F32),
        pltpu.VMEM((rows, cols), BF16),
        pltpu.VMEM((rows, 2 * cols), BF16),
        pltpu.VMEM((prompt, 2 * cols), BF16),
        pltpu.VMEM((cols, prompt), BF16),
        pltpu.VMEM((cols, prompt), BF16),
        pltpu.VMEM((cols, length), BF16),
        pltpu.VMEM((cols, length), BF16),
        pltpu.VMEM((stacked, cols), BF16),
        pltpu.VMEM((stacked, cols), BF16),
        pltpu.VMEM((cols, length), F32),
        pltpu.VMEM((cols, length), F32),
        pltpu.VMEM((length, stacked), BF16),
        pltpu.VMEM((length, stacked), BF16),
        pltpu.VMEM((2, max(prompt, width), max(stacked, rows)), BF16),
        pltpu.VMEM((rows, cols), BF16),
        pltpu.VMEM((rows, cols + ff), BF16),
        pltpu.VMEM((rows, edge), BF16),
        pltpu.VMEM((prompt, 2 * cols), F32),
        pltpu.VMEM((nc - 1, length, 2 * cols), BF16),
    ]
    scratch += [pltpu.VMEM((2, rows, width), BF16)] * 3
    scratch += [
        pltpu.VMEM((half, split, nc * own, part), BF16),
        pltpu.VMEM((half, split, nc * own, part), BF16),
        pltpu.VMEM((nc - 1, split, own, part), BF16),
        pltpu.VMEM((own, total), F32),
        pltpu.VMEM((8, sums), F32),
        pltpu.VMEM((nf, 8, sums), F32),
        pltpu.VMEM((nc, 8, sums), F32),
        pltpu.VMEM((own, 128), F32),
        pltpu.VMEM((tp, own, 128), F32),
        dma((10,)),
        dma((2, nc, nf)),
        dma((4, 6)),
        dma((4, 6)),
        dma((4, nc, half)),
        dma((4, nc, half)),
        dma((4,)),
        dma((6,)),
        dma((6,)),
        dma((nc - 1,)),
        dma((nc - 1,)),
        dma((2 * chunks,)),
        dma((2 * chunks,)),
        dma((2 * chunks,)),
        dma((2 * chunks,)),
        dma((2 * chunks,)),
        dma((half, split)),
        dma((half, split)),
        dma((nc - 1, split)),
        dma((nc - 1, split)),
        dma((2, max(half, nc - 1))),
        dma((2, max(half, nc - 1))),
        dma((tp - 1,)),
        dma((tp - 1,)),
        dma((1,)),
    ]
    return pl.pallas_call(
        functools.partial(layer_kernel, sizes),
        out_shape=shapes,
        in_specs=[smem, vmem] + [anywhere] * 8 + [vmem] * (len(operands) - 10),
        out_specs=(anywhere, anywhere, vmem, vmem, vmem),
        scratch_shapes=scratch,
        compiler_params=pltpu.CompilerParams(
            collective_id=0, has_side_effects=True, vmem_limit_bytes=63 * 1024 * 1024
        ),
        name="layer",
    )(*operands)


def close_kernel(sizes, *refs):
    nc, own, cols, ff = sizes["nc"], sizes["own"], sizes["cols"], sizes["ff"]
    first, turned = 3 * cols, sizes["turned"]
    edge = first + ff
    prompt_blocks = sizes["length"] // BLOCK
    refs = list(refs)

    def take(count):
        taken = refs[:count]
        del refs[:count]
        return taken

    x_prompt, x_cont, dy_prompt, dy_cont, totals, shifts, dw, sums, norms = take(9)
    gains = take(1 if turned else 4)
    y_prompt, y_cont, dx_prompt, dx_cont, d_qkv, b_qkv, d_dense, d_u, b_u, d_o = take(10)
    rest = take(1 if turned else 2)
    at = pl.program_id(0)

    def rows_of(x_ref, dy_ref, y_ref, dx_ref):
        x = x_ref[...].astype(F32)
        u = totals[1].astype(F32)
        centered = x - jnp.mean(x, axis=1, keepdims=True)
        scale = lax.rsqrt(jnp.mean(centered * centered, axis=1, keepdims=True) + EPS)
        unit = centered * scale
        u = u - jnp.mean(u, axis=1, keepdims=True) - unit * jnp.mean(u * unit, axis=1, keepdims=True)
        y_ref[...] = x + totals[0].astype(F32) + (shifts[0:1, :] + shifts[1:2, :])
        dx_ref[...] = dy_ref[...].astype(F32) + scale * u

    @pl.when(at < prompt_blocks)
    def _():
        rows_of(x_prompt, dy_prompt, y_prompt, dx_prompt)

    @pl.when(at >= prompt_blocks)
    def _():
        rows_of(x_cont, dy_cont, y_cont, dx_cont)

    @pl.when(at == 0)
    def _():
        if turned:
            gain_one, shift_one, gain_two, shift_two = (gains[0][:, i : i + 1] for i in range(4))
        else:
            rows = [ref[...].astype(F32).reshape(1, own) for ref in gains]
            columns = jnp.concatenate(rows * 2, axis=0).T
            gain_one, shift_one, gain_two, shift_two = (columns[:, i : i + 1] for i in range(4))
        for i in range(3):
            lanes = slice(i * cols, (i + 1) * cols)
            total = sums[0:1, lanes]
            d_qkv[i] = dw[:, lanes] * gain_one + shift_one * total
            b_qkv[i : i + 1, :] = total
        total = sums[0:1, first:edge]
        d_u[...] = dw[:, first:edge] * gain_two + shift_two * total
        b_u[...] = total
        if turned:
            d_dense[...] = dw[:, edge : edge + cols]
            d_o[...] = dw[:, edge + cols :]
            rest[0][...] = norms[...]
        else:
            d_dense[...] = dw[:, edge : edge + cols].T
            d_o[...] = dw[:, edge + cols :].T
            rest[0][...] = norms[...].T[0:8, :]
            shard = lax.axis_index("fsdp") * nc + lax.axis_index("ctx")
            lanes = pl.ds(pl.multiple_of(edge + shard * own, own), own)
            rest[1][...] = sums[0:1, lanes]


def close_layer(sizes, *operands):
    own, cols, ff, width = sizes["own"], sizes["cols"], sizes["ff"], sizes["width"]
    length, slots, turned = sizes["length"], sizes["slots"], sizes["turned"]
    near = length // BLOCK
    blocks = slots * near
    prompt = pl.BlockSpec((BLOCK, width), lambda i: (jnp.minimum(i, near - 1), 0))
    cont = pl.BlockSpec((BLOCK, width), lambda i: (jnp.maximum(i - near, 0), 0))
    both = pl.BlockSpec((2, BLOCK, width), lambda i: (0, i, 0))

    def fixed(*shape):
        return pl.BlockSpec(shape, lambda i: (0,) * len(shape))

    def array(*shape):
        return jax.ShapeDtypeStruct(shape, F32)

    kept = [
        (3, own, cols),
        (3, cols),
        (own, cols) if turned else (cols, own),
        (own, ff),
        (1, ff),
        (own, ff) if turned else (ff, own),
    ]
    kept += [(own, 128)] if turned else [(8, own), (1, own)]
    rows_prompt, rows_cont = array(length, width), array((slots - 1) * length, width)
    return pl.pallas_call(
        functools.partial(close_kernel, sizes),
        grid=(blocks,),
        in_specs=[prompt, cont, prompt, cont, both] + [fixed(*o.shape) for o in operands[5:]],
        out_specs=[prompt, cont, prompt, cont] + [fixed(*shape) for shape in kept],
        out_shape=[rows_prompt, rows_cont, rows_prompt, rows_cont] + [array(*s) for s in kept],
        compiler_params=pltpu.CompilerParams(vmem_limit_bytes=62 * 1024 * 1024),
        name="close",
    )(*operands)


def on_device(
    x_prompt,
    x_cont,
    cont_start,
    w_qkv,
    qkv_bias,
    w_dense,
    dense_bias,
    w_fc1,
    fc1_bias,
    w_fc2,
    fc2_bias,
    ln1_gain,
    ln1_bias,
    ln2_gain,
    ln2_bias,
    dy_prompt,
    dy_cont,
):
    length = x_prompt.shape[1]
    conts, cont_len, width = x_cont.shape[1:]
    own, _, cols = w_qkv.shape
    ff = w_fc1.shape[1]
    nf, nc, tp = (lax.axis_size(name) for name in ("fsdp", "ctx", "tp"))
    edge = 3 * cols + ff
    part = 256 if edge % 256 == 0 and (cols + ff) % 256 == 0 else 128
    sizes = {
        "nf": nf,
        "nc": nc,
        "tp": tp,
        "own": own,
        "cols": cols,
        "ff": ff,
        "width": width,
        "length": length,
        "slots": 1 + conts,
        "total": 4 * cols + 2 * ff,
        "part": part,
        "pieces_one": edge // part,
        "pieces_two": (cols + ff) // part,
        "turned": own % 128 != 0,
    }
    turned = [w_dense.T, w_fc2.T] if sizes["turned"] else [w_dense, w_fc2]
    lane = np.arange(128) % HD
    inverse = 10000.0 ** (-2.0 * (lane % (ROT // 2)) / ROT)
    freq = np.zeros((8, 128), np.float32)
    freq[0] = np.where(lane < ROT, inverse, 0.0)
    freq[1] = np.where(lane < ROT // 2, -1.0, 1.0)
    vectors = [dense_bias, fc2_bias, ln1_gain, ln1_bias, ln2_gain, ln2_bias]
    if sizes["turned"]:
        vectors = [jnp.pad(jnp.stack(vectors).astype(F32), ((0, 2), (0, 0)))]
    totals, dw, sums, norms, small_full = run_layer(
        sizes,
        cont_start,
        jnp.asarray(freq),
        x_prompt[0],
        x_cont.reshape(conts * cont_len, width),
        dy_prompt[0],
        dy_cont.reshape(conts * cont_len, width),
        w_qkv.transpose(1, 0, 2),
        turned[0],
        w_fc1,
        turned[1],
        *vectors,
        qkv_bias,
        fc1_bias,
    )
    gains = [ln1_gain, ln1_bias, ln2_gain, ln2_bias]
    if sizes["turned"]:
        gains = [jnp.stack(gains, axis=1).astype(F32)]
    tokens = conts * cont_len
    closed = close_layer(
        sizes,
        x_prompt[0],
        x_cont.reshape(tokens, width),
        dy_prompt[0],
        dy_cont.reshape(tokens, width),
        totals,
        small_full,
        dw,
        sums,
        norms,
        *gains,
    )
    y_prompt, y_cont, dx_prompt, dx_cont, d_qkv, b_qkv, d_dense, d_u, b_u, d_o = closed[:10]
    if sizes["turned"]:
        d_dense, d_o, four = d_dense.T, d_o.T, closed[10][:, 0:4].T
        place = (lax.axis_index("fsdp") * nc + lax.axis_index("ctx")) * own
        d_shift = lax.dynamic_slice_in_dim(sums[0, edge:], place, own)
    else:
        four, d_shift = closed[10], closed[11].reshape(own)
    shape = x_cont.shape
    return (
        y_prompt[None],
        y_cont.reshape(shape),
        dx_prompt[None],
        dx_cont.reshape(shape),
        d_qkv.transpose(1, 0, 2),
        b_qkv,
        d_dense,
        d_shift,
        d_u,
        b_u.reshape(ff),
        d_o,
        d_shift,
        four[0],
        four[1],
        four[2],
        four[3],
    )


def solution(mesh):
    both = ("fsdp", "ctx")
    rows = P("fsdp", "ctx", None)
    conts = P("fsdp", "ctx", None, None)
    vector = P(both)
    return jax.shard_map(
        on_device,
        mesh=mesh,
        in_specs=(
            rows,
            conts,
            P("fsdp", "ctx"),
            P(both, None, "tp"),
            P(None, "tp"),
            P("tp", both),
            vector,
            P(both, "tp"),
            P("tp"),
            P("tp", both),
            vector,
            vector,
            vector,
            vector,
            vector,
            rows,
            conts,
        ),
        out_specs=(
            rows,
            conts,
            rows,
            conts,
            P(both, None, "tp"),
            P(None, "tp"),
            P("tp", both),
            vector,
            P(both, "tp"),
            P("tp"),
            P("tp", both),
            vector,
            vector,
            vector,
            vector,
            vector,
        ),
        check_vma=False,
    )
```

```python
import functools

import jax
import jax.numpy as jnp
import numpy as np
from jax import lax
from jax.experimental import pallas as pl
from jax.experimental.pallas import tpu as pltpu
from jax.sharding import PartitionSpec as P

HD = 64
ROT = 16
EPS = 1e-05
MASKED = -1e30
F32 = jnp.float32
BF16 = jnp.bfloat16
MESH = pl.DeviceIdType.MESH
CHUNK = 64
BLOCK = 256
MEMORY = 63 * 1024 * 1024
LAG = 2
ERF = (0.254829592, -0.284496736, 1.421413741, -1.453152027, 1.061405429)


def nn(left, right):
    return jnp.dot(left, right, preferred_element_type=F32)


def nt(left, right):
    return lax.dot_general(left, right, (((1,), (1,)), ((), ())), preferred_element_type=F32)


def remote(src, dst, send_sem, recv_sem, device):
    return pltpu.make_async_remote_copy(
        src_ref=src,
        dst_ref=dst,
        send_sem=send_sem,
        recv_sem=recv_sem,
        device_id=device,
        device_id_type=MESH,
    )


def turn(values, cos_t, sin_t):
    lane = lax.broadcasted_iota(jnp.int32, cos_t.shape, 1)
    low_half = lax.rem(lane, HD) < ROT // 2
    pieces = []
    for start in range(0, values.shape[1], 128):
        piece = values[:, start : start + 128]
        up = pltpu.roll(piece, 128 - ROT // 2, 1)
        down = pltpu.roll(piece, ROT // 2, 1)
        pieces.append(piece * cos_t + jnp.where(low_half, up, down) * sin_t)
    return jnp.concatenate(pieces, axis=1) if len(pieces) > 1 else pieces[0]


def layer_kernel(sizes, *refs):
    nf, nc, nt_axis = sizes["nf"], sizes["nc"], sizes["tp"]
    own, cols, ff, width = sizes["own"], sizes["cols"], sizes["ff"], sizes["width"]
    length, slots, total = sizes["length"], sizes["slots"], sizes["total"]
    part, pieces_one, pieces_two = sizes["part"], sizes["pieces_one"], sizes["pieces_two"]
    turned_in = sizes["turned"]
    refs = list(refs)

    def take(count):
        taken = refs[:count]
        del refs[:count]
        return taken

    starts, freq, x_prompt, x_cont, dy_prompt, dy_cont, w_q, w_d, w_u, w_o = take(10)
    vectors = take(1 if turned_in else 6)
    small_t = take(1)[0] if turned_in else None
    bias_q, bias_up = take(2)
    tot_out, dq_out, dd_out, du_out, do_out, sums_out, norms_out, small_out = take(8)
    xv, dyv, n_t, wall = take(4)
    stat_s, cos_s, sin_s, small, smallg, bias_u = take(6)
    kvp, k_t, v_t, q_t, g_t, o_t, dq_t, p_all, score_s, slope_s, share_s = take(11)
    oa, gd, acc, kv_recv = take(4)
    part_sum, from_out, from_in, half_send, half_recv, piece_recv, stage, stage_t = take(8)
    sum_own, sum_f, sum_c, norm_own, norm_in = take(5)
    in_sem, small_sem, ws, wr, fs, fr, kvs, kvr, gks, gkr = take(10)
    zs, za, zbs, zb, zo, hs, hr, ps, pr, ss, sr, ns, nr, os = take(14)
    f, c, t = lax.axis_index("fsdp"), lax.axis_index("ctx"), lax.axis_index("tp")
    heads = cols // HD
    rows_all = slots * length
    pair = slots // 2
    prompt = nc * length
    first = 3 * cols
    edge = first + ff
    shard = f * nc + c
    own_rows = pl.ds(pl.multiple_of(shard * own, own), own)

    def ctx_to(step):
        return (f, lax.rem(c + step, nc), t)

    def ctx_from(step):
        return lax.rem(c + nc - step, nc)

    across_x = c + 1 - 2 * lax.rem(c, 2)
    across_y = lax.rem(c + 2, nc)
    corner = lax.rem(across_x + 2, nc)
    peers = (c, across_x, across_y, corner)

    def mate_to(step):
        return (lax.rem(f + step, nf), c, t)

    def mate_from(step):
        return lax.rem(f + nf - step, nf)

    def tp_to(step):
        return (f, c, lax.rem(t + step, nt_axis))

    upper = lax.div(t, nt_axis // 2)
    inward = (f, c, t + 1 - 2 * upper)
    outward = (f, c, lax.rem(t - 1 + 2 * upper + nt_axis, nt_axis))
    at_end = (t == 0) | (t == nt_axis - 1)
    not_end = (t != 0) & (t != nt_axis - 1)
    in_middle = (t == nt_axis // 2 - 1) | (t == nt_axis // 2)
    not_middle = (t != nt_axis // 2 - 1) & (t != nt_axis // 2)

    loads = [
        (x_prompt, xv.at[pl.ds(0, length)]),
        (x_cont, xv.at[pl.ds(length, rows_all - length)]),
        (dy_prompt, dyv.at[pl.ds(0, length)]),
        (dy_cont, dyv.at[pl.ds(length, rows_all - length)]),
        (w_q.at[0], wall.at[own_rows, pl.ds(0, cols)]),
        (w_q.at[1], wall.at[own_rows, pl.ds(cols, cols)]),
        (w_q.at[2], wall.at[own_rows, pl.ds(2 * cols, cols)]),
        (w_u, wall.at[own_rows, pl.ds(first, ff)]),
    ]
    if turned_in:
        loads += [
            (w_d, wall.at[own_rows, pl.ds(edge, cols)]),
            (w_o, wall.at[own_rows, pl.ds(edge + cols, ff)]),
        ]
    else:
        loads += [
            (w_d, p_all.at[1, pl.ds(0, cols), pl.ds(0, own)]),
            (w_o, p_all.at[0, pl.ds(0, ff), pl.ds(0, own)]),
        ]
    loads = [pltpu.make_async_copy(src, dst, in_sem.at[i]) for i, (src, dst) in enumerate(loads)]
    for i in (4, 5, 6, 0, 1, 8, 7, 9, 2, 3):
        loads[i].start()

    barrier = pltpu.get_barrier_semaphore()
    greeted = [ctx_to(k) for k in range(1, nc)]
    greeted += [mate_to(g) for g in range(1, nf)]
    greeted += [tp_to(k) for k in range(1, nt_axis)]
    for device in greeted:
        pl.semaphore_signal(barrier, inc=1, device_id=device, device_id_type=MESH)
    pl.semaphore_wait(barrier, len(greeted))

    spans = (
        (0, first),
        (edge, cols),
        (first, ff // 2),
        (first + ff // 2, ff // 2),
        (edge + cols, ff),
    )

    half_own = own // 2

    def block(owner, side, size):
        base = owner * size
        if side is None:
            return pl.ds(pl.multiple_of(base, size), size)
        return pl.ds(pl.multiple_of(base + side * (size // 2), size // 2), size // 2)

    routes = ((0, 0, 1), (0, 1, 2), (0, 1, 1), (0, 0, 2), (1, 0, 2), (2, 1, 1))
    lands = ((1, 0), (2, 1), (1, 1), (2, 0), (3, 0), (3, 1))

    def ctx_copy(route, source, target, size, send_sem, recv_sem):
        owner, side, to = routes[route]
        rows = block(peers[owner], side, size)
        src = source(owner, side, rows)
        return remote(src, target(rows), send_sem, recv_sem, (f, peers[to], t))

    def lanes_of(p):
        return pl.ds(spans[p][0], spans[p][1])

    def gather_copy(p, route):
        def place(rows):
            return wall.at[pl.ds(rows.start + f * nc * own, half_own), lanes_of(p)]

        return ctx_copy(
            route, lambda owner, side, rows: place(rows), place, own, ws.at[p, route], wr.at[p, route]
        )

    def mate_copy(p, peer, g):
        place = wall.at[block(f * nc + peers[peer], None, own), lanes_of(p)]
        return remote(
            place, place, fs.at[p, peer, g - 1], fr.at[p, peer, g - 1], mate_to(g)
        )

    def gather_start(p):
        for route in range(4):
            gather_copy(p, route).start()
        for g in range(1, nf):
            mate_copy(p, 0, g).start()

    def gather_relay(p):
        for arrived, route in ((0, 4), (1, 5)):
            gather_copy(p, arrived).wait_recv()
            gather_copy(p, route).start()

    def gather_pass(p):
        for peer, rest in ((1, (2,)), (2, (3,)), (3, (4, 5))):
            for route in rest:
                gather_copy(p, route).wait_recv()
            for g in range(1, nf):
                mate_copy(p, peer, g).start()

    def gather_finish(p):
        for peer in range(nc):
            for g in range(1, nf):
                mate_copy(p, peer, g).wait_recv()

    def gather_sent(p):
        for route in range(6):
            gather_copy(p, route).wait_send()
        for peer in range(nc):
            for g in range(1, nf):
                mate_copy(p, peer, g).wait_send()

    def small_copy(step, g):
        if g == 0:
            return remote(
                small, smallg.at[shard], small_sem.at[0, step, 0], small_sem.at[1, step, 0], ctx_to(step)
            )
        held = f * nc + ctx_from(step)
        src = small if step == 0 else smallg.at[held]
        return remote(
            src, smallg.at[held], small_sem.at[0, step, g], small_sem.at[1, step, g], mate_to(g)
        )

    if turned_in:
        small[...] = vectors[0][...]
    else:
        small[...] = jnp.zeros_like(small)
        for i, vector in enumerate(vectors):
            small[i : i + 1, :] = vector[...].astype(F32).reshape(1, own)
    bias_u[...] = bias_up[...].astype(F32).reshape(1, ff)
    for step in range(1, nc):
        small_copy(step, 0).start()
    for g in range(1, nf):
        small_copy(0, g).start()
    for i in (4, 5, 6):
        loads[i].wait()
    gather_start(0)
    loads[8].wait()
    if not turned_in:
        wall[own_rows, edge : edge + cols] = p_all[1, 0:cols, 0:own].astype(F32).T.astype(BF16)
    smallg[shard] = small[...]
    loads[7].wait()
    gather_relay(0)
    gather_start(1)
    gather_start(2)

    loads[0].wait()
    loads[1].wait()

    def statistics(slot):
        rows = pl.ds(pl.multiple_of(slot * length, length), length)
        block_x = xv[rows, :].astype(F32)
        mean = jnp.mean(block_x, axis=1, keepdims=True)
        block_x = block_x - mean
        scale = lax.rsqrt(jnp.mean(block_x * block_x, axis=1, keepdims=True) + EPS)
        stat_s[rows, 0:1] = mean
        stat_s[rows, 1:2] = scale
        n_t[:, rows] = (block_x * scale).T.astype(BF16)
        before = starts[0, jnp.maximum(slot - 1, 0)]
        base = jnp.where(slot == 0, c * length, before)
        place = base + lax.broadcasted_iota(jnp.int32, (length, 128), 0)
        phase = place.astype(F32) * freq[0:1, :]
        cos_s[rows, :] = jnp.cos(phase)
        sin_s[rows, :] = jnp.sin(phase) * freq[1:2, :]

    def loop(low, high, body):
        lax.fori_loop(low, high, lambda i, carry: (body(i), carry)[1], 0)

    statistics(0)
    for step in range(1, nc):
        small_copy(step, 0).wait_recv()
        for g in range(1, nf):
            small_copy(step, g).start()
    gather_relay(1)
    statistics(1)
    gather_relay(2)
    gather_pass(0)
    loop(2, slots - 1, statistics)
    for step in range(nc):
        for g in range(1, nf):
            small_copy(step, g).wait_recv()
    parts = [smallg[i] for i in range(nf * nc)]
    small_out[...] = jnp.concatenate(parts, axis=1)
    gain_one, shift_one = small_out[2:3, :], small_out[3:4, :]
    gain_two, shift_two = small_out[4:5, :], small_out[5:6, :]

    def normed(rows, gain, shift):
        block = (xv[rows, :].astype(F32) - stat_s[rows, 0:1]) * stat_s[rows, 1:2]
        return (block * gain + shift).astype(BF16)

    gather_finish(0)

    def project(slot):
        rows = pl.ds(pl.multiple_of(slot * length, length), length)
        both = nn(normed(rows, gain_one, shift_one), wall[:, 0:first])
        cos_t, sin_t = cos_s[rows, :], sin_s[rows, :]
        query = both[:, 0:cols] + bias_q[0:1, :].astype(F32)
        key = both[:, cols : 2 * cols] + bias_q[1:2, :].astype(F32)
        value = both[:, 2 * cols : first] + bias_q[2:3, :].astype(F32)
        gd[rows, 0:cols] = (turn(query, cos_t, sin_t) * 0.125).astype(BF16)
        gd[rows, cols : 2 * cols] = turn(key, cos_t, sin_t).astype(BF16)
        gd[rows, 2 * cols : first] = value.astype(BF16)

    project(0)
    mine = pl.ds(pl.multiple_of(c * length, length), length)
    kvp[mine, :] = gd[0:length, cols:first]

    def kv_copy(route):
        def source(owner, side, rows):
            if owner == 0:
                return gd.at[pl.ds(side * (length // 2), length // 2), pl.ds(cols, 2 * cols)]
            return kvp.at[rows]

        return ctx_copy(
            route, source, lambda rows: kvp.at[rows], length, kvs.at[route], kvr.at[route]
        )

    for route in range(4):
        kv_copy(route).start()
    gather_pass(1)
    loads[9].wait()
    if not turned_in:
        wall[own_rows, edge + cols : total] = p_all[0, 0:ff, 0:own].astype(F32).T.astype(BF16)
    statistics(slots - 1)
    for arrived, route in ((0, 4), (1, 5)):
        kv_copy(arrived).wait_recv()
        kv_copy(route).start()
    gather_start(3)
    gather_start(4)
    loop(1, slots, project)
    gather_relay(3)
    gather_finish(1)
    gather_pass(2)
    loads[2].wait()
    loads[3].wait()

    def back_dense(slot):
        rows = pl.ds(pl.multiple_of(slot * length, length), length)
        block_dy = dyv[rows, :]
        oa[rows, 0:cols] = nn(block_dy, wall[:, edge : edge + cols]).astype(BF16)

    loop(0, slots, back_dense)

    for route in range(2, 6):
        kv_copy(route).wait_recv()
    k_t[:, 0:prompt] = kvp[0:prompt, 0:cols].astype(F32).T.astype(BF16)
    v_t[:, 0:prompt] = kvp[0:prompt, cols : 2 * cols].astype(F32).T.astype(BF16)

    def fold(block_of, combine):
        return combine(block_of.reshape(-1, 8, block_of.shape[1]), axis=0)

    def attend(slot, is_prompt, between=()):
        rows = pl.ds(pl.multiple_of(slot * length, length), length)
        span = prompt if is_prompt else prompt + length
        stacked = heads * length
        head_row = lax.div(lax.broadcasted_iota(jnp.int32, (cols, length), 0), HD)
        query = gd[rows, 0:cols].astype(F32).T.astype(BF16)
        grad = oa[rows, 0:cols].astype(F32).T.astype(BF16)
        zero = jnp.zeros_like(query)
        for h in range(heads):
            q_t[:, h * length : (h + 1) * length] = jnp.where(head_row == h, query, zero)
            g_t[:, h * length : (h + 1) * length] = jnp.where(head_row == h, grad, zero)
        key_at = lax.broadcasted_iota(jnp.int32, (length, length), 0)
        query_at = lax.broadcasted_iota(jnp.int32, (length, length), 1)
        if is_prompt:
            limit = query_at + (c * length + 1)
        else:
            kvp[prompt:span, :] = gd[rows, cols:first]
            k_t[:, prompt:span] = gd[rows, cols : 2 * cols].astype(F32).T.astype(BF16)
            v_t[:, prompt:span] = gd[rows, 2 * cols : first].astype(F32).T.astype(BF16)
            limit = starts[0, slot - 1]

        def lanes(h):
            return slice(h * length, (h + 1) * length)

        def lines(h):
            return slice(h * HD, (h + 1) * HD)

        def score(h):
            for b in range(0, span, length):
                keys = slice(b, b + length)
                score_s[keys, :] = nn(kvp[keys, 0:cols], q_t[:, lanes(h)])

        def slope(h):
            for b in range(0, span, length):
                keys = slice(b, b + length)
                slope_s[keys, :] = nn(kvp[keys, cols : 2 * cols], g_t[:, lanes(h)])

        def mask():
            highest = jnp.full((8, length), MASKED, F32)
            for b in range(0, span, length):
                seen = key_at + b < limit if b < prompt else key_at <= query_at
                scores = jnp.where(seen, score_s[b : b + length, :], MASKED)
                score_s[b : b + length, :] = scores
                highest = jnp.maximum(highest, fold(scores, jnp.max))
            return jnp.max(highest, axis=0, keepdims=True)

        def raise_up(h, highest):
            norm = jnp.zeros((8, length), F32)
            for b in range(0, span, length):
                raised = jnp.exp(score_s[b : b + length, :] - highest)
                norm = norm + fold(raised, jnp.sum)
                p_all[0, b : b + length, lanes(h)] = raised.astype(BF16)
            share = 1.0 / jnp.sum(norm, axis=0, keepdims=True)
            share_s[h : h + 1, :] = share
            return share

        score(0)
        slope(0)
        share = raise_up(0, mask())
        for h in range(heads):
            out_t = nn(v_t[lines(h), 0:span], p_all[0, 0:span, lanes(h)]) * share
            o_t[lines(h), :] = out_t
            if h + 1 < heads:
                score(h + 1)
            inner = jnp.sum(out_t * g_t[lines(h), lanes(h)].astype(F32), axis=0, keepdims=True)
            for b in range(0, span, length):
                raised = p_all[0, b : b + length, lanes(h)].astype(F32)
                low = (raised * (slope_s[b : b + length, :] - inner)).astype(BF16)
                p_all[1, b : b + length, lanes(h)] = low
            dq_t[lines(h), :] = nn(k_t[lines(h), 0:span], p_all[1, 0:span, lanes(h)]) * share
            if h + 1 < heads:
                slope(h + 1)
                share = raise_up(h + 1, mask())
            for at, action in between:
                if at == h:
                    action()
        for h in range(heads):
            share = share_s[h : h + 1, :]
            q_t[:, lanes(h)] = (q_t[:, lanes(h)].astype(F32) * share).astype(BF16)
            g_t[:, lanes(h)] = (g_t[:, lanes(h)].astype(F32) * share).astype(BF16)
        cos_t, sin_t = cos_s[rows, :], -sin_s[rows, :]
        oa[rows, 0:cols] = o_t[...].T.astype(BF16)
        gd[rows, 0:cols] = turn(dq_t[...].T * 0.125, cos_t, sin_t).astype(BF16)
        acc[:, 0:cols] += nt(p_all[1, 0:prompt, 0:stacked], q_t[...])
        acc[:, cols : 2 * cols] += nt(p_all[0, 0:prompt, 0:stacked], g_t[...])
        if not is_prompt:
            back_k = nt(p_all[1, prompt:span, 0:stacked], q_t[...])
            gd[rows, cols : 2 * cols] = turn(back_k, cos_t, sin_t).astype(BF16)
            gd[rows, 2 * cols : first] = nt(p_all[0, prompt:span, 0:stacked], g_t[...]).astype(BF16)

    def kv_send(step):
        return p_all.at[1, pl.ds((step - 1) * length, length), pl.ds(0, 2 * cols)]

    def back_kv_copy(step):
        return remote(
            kv_send(step), kv_recv.at[step - 1], gks.at[step - 1], gkr.at[step - 1], ctx_to(step)
        )

    chunks = rows_all // CHUNK
    per_slot = length // CHUNK

    def line(q):
        which, place = lax.div(q, chunks), lax.rem(q, chunks)
        slot = lax.rem(lax.div(place, per_slot) + 1, slots)
        inner = lax.rem(place, per_slot)
        return which, pl.ds(pl.multiple_of((slot * per_slot + inner) * CHUNK, CHUNK), CHUNK)

    def line_out(q, middle):
        which, rows = line(q)
        target = from_in if middle else from_out
        landed = zb if middle else za
        return remote(
            part_sum.at[which, rows], target.at[which, rows], zs.at[q], landed.at[q], inward
        )

    def line_home(q, middle):
        which, rows = line(q)
        src = from_out if middle else from_in
        return remote(
            src.at[which, rows], from_in.at[which, rows], zbs.at[q], zb.at[q], outward
        )

    def line_store(q, middle):
        which, rows = line(q)
        src = from_out if middle else from_in
        return pltpu.make_async_copy(src.at[which, rows], tot_out.at[which, rows], zo.at[q])

    def line_send(q):
        @pl.when(in_middle)
        def _():
            line_out(q, True).start()

        @pl.when(not_middle)
        def _():
            line_out(q, False).start()

    def line_first(q):
        @pl.when(at_end)
        def _():
            line_send(q)

    def line_add(q):
        which, rows = line(q)

        @pl.when(not_end)
        def _():
            line_out(q, False).wait_recv()
            part_sum[which, rows, :] = (
                part_sum[which, rows, :].astype(F32) + from_out[which, rows, :].astype(F32)
            ).astype(BF16)
            line_send(q)

    def line_back(q):
        which, rows = line(q)

        @pl.when(in_middle)
        def _():
            line_out(q, True).wait_recv()
            from_out[which, rows, :] = (
                part_sum[which, rows, :].astype(F32) + from_in[which, rows, :].astype(F32)
            ).astype(BF16)

            @pl.when(not_end)
            def _():
                line_home(q, True).start()

            line_store(q, True).start()

        @pl.when(not_middle)
        def _():
            line_home(q, False).wait_recv()

            @pl.when(not_end)
            def _():
                line_home(q, False).start()

            line_store(q, False).start()

    def line_done(q):
        line_out(q, True).wait_send()
        line_store(q, True).wait()

        @pl.when(not_end)
        def _():
            line_home(q, True).wait_send()

    def tick(q):
        @pl.when(q < 2 * chunks)
        def _():
            line_add(q)

        @pl.when((q >= LAG) & not_end)
        def _():
            line_back(q - LAG)

    def feed(position):
        slot = lax.rem(position + 1, slots)
        rows = pl.ds(pl.multiple_of(slot * length, length), length)
        inputs = normed(rows, gain_two, shift_two)
        for at in range(0, ff, ff // 2):
            units = slice(at, at + ff // 2)
            up = slice(first + at, first + at + ff // 2)
            down = slice(edge + cols + at, edge + cols + at + ff // 2)
            hidden = nn(inputs, wall[:, up]) + bias_u[:, units]
            depth = jnp.abs(hidden) * np.float32(0.5**0.5)
            step = 1.0 / (1.0 + np.float32(0.3275911) * depth)
            poly = np.float32(ERF[4])
            for factor in ERF[3::-1]:
                poly = poly * step + np.float32(factor)
            bell = jnp.exp(-(depth * depth))
            tail = 0.5 * (poly * step) * bell
            below = jnp.where(hidden >= 0.0, 1.0 - tail, tail)
            oa[rows, cols + at : cols + at + ff // 2] = (hidden * below).astype(BF16)
            slope = below + hidden * (bell * np.float32((2.0 * np.pi) ** -0.5))
            back = nn(dyv[rows, :], wall[:, down])
            gd[rows, up] = (back * slope).astype(BF16)
        part_sum[0, rows, :] = nt(oa[rows, :], wall[:, edge:total]).astype(BF16)
        for i in range(per_slot):
            line_first(position * per_slot + i)

    def back_norms(position):
        slot = lax.rem(position + 1, slots)
        rows = pl.ds(pl.multiple_of(slot * length, length), length)
        toward_x = nt(gd[rows, 0:first], wall[:, 0:first]) * gain_one
        toward_x = toward_x + nt(gd[rows, first:edge], wall[:, first:edge]) * gain_two
        part_sum[1, rows, :] = toward_x.astype(BF16)
        for i in range(per_slot):
            line_first(chunks + position * per_slot + i)

    acc[...] = jnp.zeros_like(acc)

    def at_slot(slot, wanted, *steps):
        def action():
            @pl.when(slot == wanted)
            def _():
                for step in steps:
                    step()

        return action

    def attend_cont(slot):
        attend(
            slot,
            False,
            (
                (1, at_slot(slot, 1, lambda: gather_relay(4))),
                (heads - 1, at_slot(slot, 1, lambda: gather_pass(3))),
                (1, at_slot(slot, pair, lambda: gather_pass(4))),
            ),
        )

    loop(1, pair + 1, attend_cont)
    for p in (2, 3, 4):
        gather_finish(p)
    loop(0, pair, feed)
    for slot in range(pair + 1, slots):
        attend(slot, False, ((1, lambda: tick(0)), (heads - 1, lambda: tick(1))))
        feed(slot - 1)
    tick(2)
    attend(0, True, ((1, lambda: tick(3)), (heads - 1, lambda: tick(4))))
    for step in range(1, nc):
        there = pl.ds(pl.multiple_of(lax.rem(c + step, nc) * length, length), length)
        kv_send(step)[...] = acc[there, :].astype(BF16)
        back_kv_copy(step).start()
    feed(slots - 1)
    tick(5)
    loop(0, pair, back_norms)
    tick(6)
    loop(pair, slots - 1, back_norms)

    def turn_dy(slot):
        rows = pl.ds(pl.multiple_of(slot * length, length), length)
        p_all[0, 0:width, rows] = dyv[rows, :].astype(F32).T.astype(BF16)

    loop(0, slots, turn_dy)
    tick(7)

    group = nc * own
    split = pieces_one + pieces_two

    def product(p, rows, second):
        lanes = pl.ds(pl.multiple_of(p * part, part), part)
        if second:
            return nn(p_all[0, rows, 0:rows_all], oa[:, lanes])
        return nn(n_t[rows, :], gd[:, lanes])

    def half_copy(p, g):
        return remote(
            half_send.at[g - 1, p], half_recv.at[g - 1, p], hs.at[g - 1, p], hr.at[g - 1, p], mate_to(g)
        )

    def piece_copy(p, step):
        rows = pl.ds(pl.multiple_of(lax.rem(c + step, nc) * own, own), own)
        return remote(
            half_recv.at[0, p, rows],
            piece_recv.at[step - 1, p],
            ps.at[step - 1, p],
            pr.at[step - 1, p],
            ctx_to(step),
        )

    def give_half(p, base, second):
        for g in range(1, nf):
            rows = pl.ds(pl.multiple_of(lax.rem(f + g, nf) * group, group), group)
            half_send[g - 1, p] = product(p - base, rows, second).astype(BF16)
            half_copy(p, g).start()

    def keep_half(p, base, second):
        rows = pl.ds(pl.multiple_of(f * group, group), group)
        kept = product(p - base, rows, second)
        for g in range(1, nf):
            half_copy(p, g).wait_recv()
            kept = kept + half_recv[g - 1, p].astype(F32)
        half_recv[0, p] = kept.astype(BF16)
        for step in range(1, nc):
            piece_copy(p, step).start()

    early = first // part

    def with_tick(body, start):
        def step(p):
            body(p)

            @pl.when(lax.rem(p, 3) == 2)
            def _():
                tick(start + lax.div(p, 3))

        return step

    give_start = 8 - early // 3
    loop(early, pieces_one, with_tick(lambda p: give_half(p, 0, False), give_start))
    loop(pieces_one, split, with_tick(lambda p: give_half(p, pieces_one, True), give_start))
    keep_start = give_start + split // 3 - early // 3
    loop(early, pieces_one, with_tick(lambda p: keep_half(p, 0, False), keep_start))
    loop(pieces_one, split, with_tick(lambda p: keep_half(p, pieces_one, True), keep_start))
    ticked = keep_start + split // 3

    for route in range(6):
        kv_copy(route).wait_send()
    grad_kv = acc[mine, :]
    for step in range(1, nc):
        back_kv_copy(step).wait_recv()
        grad_kv = grad_kv + kv_recv[step - 1].astype(F32)
    gd[0:length, cols : 2 * cols] = turn(
        grad_kv[:, 0:cols], cos_s[0:length, :], -sin_s[0:length, :]
    ).astype(BF16)
    gd[0:length, 2 * cols : first] = grad_kv[:, cols : 2 * cols].astype(BF16)
    back_norms(slots - 1)
    tick(ticked)
    loop(0, early, lambda p: give_half(p, 0, False))
    tick(ticked + 1)
    loop(0, early, lambda p: keep_half(p, 0, False))
    tick(ticked + 2)
    ticked += 3

    ones = jnp.ones((16, rows_all), BF16)
    sum_own[:, 0:edge] = nn(ones, gd[...])[0:8, :]
    sum_own[:, edge : edge + width] = nn(ones, dyv[...])[0:8, :]

    def sum_copy(step, g):
        if g:
            return remote(
                sum_own, sum_f.at[f], ss.at[0, g - 1], sr.at[0, g - 1], mate_to(g)
            )
        return remote(
            sum_own, sum_c.at[c], ss.at[1, step - 1], sr.at[1, step - 1], ctx_to(step)
        )

    sum_f[f] = sum_own[...]
    for g in range(1, nf):
        sum_copy(0, g).start()

    tick(ticked)
    tick(ticked + 1)
    for g in range(1, nf):
        sum_copy(0, g).wait_recv()
        sum_copy(0, g).wait_send()
    held = sum_f[0]
    for i in range(1, nf):
        held = held + sum_f[i]
    sum_own[...] = held
    sum_c[c] = held
    for step in range(1, nc):
        sum_copy(step, 0).start()
    loop(ticked + 2, ticked + 6, tick)
    ticked += 6
    for step in range(1, nc):
        sum_copy(step, 0).wait_recv()
        sum_copy(step, 0).wait_send()
    held = sum_c[0]
    for i in range(1, nc):
        held = held + sum_c[i]
    sums_out[...] = held

    lane = lax.broadcasted_iota(jnp.int32, (own, 128), 1)
    norm_own[...] = jnp.zeros_like(norm_own)

    columns = small_t[...] if turned_in else small[...].T

    def stored(p, out, base, across):
        slot = lax.rem(p, 2)
        at = pl.ds(pl.multiple_of((p - base) * part, part), part)
        if across:
            return pltpu.make_async_copy(stage.at[slot], out.at[:, at], os.at[slot])
        return pltpu.make_async_copy(stage_t.at[slot], out.at[at], os.at[slot])

    def stage_done(p):
        slot = lax.rem(p, 2)
        pltpu.make_async_copy(stage.at[slot], du_out.at[:, pl.ds(0, part)], os.at[slot]).wait()

    def q_stored(p):
        per = cols // part
        slot = lax.rem(p, 2)
        at = pl.ds(pl.multiple_of(lax.rem(p, per) * part, part), part)
        return pltpu.make_async_copy(stage.at[slot], dq_out.at[lax.div(p, per), :, at], os.at[slot])

    def settle(p, copy_of, group_at):
        rows = pl.ds(pl.multiple_of(c * own, own), own)
        lanes = pl.ds(pl.multiple_of(p * part, part), part)
        kept = half_recv[0, p, rows, :].astype(F32)
        for step in range(1, nc):
            piece_copy(p, step).wait_recv()
            kept = kept + piece_recv[step - 1, p].astype(F32)

        @pl.when(p >= 2)
        def _():
            stage_done(p)

        if group_at is None:
            if turned_in:
                stage[lax.rem(p, 2)] = kept
            else:
                stage_t[lax.rem(p, 2)] = kept.T
        else:
            weights = wall[own_rows, lanes].astype(F32)
            column = sums_out[0:1, lanes]
            moment = jnp.sum(kept * weights, axis=1, keepdims=True)
            against = jnp.sum(weights * column, axis=1, keepdims=True)
            norm_own[...] += jnp.where(
                lane == 2 * group_at, moment, jnp.where(lane == 2 * group_at + 1, against, 0.0)
            )
            at = 2 + 2 * group_at
            gain, shift = columns[:, at : at + 1], columns[:, at + 1 : at + 2]
            stage[lax.rem(p, 2)] = kept * gain + shift * column
        copy_of(p).start()

    loop(0, early, with_tick(lambda p: settle(p, q_stored, 0), ticked))
    loop(
        early,
        pieces_one,
        with_tick(lambda p: settle(p, lambda q: stored(q, du_out, early, True), 1), ticked),
    )
    norm_in[t] = norm_own[...]

    def norm_copy(k):
        return remote(norm_own, norm_in.at[t], ns.at[k - 1], nr.at[k - 1], tp_to(k))

    for k in range(1, nt_axis):
        norm_copy(k).start()
    dense_end = pieces_one + cols // part
    loop(
        pieces_one,
        dense_end,
        with_tick(
            lambda p: settle(p, lambda q: stored(q, dd_out, pieces_one, turned_in), None), ticked
        ),
    )
    loop(
        dense_end,
        split,
        with_tick(
            lambda p: settle(p, lambda q: stored(q, do_out, dense_end, turned_in), None), ticked
        ),
    )
    ticked += split // 3

    def finish_line(q):
        tick(q)

        @pl.when(at_end)
        def _():
            line_back(q - LAG)

    @pl.when(at_end)
    def _():
        loop(0, ticked - LAG, line_back)

    loop(ticked, 2 * chunks + LAG, finish_line)

    for k in range(1, nt_axis):
        norm_copy(k).wait_recv()
        norm_copy(k).wait_send()
    held = norm_in[0]
    for i in range(1, nt_axis):
        held = held + norm_in[i]
    norms_out[...] = held if turned_in else held.T[0:8, :]

    loop(0, 2 * chunks, line_done)
    for p in range(5):
        gather_sent(p)
    for step in range(1, nc):
        small_copy(step, 0).wait_send()
        back_kv_copy(step).wait_send()
    for step in range(nc):
        for g in range(1, nf):
            small_copy(step, g).wait_send()

    def sent(p):
        for g in range(1, nf):
            half_copy(p, g).wait_send()
        for step in range(1, nc):
            piece_copy(p, step).wait_send()

    loop(0, split, sent)
    stage_done(split - 2)
    stage_done(split - 1)


def run_layer(sizes, *operands):
    nf, nc, tp = sizes["nf"], sizes["nc"], sizes["tp"]
    own, cols, ff, width = sizes["own"], sizes["cols"], sizes["ff"], sizes["width"]
    length, slots, total = sizes["length"], sizes["slots"], sizes["total"]
    part, split = sizes["part"], sizes["pieces_one"] + sizes["pieces_two"]
    rows = slots * length
    prompt = nc * length
    stacked = cols // HD * length
    edge = 3 * cols + ff
    chunks = rows // CHUNK
    sums = edge + width
    anywhere = pl.BlockSpec(memory_space=pl.ANY)
    vmem = pl.BlockSpec(memory_space=pltpu.VMEM)
    smem = pl.BlockSpec(memory_space=pltpu.SMEM)
    dma = pltpu.SemaphoreType.DMA
    shapes = (
        jax.ShapeDtypeStruct((2, rows, width), BF16),
        jax.ShapeDtypeStruct((3, own, cols), F32),
        jax.ShapeDtypeStruct((own, cols) if sizes["turned"] else (cols, own), F32),
        jax.ShapeDtypeStruct((own, ff), F32),
        jax.ShapeDtypeStruct((own, ff) if sizes["turned"] else (ff, own), F32),
        jax.ShapeDtypeStruct((8, sums), F32),
        jax.ShapeDtypeStruct((own, 128) if sizes["turned"] else (8, own), F32),
        jax.ShapeDtypeStruct((8, width), F32),
    )
    half = nf - 1
    keys = prompt + length
    scratch = [
        pltpu.VMEM((rows, width), BF16),
        pltpu.VMEM((rows, width), BF16),
        pltpu.VMEM((width, rows), BF16),
        pltpu.VMEM((width, total), BF16),
        pltpu.VMEM((rows, 2), F32),
        pltpu.VMEM((rows, 128), F32),
        pltpu.VMEM((rows, 128), F32),
        pltpu.VMEM((8, own), F32),
        pltpu.VMEM((nf * nc, 8, own), F32),
        pltpu.VMEM((1, ff), F32),
        pltpu.VMEM((keys, 2 * cols), BF16),
        pltpu.VMEM((cols, keys), BF16),
        pltpu.VMEM((cols, keys), BF16),
        pltpu.VMEM((cols, stacked), BF16),
        pltpu.VMEM((cols, stacked), BF16),
        pltpu.VMEM((cols, length), F32),
        pltpu.VMEM((cols, length), F32),
        pltpu.VMEM((2, max(keys, width), max(stacked, rows)), BF16),
        pltpu.VMEM((keys, length), F32),
        pltpu.VMEM((keys, length), F32),
        pltpu.VMEM((8, length), F32),
        pltpu.VMEM((rows, cols + ff), BF16),
        pltpu.VMEM((rows, edge), BF16),
        pltpu.VMEM((prompt, 2 * cols), F32),
        pltpu.VMEM((nc - 1, length, 2 * cols), BF16),
    ]
    scratch += [pltpu.VMEM((2, rows, width), BF16)] * 3
    scratch += [
        pltpu.VMEM((half, split, nc * own, part), BF16),
        pltpu.VMEM((half, split, nc * own, part), BF16),
        pltpu.VMEM((nc - 1, split, own, part), BF16),
        pltpu.VMEM((2, own, part), F32),
        pltpu.VMEM((2, part, own), F32),
        pltpu.VMEM((8, sums), F32),
        pltpu.VMEM((nf, 8, sums), F32),
        pltpu.VMEM((nc, 8, sums), F32),
        pltpu.VMEM((own, 128), F32),
        pltpu.VMEM((tp, own, 128), F32),
        dma((10,)),
        dma((2, nc, nf)),
        dma((5, 6)),
        dma((5, 6)),
        dma((5, nc, half)),
        dma((5, nc, half)),
        dma((6,)),
        dma((6,)),
        dma((nc - 1,)),
        dma((nc - 1,)),
        dma((2 * chunks,)),
        dma((2 * chunks,)),
        dma((2 * chunks,)),
        dma((2 * chunks,)),
        dma((2 * chunks,)),
        dma((half, split)),
        dma((half, split)),
        dma((nc - 1, split)),
        dma((nc - 1, split)),
        dma((2, max(half, nc - 1))),
        dma((2, max(half, nc - 1))),
        dma((tp - 1,)),
        dma((tp - 1,)),
        dma((2,)),
    ]
    return pl.pallas_call(
        functools.partial(layer_kernel, sizes),
        out_shape=shapes,
        in_specs=[smem, vmem] + [anywhere] * 8 + [vmem] * (len(operands) - 10),
        out_specs=(anywhere,) * 5 + (vmem,) * 3,
        scratch_shapes=scratch,
        compiler_params=pltpu.CompilerParams(
            collective_id=0, has_side_effects=True, vmem_limit_bytes=MEMORY
        ),
        name="layer",
    )(*operands)


def close_kernel(sizes, *refs):
    nc, own, cols, ff = sizes["nc"], sizes["own"], sizes["cols"], sizes["ff"]
    first, turned = 3 * cols, sizes["turned"]
    edge = first + ff
    prompt_blocks = sizes["length"] // BLOCK
    refs = list(refs)

    def take(count):
        taken = refs[:count]
        del refs[:count]
        return taken

    x_prompt, x_cont, dy_prompt, dy_cont, totals, shifts, sums, norms = take(8)
    given = take(4)
    y_prompt, y_cont, dx_prompt, dx_cont, b_qkv, b_u = take(6)
    singles = take(0 if turned else 6)
    taken = take(4)
    at = pl.program_id(0)
    for source, target in zip(given, taken):
        target[...] = source[...]

    def rows_of(x_ref, dy_ref, y_ref, dx_ref):
        x = x_ref[...].astype(F32)
        u = totals[1].astype(F32)
        centered = x - jnp.mean(x, axis=1, keepdims=True)
        scale = lax.rsqrt(jnp.mean(centered * centered, axis=1, keepdims=True) + EPS)
        unit = centered * scale
        u = u - jnp.mean(u, axis=1, keepdims=True) - unit * jnp.mean(u * unit, axis=1, keepdims=True)
        y_ref[...] = x + totals[0].astype(F32) + (shifts[0:1, :] + shifts[1:2, :])
        dx_ref[...] = dy_ref[...].astype(F32) + scale * u

    @pl.when(at < prompt_blocks)
    def _():
        rows_of(x_prompt, dy_prompt, y_prompt, dx_prompt)

    @pl.when(at >= prompt_blocks)
    def _():
        rows_of(x_cont, dy_cont, y_cont, dx_cont)

    @pl.when(at == 0)
    def _():
        for i in range(3):
            b_qkv[i : i + 1, :] = sums[0:1, i * cols : (i + 1) * cols]
        b_u[...] = sums[0:1, first:edge]
        if not turned:
            for i in range(4):
                singles[i][...] = norms[i : i + 1, :]
            shard = lax.axis_index("fsdp") * nc + lax.axis_index("ctx")
            lanes = pl.ds(pl.multiple_of(edge + shard * own, own), own)
            singles[4][...] = sums[0:1, lanes]
            singles[5][...] = sums[0:1, lanes]


def close_layer(sizes, *operands):
    own, cols, ff, width = sizes["own"], sizes["cols"], sizes["ff"], sizes["width"]
    length, slots, turned = sizes["length"], sizes["slots"], sizes["turned"]
    near = length // BLOCK
    blocks = slots * near
    prompt = pl.BlockSpec((BLOCK, width), lambda i: (jnp.minimum(i, near - 1), 0))
    cont = pl.BlockSpec((BLOCK, width), lambda i: (jnp.maximum(i - near, 0), 0))
    both = pl.BlockSpec((2, BLOCK, width), lambda i: (0, i, 0))

    def fixed(*shape):
        return pl.BlockSpec(shape, lambda i: (0,) * len(shape))

    def array(*shape):
        return jax.ShapeDtypeStruct(shape, F32)

    kept = [(3, cols), (1, ff)] + ([] if turned else [(1, own)] * 6)
    given = [tuple(o.shape) for o in operands[8:]]

    def shared(shape):
        axis = len(shape) - 2
        if shape[axis] % (8 * blocks):
            return fixed(*shape)
        block = shape[:axis] + (shape[axis] // blocks,) + shape[axis + 1 :]
        return pl.BlockSpec(block, lambda i: (0,) * axis + (i, 0))

    moved = [shared(shape) for shape in given]
    rows_prompt, rows_cont = array(length, width), array((slots - 1) * length, width)
    return pl.pallas_call(
        functools.partial(close_kernel, sizes),
        grid=(blocks,),
        in_specs=[prompt, cont, prompt, cont, both]
        + [fixed(*o.shape) for o in operands[5:8]]
        + moved,
        out_specs=[prompt, cont, prompt, cont] + [fixed(*shape) for shape in kept] + moved,
        out_shape=[rows_prompt, rows_cont, rows_prompt, rows_cont]
        + [array(*shape) for shape in kept + given],
        compiler_params=pltpu.CompilerParams(vmem_limit_bytes=62 * 1024 * 1024),
        name="close",
    )(*operands)


def on_device(
    x_prompt,
    x_cont,
    cont_start,
    w_qkv,
    qkv_bias,
    w_dense,
    dense_bias,
    w_fc1,
    fc1_bias,
    w_fc2,
    fc2_bias,
    ln1_gain,
    ln1_bias,
    ln2_gain,
    ln2_bias,
    dy_prompt,
    dy_cont,
):
    length = x_prompt.shape[1]
    conts, cont_len, width = x_cont.shape[1:]
    own, _, cols = w_qkv.shape
    ff = w_fc1.shape[1]
    nf, nc, tp = (lax.axis_size(name) for name in ("fsdp", "ctx", "tp"))
    edge = 3 * cols + ff
    part = 256 if edge % 256 == 0 and (cols + ff) % 256 == 0 else 128
    sizes = {
        "nf": nf,
        "nc": nc,
        "tp": tp,
        "own": own,
        "cols": cols,
        "ff": ff,
        "width": width,
        "length": length,
        "slots": 1 + conts,
        "total": 4 * cols + 2 * ff,
        "part": part,
        "pieces_one": edge // part,
        "pieces_two": (cols + ff) // part,
        "turned": own % 128 != 0,
    }
    turned = [w_dense.T, w_fc2.T] if sizes["turned"] else [w_dense, w_fc2]
    lane = np.arange(128) % HD
    inverse = 10000.0 ** (-2.0 * (lane % (ROT // 2)) / ROT)
    freq = np.zeros((8, 128), np.float32)
    freq[0] = np.where(lane < ROT, inverse, 0.0)
    freq[1] = np.where(lane < ROT // 2, -1.0, 1.0)
    vectors = [dense_bias, fc2_bias, ln1_gain, ln1_bias, ln2_gain, ln2_bias]
    if sizes["turned"]:
        stacked = jnp.pad(jnp.stack(vectors).astype(F32), ((0, 2), (0, 0)))
        vectors = [stacked, stacked.T]
    totals, d_q, d_d, d_u, d_o, sums, norms, small_full = run_layer(
        sizes,
        cont_start,
        jnp.asarray(freq),
        x_prompt[0],
        x_cont.reshape(conts * cont_len, width),
        dy_prompt[0],
        dy_cont.reshape(conts * cont_len, width),
        w_qkv.transpose(1, 0, 2),
        turned[0],
        w_fc1,
        turned[1],
        *vectors,
        qkv_bias,
        fc1_bias,
    )
    tokens = conts * cont_len
    closed = close_layer(
        sizes,
        x_prompt[0],
        x_cont.reshape(tokens, width),
        dy_prompt[0],
        dy_cont.reshape(tokens, width),
        totals,
        small_full,
        sums,
        norms,
        d_q,
        d_d,
        d_u,
        d_o,
    )
    y_prompt, y_cont, dx_prompt, dx_cont, b_qkv, b_u = closed[:6]
    d_qkv, d_dense, d_u, d_o = closed[-4:]
    if sizes["turned"]:
        d_dense, d_o = d_dense.T, d_o.T
        four = [norms[:, i] for i in range(4)]
        place = (lax.axis_index("fsdp") * nc + lax.axis_index("ctx")) * own
        shifts = [lax.dynamic_slice_in_dim(sums[0, edge:], place, own)] * 2
    else:
        *four, shift_one, shift_two = (row.reshape(own) for row in closed[6:12])
        shifts = [shift_one, shift_two]
    shape = x_cont.shape
    return (
        y_prompt[None],
        y_cont.reshape(shape),
        dx_prompt[None],
        dx_cont.reshape(shape),
        d_qkv.transpose(1, 0, 2),
        b_qkv,
        d_dense,
        shifts[0],
        d_u,
        b_u.reshape(ff),
        d_o,
        shifts[1],
        four[0],
        four[1],
        four[2],
        four[3],
    )


def solution(mesh):
    both = ("fsdp", "ctx")
    rows = P("fsdp", "ctx", None)
    conts = P("fsdp", "ctx", None, None)
    vector = P(both)
    return jax.shard_map(
        on_device,
        mesh=mesh,
        in_specs=(
            rows,
            conts,
            P("fsdp", "ctx"),
            P(both, None, "tp"),
            P(None, "tp"),
            P("tp", both),
            vector,
            P(both, "tp"),
            P("tp"),
            P("tp", both),
            vector,
            vector,
            vector,
            vector,
            vector,
            rows,
            conts,
        ),
        out_specs=(
            rows,
            conts,
            rows,
            conts,
            P(both, None, "tp"),
            P(None, "tp"),
            P("tp", both),
            vector,
            P(both, "tp"),
            P("tp"),
            P("tp", both),
            vector,
            vector,
            vector,
            vector,
            vector,
        ),
        check_vma=False,
    )
```

```python
import functools

import jax
import jax.numpy as jnp
import numpy as np
from jax import lax
from jax.experimental import pallas as pl
from jax.experimental.pallas import tpu as pltpu
from jax.sharding import PartitionSpec as P

HD = 64
ROT = 16
EPS = 1e-05
MASKED = -1e30
F32 = jnp.float32
BF16 = jnp.bfloat16
MESH = pl.DeviceIdType.MESH
CHUNK = 64
BLOCK = 128
MEMORY = 63 * 1024 * 1024
LAG = 2
PACE = 1
BEHIND = 3
ERF = (0.254829592, -0.284496736, 1.421413741, -1.453152027, 1.061405429)


def nn(left, right):
    return jnp.dot(left, right, preferred_element_type=F32)


def nt(left, right):
    return lax.dot_general(left, right, (((1,), (1,)), ((), ())), preferred_element_type=F32)


def remote(src, dst, send_sem, recv_sem, device):
    return pltpu.make_async_remote_copy(
        src_ref=src,
        dst_ref=dst,
        send_sem=send_sem,
        recv_sem=recv_sem,
        device_id=device,
        device_id_type=MESH,
    )


def turn(values, cos_t, sin_t):
    lane = lax.broadcasted_iota(jnp.int32, cos_t.shape, 1)
    low_half = lax.rem(lane, HD) < ROT // 2
    pieces = []
    for start in range(0, values.shape[1], 128):
        piece = values[:, start : start + 128]
        up = pltpu.roll(piece, 128 - ROT // 2, 1)
        down = pltpu.roll(piece, ROT // 2, 1)
        pieces.append(piece * cos_t + jnp.where(low_half, up, down) * sin_t)
    return jnp.concatenate(pieces, axis=1) if len(pieces) > 1 else pieces[0]


def layer_kernel(sizes, *refs):
    nf, nc, nt_axis = sizes["nf"], sizes["nc"], sizes["tp"]
    own, cols, ff, width = sizes["own"], sizes["cols"], sizes["ff"], sizes["width"]
    length, slots, total = sizes["length"], sizes["slots"], sizes["total"]
    part, pieces_one, pieces_two = sizes["part"], sizes["pieces_one"], sizes["pieces_two"]
    turned_in = sizes["turned"]
    refs = list(refs)

    def take(count):
        taken = refs[:count]
        del refs[:count]
        return taken

    starts, freq, x_prompt, x_cont, dy_prompt, dy_cont, w_q, w_d, w_u, w_o = take(10)
    vectors = take(1 if turned_in else 6)
    small_t = take(1)[0] if turned_in else None
    bias_q, bias_up = take(2)
    tot_out, dq_out, dd_out, du_out, do_out, sums_out, norms_out, small_out = take(8)
    xv, dyv, n_t, wall = take(4)
    stat_s, cos_s, sin_s, small, smallg, bias_u = take(6)
    kvp, k_t, v_t, q_t, g_t, o_t, dq_t, p_all, score_s, slope_s, share_s = take(11)
    oa, gd, acc, kv_recv = take(4)
    part_sum, from_out, from_in, half_send, half_recv, piece_recv, stage, stage_t = take(8)
    sum_own, sum_f, sum_c, norm_own, norm_in = take(5)
    in_sem, small_sem, ws, wr, fs, fr, kvs, kvr, gks, gkr = take(10)
    zs, za, zbs, zb, zo, hs, hr, ps, pr, ss, sr, ns, nr, os = take(14)
    f, c, t = lax.axis_index("fsdp"), lax.axis_index("ctx"), lax.axis_index("tp")
    heads = cols // HD
    rows_all = slots * length
    pair = slots // 2
    prompt = nc * length
    first = 3 * cols
    edge = first + ff
    shard = f * nc + c
    own_rows = pl.ds(pl.multiple_of(shard * own, own), own)

    def ctx_to(step):
        return (f, lax.rem(c + step, nc), t)

    def ctx_from(step):
        return lax.rem(c + nc - step, nc)

    across_x = c + 1 - 2 * lax.rem(c, 2)
    across_y = lax.rem(c + 2, nc)
    corner = lax.rem(across_x + 2, nc)
    peers = (c, across_x, across_y, corner)

    def mate_to(step):
        return (lax.rem(f + step, nf), c, t)

    def mate_from(step):
        return lax.rem(f + nf - step, nf)

    def tp_to(step):
        return (f, c, lax.rem(t + step, nt_axis))

    upper = lax.div(t, nt_axis // 2)
    inward = (f, c, t + 1 - 2 * upper)
    outward = (f, c, lax.rem(t - 1 + 2 * upper + nt_axis, nt_axis))
    at_end = (t == 0) | (t == nt_axis - 1)
    not_end = (t != 0) & (t != nt_axis - 1)
    in_middle = (t == nt_axis // 2 - 1) | (t == nt_axis // 2)
    not_middle = (t != nt_axis // 2 - 1) & (t != nt_axis // 2)

    loads = [
        (x_prompt, xv.at[pl.ds(0, length)]),
        (x_cont, xv.at[pl.ds(length, rows_all - length)]),
        (dy_prompt, dyv.at[pl.ds(0, length)]),
        (dy_cont, dyv.at[pl.ds(length, rows_all - length)]),
        (w_q.at[0], wall.at[own_rows, pl.ds(0, cols)]),
        (w_q.at[1], wall.at[own_rows, pl.ds(cols, cols)]),
        (w_q.at[2], wall.at[own_rows, pl.ds(2 * cols, cols)]),
        (w_u, wall.at[own_rows, pl.ds(first, ff)]),
    ]
    if turned_in:
        loads += [
            (w_d, wall.at[own_rows, pl.ds(edge, cols)]),
            (w_o, wall.at[own_rows, pl.ds(edge + cols, ff)]),
        ]
    else:
        loads += [
            (w_d, p_all.at[1, pl.ds(0, cols), pl.ds(0, own)]),
            (w_o, p_all.at[0, pl.ds(0, ff), pl.ds(0, own)]),
        ]
    loads = [pltpu.make_async_copy(src, dst, in_sem.at[i]) for i, (src, dst) in enumerate(loads)]
    for i in (4, 5, 6, 0, 1, 8, 7, 9, 2, 3):
        loads[i].start()

    barrier = pltpu.get_barrier_semaphore()
    greeted = [ctx_to(k) for k in range(1, nc)]
    greeted += [mate_to(g) for g in range(1, nf)]
    greeted += [tp_to(k) for k in range(1, nt_axis)]
    for device in greeted:
        pl.semaphore_signal(barrier, inc=1, device_id=device, device_id_type=MESH)
    pl.semaphore_wait(barrier, len(greeted))

    spans = (
        (0, first),
        (edge, cols),
        (first, ff // 2),
        (first + ff // 2, ff // 2),
        (edge + cols, ff),
    )

    half_own = own // 2

    def block(owner, side, size):
        base = owner * size
        if side is None:
            return pl.ds(pl.multiple_of(base, size), size)
        return pl.ds(pl.multiple_of(base + side * (size // 2), size // 2), size // 2)

    routes = ((0, 0, 1), (0, 1, 2), (0, 1, 1), (0, 0, 2), (1, 0, 2), (2, 1, 1))
    lands = ((1, 0), (2, 1), (1, 1), (2, 0), (3, 0), (3, 1))

    def ctx_copy(route, source, target, size, send_sem, recv_sem):
        owner, side, to = routes[route]
        rows = block(peers[owner], side, size)
        src = source(owner, side, rows)
        return remote(src, target(rows), send_sem, recv_sem, (f, peers[to], t))

    def lanes_of(p):
        return pl.ds(spans[p][0], spans[p][1])

    def gather_copy(p, route):
        def place(rows):
            return wall.at[pl.ds(rows.start + f * nc * own, half_own), lanes_of(p)]

        return ctx_copy(
            route, lambda owner, side, rows: place(rows), place, own, ws.at[p, route], wr.at[p, route]
        )

    def mate_copy(p, peer, g):
        place = wall.at[block(f * nc + peers[peer], None, own), lanes_of(p)]
        return remote(
            place, place, fs.at[p, peer, g - 1], fr.at[p, peer, g - 1], mate_to(g)
        )

    def gather_start(p):
        for route in range(4):
            gather_copy(p, route).start()
        for g in range(1, nf):
            mate_copy(p, 0, g).start()

    def gather_relay(p):
        for arrived, route in ((0, 4), (1, 5)):
            gather_copy(p, arrived).wait_recv()
            gather_copy(p, route).start()

    def gather_pass(p):
        for peer, rest in ((1, (2,)), (2, (3,)), (3, (4, 5))):
            for route in rest:
                gather_copy(p, route).wait_recv()
            for g in range(1, nf):
                mate_copy(p, peer, g).start()

    def gather_finish(p):
        for peer in range(nc):
            for g in range(1, nf):
                mate_copy(p, peer, g).wait_recv()

    def gather_sent(p):
        for route in range(6):
            gather_copy(p, route).wait_send()
        for peer in range(nc):
            for g in range(1, nf):
                mate_copy(p, peer, g).wait_send()

    def small_copy(step, g):
        if g == 0:
            return remote(
                small, smallg.at[shard], small_sem.at[0, step, 0], small_sem.at[1, step, 0], ctx_to(step)
            )
        held = f * nc + ctx_from(step)
        src = small if step == 0 else smallg.at[held]
        return remote(
            src, smallg.at[held], small_sem.at[0, step, g], small_sem.at[1, step, g], mate_to(g)
        )

    if turned_in:
        small[...] = vectors[0][...]
    else:
        small[...] = jnp.zeros_like(small)
        for i, vector in enumerate(vectors):
            small[i : i + 1, :] = vector[...].astype(F32).reshape(1, own)
    bias_u[...] = bias_up[...].astype(F32).reshape(1, ff)
    for step in range(1, nc):
        small_copy(step, 0).start()
    for g in range(1, nf):
        small_copy(0, g).start()
    for i in (4, 5, 6):
        loads[i].wait()
    gather_start(0)
    loads[8].wait()
    if not turned_in:
        wall[own_rows, edge : edge + cols] = p_all[1, 0:cols, 0:own].astype(F32).T.astype(BF16)
    smallg[shard] = small[...]
    loads[7].wait()
    gather_relay(0)
    gather_start(1)
    gather_start(2)

    loads[0].wait()
    loads[1].wait()

    def statistics(slot):
        rows = pl.ds(pl.multiple_of(slot * length, length), length)
        block_x = xv[rows, :].astype(F32)
        mean = jnp.mean(block_x, axis=1, keepdims=True)
        block_x = block_x - mean
        scale = lax.rsqrt(jnp.mean(block_x * block_x, axis=1, keepdims=True) + EPS)
        stat_s[rows, 0:1] = mean
        stat_s[rows, 1:2] = scale
        n_t[:, rows] = (block_x * scale).T.astype(BF16)
        before = starts[0, jnp.maximum(slot - 1, 0)]
        base = jnp.where(slot == 0, c * length, before)
        place = base + lax.broadcasted_iota(jnp.int32, (length, 128), 0)
        phase = place.astype(F32) * freq[0:1, :]
        cos_s[rows, :] = jnp.cos(phase)
        sin_s[rows, :] = jnp.sin(phase) * freq[1:2, :]

    def loop(low, high, body):
        lax.fori_loop(low, high, lambda i, carry: (body(i), carry)[1], 0)

    statistics(0)
    for step in range(1, nc):
        small_copy(step, 0).wait_recv()
        for g in range(1, nf):
            small_copy(step, g).start()
    gather_relay(1)
    statistics(1)
    gather_relay(2)
    gather_pass(0)
    loop(2, slots - 1, statistics)
    for step in range(nc):
        for g in range(1, nf):
            small_copy(step, g).wait_recv()
    parts = [smallg[i] for i in range(nf * nc)]
    small_out[...] = jnp.concatenate(parts, axis=1)
    gain_one, shift_one = small_out[2:3, :], small_out[3:4, :]
    gain_two, shift_two = small_out[4:5, :], small_out[5:6, :]

    def normed(rows, gain, shift):
        block = (xv[rows, :].astype(F32) - stat_s[rows, 0:1]) * stat_s[rows, 1:2]
        return (block * gain + shift).astype(BF16)

    gather_finish(0)

    def project(slot):
        rows = pl.ds(pl.multiple_of(slot * length, length), length)
        both = nn(normed(rows, gain_one, shift_one), wall[:, 0:first])
        cos_t, sin_t = cos_s[rows, :], sin_s[rows, :]
        query = both[:, 0:cols] + bias_q[0:1, :].astype(F32)
        key = both[:, cols : 2 * cols] + bias_q[1:2, :].astype(F32)
        value = both[:, 2 * cols : first] + bias_q[2:3, :].astype(F32)
        gd[rows, 0:cols] = (turn(query, cos_t, sin_t) * 0.125).astype(BF16)
        gd[rows, cols : 2 * cols] = turn(key, cos_t, sin_t).astype(BF16)
        gd[rows, 2 * cols : first] = value.astype(BF16)

    project(0)
    mine = pl.ds(pl.multiple_of(c * length, length), length)
    kvp[mine, :] = gd[0:length, cols:first]

    def kv_copy(route):
        def source(owner, side, rows):
            if owner == 0:
                return gd.at[pl.ds(side * (length // 2), length // 2), pl.ds(cols, 2 * cols)]
            return kvp.at[rows]

        return ctx_copy(
            route, source, lambda rows: kvp.at[rows], length, kvs.at[route], kvr.at[route]
        )

    for route in range(4):
        kv_copy(route).start()
    gather_pass(1)
    loads[9].wait()
    if not turned_in:
        wall[own_rows, edge + cols : total] = p_all[0, 0:ff, 0:own].astype(F32).T.astype(BF16)
    statistics(slots - 1)
    for arrived, route in ((0, 4), (1, 5)):
        kv_copy(arrived).wait_recv()
        kv_copy(route).start()
    gather_start(3)
    gather_start(4)
    loop(1, slots, project)
    gather_relay(3)
    gather_finish(1)
    gather_pass(2)
    loads[2].wait()
    loads[3].wait()

    def back_dense(slot):
        rows = pl.ds(pl.multiple_of(slot * length, length), length)
        block_dy = dyv[rows, :]
        oa[rows, 0:cols] = nn(block_dy, wall[:, edge : edge + cols]).astype(BF16)

    loop(0, slots, back_dense)

    for route in range(2, 6):
        kv_copy(route).wait_recv()
    k_t[:, 0:prompt] = kvp[0:prompt, 0:cols].astype(F32).T.astype(BF16)
    v_t[:, 0:prompt] = kvp[0:prompt, cols : 2 * cols].astype(F32).T.astype(BF16)

    def fold(block_of, combine):
        return combine(block_of.reshape(-1, 8, block_of.shape[1]), axis=0)

    def attend(slot, is_prompt, between=()):
        rows = pl.ds(pl.multiple_of(slot * length, length), length)
        span = prompt if is_prompt else prompt + length
        stacked = heads * length
        head_row = lax.div(lax.broadcasted_iota(jnp.int32, (cols, length), 0), HD)
        query = gd[rows, 0:cols].astype(F32).T.astype(BF16)
        grad = oa[rows, 0:cols].astype(F32).T.astype(BF16)
        zero = jnp.zeros_like(query)
        for h in range(heads):
            q_t[:, h * length : (h + 1) * length] = jnp.where(head_row == h, query, zero)
            g_t[:, h * length : (h + 1) * length] = jnp.where(head_row == h, grad, zero)
        key_at = lax.broadcasted_iota(jnp.int32, (length, length), 0)
        query_at = lax.broadcasted_iota(jnp.int32, (length, length), 1)
        if is_prompt:
            limit = query_at + (c * length + 1)
        else:
            kvp[prompt:span, :] = gd[rows, cols:first]
            k_t[:, prompt:span] = gd[rows, cols : 2 * cols].astype(F32).T.astype(BF16)
            v_t[:, prompt:span] = gd[rows, 2 * cols : first].astype(F32).T.astype(BF16)
            limit = starts[0, slot - 1]

        def lanes(h):
            return slice(h * length, (h + 1) * length)

        def lines(h):
            return slice(h * HD, (h + 1) * HD)

        def score(h):
            for b in range(0, span, length):
                keys = slice(b, b + length)
                score_s[keys, :] = nn(kvp[keys, 0:cols], q_t[:, lanes(h)])

        def slope(h):
            for b in range(0, span, length):
                keys = slice(b, b + length)
                slope_s[keys, :] = nn(kvp[keys, cols : 2 * cols], g_t[:, lanes(h)])

        def mask():
            highest = jnp.full((8, length), MASKED, F32)
            for b in range(0, span, length):
                seen = key_at + b < limit if b < prompt else key_at <= query_at
                scores = jnp.where(seen, score_s[b : b + length, :], MASKED)
                score_s[b : b + length, :] = scores
                highest = jnp.maximum(highest, fold(scores, jnp.max))
            return jnp.max(highest, axis=0, keepdims=True)

        def raise_up(h, highest):
            norm = jnp.zeros((8, length), F32)
            for b in range(0, span, length):
                raised = jnp.exp(score_s[b : b + length, :] - highest)
                norm = norm + fold(raised, jnp.sum)
                p_all[0, b : b + length, lanes(h)] = raised.astype(BF16)
            share = 1.0 / jnp.sum(norm, axis=0, keepdims=True)
            share_s[h : h + 1, :] = share
            return share

        score(0)
        slope(0)
        share = raise_up(0, mask())
        for h in range(heads):
            out_t = nn(v_t[lines(h), 0:span], p_all[0, 0:span, lanes(h)]) * share
            o_t[lines(h), :] = out_t
            if h + 1 < heads:
                score(h + 1)
            inner = jnp.sum(out_t * g_t[lines(h), lanes(h)].astype(F32), axis=0, keepdims=True)
            for b in range(0, span, length):
                raised = p_all[0, b : b + length, lanes(h)].astype(F32)
                low = (raised * (slope_s[b : b + length, :] - inner)).astype(BF16)
                p_all[1, b : b + length, lanes(h)] = low
            dq_t[lines(h), :] = nn(k_t[lines(h), 0:span], p_all[1, 0:span, lanes(h)]) * share
            if h + 1 < heads:
                slope(h + 1)
                share = raise_up(h + 1, mask())
            for at, action in between:
                if at == h:
                    action()
        for h in range(heads):
            share = share_s[h : h + 1, :]
            q_t[:, lanes(h)] = (q_t[:, lanes(h)].astype(F32) * share).astype(BF16)
            g_t[:, lanes(h)] = (g_t[:, lanes(h)].astype(F32) * share).astype(BF16)
        cos_t, sin_t = cos_s[rows, :], -sin_s[rows, :]
        oa[rows, 0:cols] = o_t[...].T.astype(BF16)
        gd[rows, 0:cols] = turn(dq_t[...].T * 0.125, cos_t, sin_t).astype(BF16)
        acc[:, 0:cols] += nt(p_all[1, 0:prompt, 0:stacked], q_t[...])
        acc[:, cols : 2 * cols] += nt(p_all[0, 0:prompt, 0:stacked], g_t[...])
        if not is_prompt:
            back_k = nt(p_all[1, prompt:span, 0:stacked], q_t[...])
            gd[rows, cols : 2 * cols] = turn(back_k, cos_t, sin_t).astype(BF16)
            gd[rows, 2 * cols : first] = nt(p_all[0, prompt:span, 0:stacked], g_t[...]).astype(BF16)

    def kv_send(step):
        return p_all.at[1, pl.ds((step - 1) * length, length), pl.ds(0, 2 * cols)]

    def back_kv_copy(step):
        return remote(
            kv_send(step), kv_recv.at[step - 1], gks.at[step - 1], gkr.at[step - 1], ctx_to(step)
        )

    chunks = rows_all // CHUNK
    per_slot = length // CHUNK

    def line(q):
        which, place = lax.div(q, chunks), lax.rem(q, chunks)
        slot = lax.rem(lax.div(place, per_slot) + 1, slots)
        inner = lax.rem(place, per_slot)
        return which, pl.ds(pl.multiple_of((slot * per_slot + inner) * CHUNK, CHUNK), CHUNK)

    def line_out(q, middle):
        which, rows = line(q)
        target = from_in if middle else from_out
        landed = zb if middle else za
        return remote(
            part_sum.at[which, rows], target.at[which, rows], zs.at[q], landed.at[q], inward
        )

    def line_home(q, middle):
        which, rows = line(q)
        src = from_out if middle else from_in
        return remote(
            src.at[which, rows], from_in.at[which, rows], zbs.at[q], zb.at[q], outward
        )

    def line_store(q, middle):
        which, rows = line(q)
        src = from_out if middle else from_in
        return pltpu.make_async_copy(src.at[which, rows], tot_out.at[which, rows], zo.at[q])

    def line_send(q):
        @pl.when(in_middle)
        def _():
            line_out(q, True).start()

        @pl.when(not_middle)
        def _():
            line_out(q, False).start()

    def line_first(q):
        @pl.when(at_end)
        def _():
            line_send(q)

    def line_add(q):
        which, rows = line(q)

        @pl.when(not_end)
        def _():
            line_out(q, False).wait_recv()
            part_sum[which, rows, :] = (
                part_sum[which, rows, :].astype(F32) + from_out[which, rows, :].astype(F32)
            ).astype(BF16)
            line_send(q)

    def line_back(q):
        which, rows = line(q)

        @pl.when(in_middle)
        def _():
            line_out(q, True).wait_recv()
            from_out[which, rows, :] = (
                part_sum[which, rows, :].astype(F32) + from_in[which, rows, :].astype(F32)
            ).astype(BF16)

            @pl.when(not_end)
            def _():
                line_home(q, True).start()

            line_store(q, True).start()

        @pl.when(not_middle)
        def _():
            line_home(q, False).wait_recv()

            @pl.when(not_end)
            def _():
                line_home(q, False).start()

            line_store(q, False).start()

    def line_done(q):
        line_out(q, True).wait_send()
        line_store(q, True).wait()

        @pl.when(not_end)
        def _():
            line_home(q, True).wait_send()

    def step_line(q):
        @pl.when(q < 2 * chunks)
        def _():
            line_add(q)

        @pl.when((q >= LAG) & not_end)
        def _():
            line_back(q - LAG)

    def tick(k):
        for i in range(PACE):
            step_line(k * PACE + i)

    def feed(position):
        slot = lax.rem(position + 1, slots)
        rows = pl.ds(pl.multiple_of(slot * length, length), length)
        inputs = normed(rows, gain_two, shift_two)
        for at in range(0, ff, ff // 2):
            units = slice(at, at + ff // 2)
            up = slice(first + at, first + at + ff // 2)
            hidden = nn(inputs, wall[:, up]) + bias_u[:, units]
            depth = jnp.abs(hidden) * np.float32(0.5**0.5)
            step = 1.0 / (1.0 + np.float32(0.3275911) * depth)
            poly = np.float32(ERF[4])
            for factor in ERF[3::-1]:
                poly = poly * step + np.float32(factor)
            bell = jnp.exp(-(depth * depth))
            tail = 0.5 * (poly * step) * bell
            below = jnp.where(hidden >= 0.0, 1.0 - tail, tail)
            oa[rows, cols + at : cols + at + ff // 2] = (hidden * below).astype(BF16)
            slope = below + hidden * (bell * np.float32((2.0 * np.pi) ** -0.5))
            for b in range(0, ff // 2, length):
                lines = slice(at + b, at + b + length)
                score_s[lines, :] = slope[:, b : b + length]
        part_sum[0, rows, :] = nt(oa[rows, :], wall[:, edge:total]).astype(BF16)
        for i in range(per_slot):
            line_first(position * per_slot + i)
        for at in range(0, ff, length):
            down = slice(edge + cols + at, edge + cols + at + length)
            back = nn(dyv[rows, :], wall[:, down])
            gd[rows, first + at : first + at + length] = (
                back * score_s[at : at + length, :]
            ).astype(BF16)

    def back_norms(position):
        slot = lax.rem(position + 1, slots)
        rows = pl.ds(pl.multiple_of(slot * length, length), length)
        toward_x = nt(gd[rows, 0:first], wall[:, 0:first]) * gain_one
        toward_x = toward_x + nt(gd[rows, first:edge], wall[:, first:edge]) * gain_two
        part_sum[1, rows, :] = toward_x.astype(BF16)
        for i in range(per_slot):
            line_first(chunks + position * per_slot + i)

    acc[...] = jnp.zeros_like(acc)

    def at_slot(slot, wanted, *steps):
        def action():
            @pl.when(slot == wanted)
            def _():
                for step in steps:
                    step()

        return action

    def attend_cont(slot):
        attend(
            slot,
            False,
            (
                (heads // 2, at_slot(slot, 1, lambda: gather_relay(4))),
                (heads // 2, at_slot(slot, pair, lambda: gather_pass(3))),
            ),
        )

    loop(1, pair + 1, attend_cont)
    gather_pass(4)
    for p in (2, 3, 4):
        gather_finish(p)
    loop(0, pair, feed)
    for slot in range(pair + 1, slots):
        attend(slot, False, ((1, lambda: tick(0)), (heads - 1, lambda: tick(1))))
        feed(slot - 1)
    tick(2)
    attend(0, True, ((0, lambda: tick(3)), (heads // 2, lambda: tick(4))))
    for step in range(1, nc):
        there = pl.ds(pl.multiple_of(lax.rem(c + step, nc) * length, length), length)
        kv_send(step)[...] = acc[there, :].astype(BF16)
        back_kv_copy(step).start()
    tick(5)
    feed(slots - 1)
    tick(6)
    loop(0, pair, back_norms)
    tick(7)
    loop(pair, slots - 1, back_norms)
    tick(8)

    def turn_dy(slot):
        rows = pl.ds(pl.multiple_of(slot * length, length), length)
        p_all[0, 0:width, rows] = dyv[rows, :].astype(F32).T.astype(BF16)

    loop(0, slots, turn_dy)
    tick(9)

    group = nc * own
    split = pieces_one + pieces_two

    def product(p, rows, second):
        lanes = pl.ds(pl.multiple_of(p * part, part), part)
        if second:
            return nn(p_all[0, rows, 0:rows_all], oa[:, lanes])
        return nn(n_t[rows, :], gd[:, lanes])

    def half_copy(p, g):
        return remote(
            half_send.at[g - 1, p], half_recv.at[g - 1, p], hs.at[g - 1, p], hr.at[g - 1, p], mate_to(g)
        )

    def piece_copy(p, step):
        rows = pl.ds(pl.multiple_of(lax.rem(c + step, nc) * own, own), own)
        return remote(
            half_recv.at[0, p, rows],
            piece_recv.at[step - 1, p],
            ps.at[step - 1, p],
            pr.at[step - 1, p],
            ctx_to(step),
        )

    def give_half(p, base, second):
        for g in range(1, nf):
            rows = pl.ds(pl.multiple_of(lax.rem(f + g, nf) * group, group), group)
            half_send[g - 1, p] = product(p - base, rows, second).astype(BF16)
            half_copy(p, g).start()

    def keep_half(p, base, second):
        rows = pl.ds(pl.multiple_of(f * group, group), group)
        kept = product(p - base, rows, second)
        for g in range(1, nf):
            half_copy(p, g).wait_recv()
            kept = kept + half_recv[g - 1, p].astype(F32)
        half_recv[0, p] = kept.astype(BF16)
        for step in range(1, nc):
            piece_copy(p, step).start()

    early = first // part

    def with_tick(body, start, lowest=0):
        def step(p):
            body(p)

            @pl.when((lax.rem(p, 3) == 2) & (p >= lowest))
            def _():
                tick(start + lax.div(p, 3))

        return step

    give_start, keep_start, lowest = 8, 10, 2 * early
    for start, body in ((give_start, give_half), (keep_start, keep_half)):
        one = with_tick(lambda p, body=body: body(p, 0, False), start, lowest)
        two = with_tick(lambda p, body=body: body(p, pieces_one, True), start, lowest)
        loop(early, pieces_one, one)
        loop(pieces_one, split, two)
    ticked = keep_start + split // 3

    for route in range(6):
        kv_copy(route).wait_send()
    grad_kv = acc[mine, :]
    for step in range(1, nc):
        back_kv_copy(step).wait_recv()
        grad_kv = grad_kv + kv_recv[step - 1].astype(F32)
    gd[0:length, cols : 2 * cols] = turn(
        grad_kv[:, 0:cols], cos_s[0:length, :], -sin_s[0:length, :]
    ).astype(BF16)
    gd[0:length, 2 * cols : first] = grad_kv[:, cols : 2 * cols].astype(BF16)
    back_norms(slots - 1)
    tick(ticked)
    loop(0, early, lambda p: give_half(p, 0, False))
    tick(ticked + 1)
    loop(0, early, lambda p: keep_half(p, 0, False))
    tick(ticked + 2)
    ticked += 3

    ones = jnp.ones((16, rows_all), BF16)
    sum_own[:, 0:edge] = nn(ones, gd[...])[0:8, :]
    sum_own[:, edge : edge + width] = nn(ones, dyv[...])[0:8, :]

    def sum_copy(step, g):
        if g:
            return remote(
                sum_own, sum_f.at[f], ss.at[0, g - 1], sr.at[0, g - 1], mate_to(g)
            )
        return remote(
            sum_own, sum_c.at[c], ss.at[1, step - 1], sr.at[1, step - 1], ctx_to(step)
        )

    sum_f[f] = sum_own[...]
    for g in range(1, nf):
        sum_copy(0, g).start()

    tick(ticked)
    tick(ticked + 1)
    for g in range(1, nf):
        sum_copy(0, g).wait_recv()
        sum_copy(0, g).wait_send()
    held = sum_f[0]
    for i in range(1, nf):
        held = held + sum_f[i]
    sum_own[...] = held
    sum_c[c] = held
    for step in range(1, nc):
        sum_copy(step, 0).start()
    loop(ticked + 2, ticked + 8, tick)
    ticked += 8
    for step in range(1, nc):
        sum_copy(step, 0).wait_recv()
        sum_copy(step, 0).wait_send()
    held = sum_c[0]
    for i in range(1, nc):
        held = held + sum_c[i]
    sums_out[...] = held

    lane = lax.broadcasted_iota(jnp.int32, (own, 128), 1)
    norm_own[...] = jnp.zeros_like(norm_own)

    columns = small_t[...] if turned_in else small[...].T

    def stored(p, out, base, across):
        slot = lax.rem(p, 2)
        at = pl.ds(pl.multiple_of((p - base) * part, part), part)
        if across:
            return pltpu.make_async_copy(stage.at[slot], out.at[:, at], os.at[slot])
        return pltpu.make_async_copy(stage_t.at[slot], out.at[at], os.at[slot])

    def stage_done(p):
        slot = lax.rem(p, 2)
        pltpu.make_async_copy(stage.at[slot], du_out.at[:, pl.ds(0, part)], os.at[slot]).wait()

    def q_stored(p):
        per = cols // part
        slot = lax.rem(p, 2)
        at = pl.ds(pl.multiple_of(lax.rem(p, per) * part, part), part)
        return pltpu.make_async_copy(stage.at[slot], dq_out.at[lax.div(p, per), :, at], os.at[slot])

    def settle(p, copy_of, group_at):
        rows = pl.ds(pl.multiple_of(c * own, own), own)
        lanes = pl.ds(pl.multiple_of(p * part, part), part)
        kept = half_recv[0, p, rows, :].astype(F32)
        for step in range(1, nc):
            piece_copy(p, step).wait_recv()
            kept = kept + piece_recv[step - 1, p].astype(F32)

        @pl.when((p != early) & (p != early + 1))
        def _():
            stage_done(p)

        if group_at is None:
            if turned_in:
                stage[lax.rem(p, 2)] = kept
            else:
                stage_t[lax.rem(p, 2)] = kept.T
        else:
            weights = wall[own_rows, lanes].astype(F32)
            column = sums_out[0:1, lanes]
            moment = jnp.sum(kept * weights, axis=1, keepdims=True)
            against = jnp.sum(weights * column, axis=1, keepdims=True)
            norm_own[...] += jnp.where(
                lane == 2 * group_at, moment, jnp.where(lane == 2 * group_at + 1, against, 0.0)
            )
            at = 2 + 2 * group_at
            gain, shift = columns[:, at : at + 1], columns[:, at + 1 : at + 2]
            stage[lax.rem(p, 2)] = kept * gain + shift * column
        copy_of(p).start()

    dense_end = pieces_one + cols // part
    orders = (
        (early, pieces_one, lambda q: stored(q, du_out, early, True), 1),
        (pieces_one, dense_end, lambda q: stored(q, dd_out, pieces_one, turned_in), None),
        (dense_end, split, lambda q: stored(q, do_out, dense_end, turned_in), None),
        (0, early, q_stored, 0),
    )
    settled = ticked - early // 3
    for low, high, copy_of, group_at in orders:
        start = settled if low else settled + split // 3
        loop(
            low,
            high,
            with_tick(functools.partial(settle, copy_of=copy_of, group_at=group_at), start),
        )
    ticked += split // 3
    norm_in[t] = norm_own[...]

    def norm_copy(k):
        return remote(norm_own, norm_in.at[t], ns.at[k - 1], nr.at[k - 1], tp_to(k))

    for k in range(1, nt_axis):
        norm_copy(k).start()

    for p in range(5):
        gather_sent(p)
    for step in range(1, nc):
        small_copy(step, 0).wait_send()
        back_kv_copy(step).wait_send()
    for step in range(nc):
        for g in range(1, nf):
            small_copy(step, g).wait_send()

    def sent(p):
        for g in range(1, nf):
            half_copy(p, g).wait_send()
        for step in range(1, nc):
            piece_copy(p, step).wait_send()

    loop(0, split, sent)

    def finish_line(q):
        step_line(q)

        @pl.when(at_end)
        def _():
            line_back(q - LAG)

        line_done(q - BEHIND - LAG)

    @pl.when(at_end)
    def _():
        loop(0, ticked * PACE - LAG, line_back)

    loop(0, ticked * PACE - BEHIND - LAG, line_done)
    loop(ticked * PACE, 2 * chunks + LAG, finish_line)

    for k in range(1, nt_axis):
        norm_copy(k).wait_recv()
        norm_copy(k).wait_send()
    held = norm_in[0]
    for i in range(1, nt_axis):
        held = held + norm_in[i]
    norms_out[...] = held if turned_in else held.T[0:8, :]

    loop(2 * chunks - BEHIND, 2 * chunks, line_done)
    stage_done(split - 2)
    stage_done(split - 1)


def run_layer(sizes, *operands):
    nf, nc, tp = sizes["nf"], sizes["nc"], sizes["tp"]
    own, cols, ff, width = sizes["own"], sizes["cols"], sizes["ff"], sizes["width"]
    length, slots, total = sizes["length"], sizes["slots"], sizes["total"]
    part, split = sizes["part"], sizes["pieces_one"] + sizes["pieces_two"]
    rows = slots * length
    prompt = nc * length
    stacked = cols // HD * length
    edge = 3 * cols + ff
    chunks = rows // CHUNK
    sums = edge + width
    anywhere = pl.BlockSpec(memory_space=pl.ANY)
    vmem = pl.BlockSpec(memory_space=pltpu.VMEM)
    smem = pl.BlockSpec(memory_space=pltpu.SMEM)
    dma = pltpu.SemaphoreType.DMA
    shapes = (
        jax.ShapeDtypeStruct((2, rows, width), BF16),
        jax.ShapeDtypeStruct((3, own, cols), F32),
        jax.ShapeDtypeStruct((own, cols) if sizes["turned"] else (cols, own), F32),
        jax.ShapeDtypeStruct((own, ff), F32),
        jax.ShapeDtypeStruct((own, ff) if sizes["turned"] else (ff, own), F32),
        jax.ShapeDtypeStruct((8, sums), F32),
        jax.ShapeDtypeStruct((own, 128) if sizes["turned"] else (8, own), F32),
        jax.ShapeDtypeStruct((8, width), F32),
    )
    half = nf - 1
    keys = prompt + length
    scratch = [
        pltpu.VMEM((rows, width), BF16),
        pltpu.VMEM((rows, width), BF16),
        pltpu.VMEM((width, rows), BF16),
        pltpu.VMEM((width, total), BF16),
        pltpu.VMEM((rows, 2), F32),
        pltpu.VMEM((rows, 128), F32),
        pltpu.VMEM((rows, 128), F32),
        pltpu.VMEM((8, own), F32),
        pltpu.VMEM((nf * nc, 8, own), F32),
        pltpu.VMEM((1, ff), F32),
        pltpu.VMEM((keys, 2 * cols), BF16),
        pltpu.VMEM((cols, keys), BF16),
        pltpu.VMEM((cols, keys), BF16),
        pltpu.VMEM((cols, stacked), BF16),
        pltpu.VMEM((cols, stacked), BF16),
        pltpu.VMEM((cols, length), F32),
        pltpu.VMEM((cols, length), F32),
        pltpu.VMEM((2, max(keys, width), max(stacked, rows)), BF16),
        pltpu.VMEM((keys, length), F32),
        pltpu.VMEM((keys, length), F32),
        pltpu.VMEM((8, length), F32),
        pltpu.VMEM((rows, cols + ff), BF16),
        pltpu.VMEM((rows, edge), BF16),
        pltpu.VMEM((prompt, 2 * cols), F32),
        pltpu.VMEM((nc - 1, length, 2 * cols), BF16),
    ]
    scratch += [pltpu.VMEM((2, rows, width), BF16)] * 3
    scratch += [
        pltpu.VMEM((half, split, nc * own, part), BF16),
        pltpu.VMEM((half, split, nc * own, part), BF16),
        pltpu.VMEM((nc - 1, split, own, part), BF16),
        pltpu.VMEM((2, own, part), F32),
        pltpu.VMEM((2, part, own), F32),
        pltpu.VMEM((8, sums), F32),
        pltpu.VMEM((nf, 8, sums), F32),
        pltpu.VMEM((nc, 8, sums), F32),
        pltpu.VMEM((own, 128), F32),
        pltpu.VMEM((tp, own, 128), F32),
        dma((10,)),
        dma((2, nc, nf)),
        dma((5, 6)),
        dma((5, 6)),
        dma((5, nc, half)),
        dma((5, nc, half)),
        dma((6,)),
        dma((6,)),
        dma((nc - 1,)),
        dma((nc - 1,)),
        dma((2 * chunks,)),
        dma((2 * chunks,)),
        dma((2 * chunks,)),
        dma((2 * chunks,)),
        dma((2 * chunks,)),
        dma((half, split)),
        dma((half, split)),
        dma((nc - 1, split)),
        dma((nc - 1, split)),
        dma((2, max(half, nc - 1))),
        dma((2, max(half, nc - 1))),
        dma((tp - 1,)),
        dma((tp - 1,)),
        dma((2,)),
    ]
    return pl.pallas_call(
        functools.partial(layer_kernel, sizes),
        out_shape=shapes,
        in_specs=[smem, vmem] + [anywhere] * 8 + [vmem] * (len(operands) - 10),
        out_specs=(anywhere,) * 5 + (vmem,) * 3,
        scratch_shapes=scratch,
        compiler_params=pltpu.CompilerParams(
            collective_id=0, has_side_effects=True, vmem_limit_bytes=MEMORY
        ),
        name="layer",
    )(*operands)


def close_kernel(sizes, *refs):
    nc, own, cols, ff = sizes["nc"], sizes["own"], sizes["cols"], sizes["ff"]
    length, rows_all = sizes["length"], sizes["slots"] * sizes["length"]
    first, turned = 3 * cols, sizes["turned"]
    edge = first + ff
    refs = list(refs)

    def take(count):
        taken = refs[:count]
        del refs[:count]
        return taken

    x_prompt, x_cont, dy_prompt, dy_cont, totals, shifts, sums, norms = take(8)
    given = take(4)
    y_prompt, y_cont, dx_prompt, dx_cont, b_qkv, b_u = take(6)
    singles = take(0 if turned else 6)
    taken = take(4)
    x_v, dy_v, tot_v, y_v, dx_v = take(5)
    held = take(4)
    in_sem, out_sem, held_sem = refs

    def at_rows(start, prompt, cont):
        if start < length:
            return prompt.at[pl.ds(start, BLOCK)]
        return cont.at[pl.ds(start - length, BLOCK)]

    loads, stores = [], []
    for i, start in enumerate(range(0, rows_all, BLOCK)):
        rows = pl.ds(start, BLOCK)
        pairs = (
            (at_rows(start, x_prompt, x_cont), x_v.at[rows]),
            (totals.at[1, rows], tot_v.at[1, rows]),
            (totals.at[0, rows], tot_v.at[0, rows]),
            (at_rows(start, dy_prompt, dy_cont), dy_v.at[rows]),
        )
        loads.append(
            [pltpu.make_async_copy(a, b, in_sem.at[i, k]) for k, (a, b) in enumerate(pairs)]
        )
        pairs = (
            (y_v.at[rows], at_rows(start, y_prompt, y_cont)),
            (dx_v.at[rows], at_rows(start, dx_prompt, dx_cont)),
        )
        stores.append(
            [pltpu.make_async_copy(a, b, out_sem.at[i, k]) for k, (a, b) in enumerate(pairs)]
        )
    brought = [pltpu.make_async_copy(a, b, held_sem.at[0, i]) for i, (a, b) in enumerate(zip(given, held))]
    handed = [pltpu.make_async_copy(a, b, held_sem.at[1, i]) for i, (a, b) in enumerate(zip(held, taken))]
    for copies in loads[:2] + [brought] + loads[2:]:
        for copy in copies:
            copy.start()

    for i in range(3):
        b_qkv[i : i + 1, :] = sums[0:1, i * cols : (i + 1) * cols]
    b_u[...] = sums[0:1, first:edge]
    if not turned:
        for i in range(4):
            singles[i][...] = norms[i : i + 1, :]
        shard = lax.axis_index("fsdp") * nc + lax.axis_index("ctx")
        lanes = pl.ds(pl.multiple_of(edge + shard * own, own), own)
        singles[4][...] = sums[0:1, lanes]
        singles[5][...] = sums[0:1, lanes]

    shift = shifts[0:1, :] + shifts[1:2, :]
    for i, start in enumerate(range(0, rows_all, BLOCK)):
        rows = slice(start, start + BLOCK)
        for copy in loads[i]:
            copy.wait()
        x = x_v[rows, :].astype(F32)
        u = tot_v[1, rows, :].astype(F32)
        centered = x - jnp.mean(x, axis=1, keepdims=True)
        scale = lax.rsqrt(jnp.mean(centered * centered, axis=1, keepdims=True) + EPS)
        unit = centered * scale
        along = jnp.mean(u * unit, axis=1, keepdims=True)
        u = u - jnp.mean(u, axis=1, keepdims=True) - unit * along
        y_v[rows, :] = x + tot_v[0, rows, :].astype(F32) + shift
        stores[i][0].start()
        dx_v[rows, :] = dy_v[rows, :].astype(F32) + scale * u
        stores[i][1].start()
        if i == 2:
            for back, on in zip(brought, handed):
                back.wait()
                on.start()
    for copies in stores + [handed]:
        for copy in copies:
            copy.wait()


def close_layer(sizes, *operands):
    own, ff, width, cols = sizes["own"], sizes["ff"], sizes["width"], sizes["cols"]
    length, rows = sizes["length"], sizes["slots"] * sizes["length"]
    blocks = rows // BLOCK

    def array(shape):
        return jax.ShapeDtypeStruct(shape, F32)

    kept = [(3, cols), (1, ff)] + ([] if sizes["turned"] else [(1, own)] * 6)
    given = [tuple(o.shape) for o in operands[8:]]
    anywhere = pl.BlockSpec(memory_space=pl.ANY)
    vmem = pl.BlockSpec(memory_space=pltpu.VMEM)
    large = [(length, width), (rows - length, width)] * 2
    return pl.pallas_call(
        functools.partial(close_kernel, sizes),
        in_specs=[anywhere] * 5 + [vmem] * 3 + [anywhere] * 4,
        out_specs=[anywhere] * 4 + [vmem] * len(kept) + [anywhere] * 4,
        out_shape=[array(shape) for shape in large + kept + given],
        scratch_shapes=[
            pltpu.VMEM((rows, width), BF16),
            pltpu.VMEM((rows, width), BF16),
            pltpu.VMEM((2, rows, width), BF16),
            pltpu.VMEM((rows, width), F32),
            pltpu.VMEM((rows, width), F32),
        ]
        + [pltpu.VMEM(shape, F32) for shape in given]
        + [
            pltpu.SemaphoreType.DMA((blocks, 4)),
            pltpu.SemaphoreType.DMA((blocks, 2)),
            pltpu.SemaphoreType.DMA((2, 4)),
        ],
        compiler_params=pltpu.CompilerParams(vmem_limit_bytes=62 * 1024 * 1024),
        name="close",
    )(*operands)


def on_device(
    x_prompt,
    x_cont,
    cont_start,
    w_qkv,
    qkv_bias,
    w_dense,
    dense_bias,
    w_fc1,
    fc1_bias,
    w_fc2,
    fc2_bias,
    ln1_gain,
    ln1_bias,
    ln2_gain,
    ln2_bias,
    dy_prompt,
    dy_cont,
):
    length = x_prompt.shape[1]
    conts, cont_len, width = x_cont.shape[1:]
    own, _, cols = w_qkv.shape
    ff = w_fc1.shape[1]
    nf, nc, tp = (lax.axis_size(name) for name in ("fsdp", "ctx", "tp"))
    edge = 3 * cols + ff
    part = 256 if edge % 256 == 0 and (cols + ff) % 256 == 0 else 128
    sizes = {
        "nf": nf,
        "nc": nc,
        "tp": tp,
        "own": own,
        "cols": cols,
        "ff": ff,
        "width": width,
        "length": length,
        "slots": 1 + conts,
        "total": 4 * cols + 2 * ff,
        "part": part,
        "pieces_one": edge // part,
        "pieces_two": (cols + ff) // part,
        "turned": own % 128 != 0,
    }
    turned = [w_dense.T, w_fc2.T] if sizes["turned"] else [w_dense, w_fc2]
    lane = np.arange(128) % HD
    inverse = 10000.0 ** (-2.0 * (lane % (ROT // 2)) / ROT)
    freq = np.zeros((8, 128), np.float32)
    freq[0] = np.where(lane < ROT, inverse, 0.0)
    freq[1] = np.where(lane < ROT // 2, -1.0, 1.0)
    vectors = [dense_bias, fc2_bias, ln1_gain, ln1_bias, ln2_gain, ln2_bias]
    if sizes["turned"]:
        stacked = jnp.pad(jnp.stack(vectors).astype(F32), ((0, 2), (0, 0)))
        vectors = [stacked, stacked.T]
    totals, d_q, d_d, d_u, d_o, sums, norms, small_full = run_layer(
        sizes,
        cont_start,
        jnp.asarray(freq),
        x_prompt[0],
        x_cont.reshape(conts * cont_len, width),
        dy_prompt[0],
        dy_cont.reshape(conts * cont_len, width),
        w_qkv.transpose(1, 0, 2),
        turned[0],
        w_fc1,
        turned[1],
        *vectors,
        qkv_bias,
        fc1_bias,
    )
    tokens = conts * cont_len
    closed = close_layer(
        sizes,
        x_prompt[0],
        x_cont.reshape(tokens, width),
        dy_prompt[0],
        dy_cont.reshape(tokens, width),
        totals,
        small_full,
        sums,
        norms,
        d_q,
        d_d,
        d_u,
        d_o,
    )
    y_prompt, y_cont, dx_prompt, dx_cont, b_qkv, b_u = closed[:6]
    d_qkv, d_dense, d_u, d_o = closed[-4:]
    if sizes["turned"]:
        d_dense, d_o = d_dense.T, d_o.T
        four = [norms[:, i] for i in range(4)]
        place = (lax.axis_index("fsdp") * nc + lax.axis_index("ctx")) * own
        shifts = [lax.dynamic_slice_in_dim(sums[0, edge:], place, own)] * 2
    else:
        *four, shift_one, shift_two = (row.reshape(own) for row in closed[6:12])
        shifts = [shift_one, shift_two]
    shape = x_cont.shape
    return (
        y_prompt[None],
        y_cont.reshape(shape),
        dx_prompt[None],
        dx_cont.reshape(shape),
        d_qkv.transpose(1, 0, 2),
        b_qkv,
        d_dense,
        shifts[0],
        d_u,
        b_u.reshape(ff),
        d_o,
        shifts[1],
        four[0],
        four[1],
        four[2],
        four[3],
    )


def solution(mesh):
    both = ("fsdp", "ctx")
    rows = P("fsdp", "ctx", None)
    conts = P("fsdp", "ctx", None, None)
    vector = P(both)
    return jax.shard_map(
        on_device,
        mesh=mesh,
        in_specs=(
            rows,
            conts,
            P("fsdp", "ctx"),
            P(both, None, "tp"),
            P(None, "tp"),
            P("tp", both),
            vector,
            P(both, "tp"),
            P("tp"),
            P("tp", both),
            vector,
            vector,
            vector,
            vector,
            vector,
            rows,
            conts,
        ),
        out_specs=(
            rows,
            conts,
            rows,
            conts,
            P(both, None, "tp"),
            P(None, "tp"),
            P("tp", both),
            vector,
            P(both, "tp"),
            P("tp"),
            P("tp", both),
            vector,
            vector,
            vector,
            vector,
            vector,
        ),
        check_vma=False,
    )
```

```python
import functools

import jax
import jax.numpy as jnp
import numpy as np
from jax import lax
from jax.experimental import pallas as pl
from jax.experimental.pallas import tpu as pltpu
from jax.sharding import PartitionSpec as P

HD = 64
ROT = 16
EPS = 1e-05
MASKED = -1e30
F32 = jnp.float32
BF16 = jnp.bfloat16
MESH = pl.DeviceIdType.MESH
CHUNK = 64
BLOCK = 128
MEMORY = 63 * 1024 * 1024
LAG = 2
PACE = 1
BEHIND = 3
ERF = (0.254829592, -0.284496736, 1.421413741, -1.453152027, 1.061405429)


def nn(left, right):
    return jnp.dot(left, right, preferred_element_type=F32)


def nt(left, right):
    return lax.dot_general(left, right, (((1,), (1,)), ((), ())), preferred_element_type=F32)


def remote(src, dst, send_sem, recv_sem, device):
    return pltpu.make_async_remote_copy(
        src_ref=src,
        dst_ref=dst,
        send_sem=send_sem,
        recv_sem=recv_sem,
        device_id=device,
        device_id_type=MESH,
    )


def turn(values, cos_t, sin_t):
    lane = lax.broadcasted_iota(jnp.int32, cos_t.shape, 1)
    low_half = lax.rem(lane, HD) < ROT // 2
    pieces = []
    for start in range(0, values.shape[1], 128):
        piece = values[:, start : start + 128]
        up = pltpu.roll(piece, 128 - ROT // 2, 1)
        down = pltpu.roll(piece, ROT // 2, 1)
        pieces.append(piece * cos_t + jnp.where(low_half, up, down) * sin_t)
    return jnp.concatenate(pieces, axis=1) if len(pieces) > 1 else pieces[0]


def layer_kernel(sizes, *refs):
    nf, nc, nt_axis = sizes["nf"], sizes["nc"], sizes["tp"]
    own, cols, ff, width = sizes["own"], sizes["cols"], sizes["ff"], sizes["width"]
    length, slots, total = sizes["length"], sizes["slots"], sizes["total"]
    part, pieces_one, pieces_two = sizes["part"], sizes["pieces_one"], sizes["pieces_two"]
    turned_in = sizes["turned"]
    refs = list(refs)

    def take(count):
        taken = refs[:count]
        del refs[:count]
        return taken

    starts, freq, x_prompt, x_cont, dy_prompt, dy_cont, w_q, w_d, w_u, w_o = take(10)
    vectors = take(1 if turned_in else 6)
    small_t = take(1)[0] if turned_in else None
    bias_q, bias_up = take(2)
    tot_out, dq_out, dd_out, du_out, do_out, sums_out, norms_out, small_out = take(8)
    xv, dyv, n_t, wall = take(4)
    stat_s, cos_s, sin_s, small, smallg, bias_u = take(6)
    kvp, k_t, v_t, q_t, g_t, o_t, dq_t, p_all, score_s, slope_s, share_s = take(11)
    oa, gd, acc, kv_recv = take(4)
    part_sum, from_out, from_in, half_send, half_recv, piece_recv, stage, stage_t = take(8)
    sum_own, sum_f, sum_c, norm_own, norm_in = take(5)
    in_sem, small_sem, ws, wr, fs, fr, kvs, kvr, gks, gkr = take(10)
    zs, za, zbs, zb, zo, hs, hr, ps, pr, ss, sr, ns, nr, os = take(14)
    f, c, t = lax.axis_index("fsdp"), lax.axis_index("ctx"), lax.axis_index("tp")
    heads = cols // HD
    rows_all = slots * length
    pair = slots // 2
    prompt = nc * length
    first = 3 * cols
    edge = first + ff
    shard = f * nc + c
    own_rows = pl.ds(pl.multiple_of(shard * own, own), own)

    def ctx_to(step):
        return (f, lax.rem(c + step, nc), t)

    def ctx_from(step):
        return lax.rem(c + nc - step, nc)

    across_x = c + 1 - 2 * lax.rem(c, 2)
    across_y = lax.rem(c + 2, nc)
    corner = lax.rem(across_x + 2, nc)
    peers = (c, across_x, across_y, corner)

    def mate_to(step):
        return (lax.rem(f + step, nf), c, t)

    def mate_from(step):
        return lax.rem(f + nf - step, nf)

    def tp_to(step):
        return (f, c, lax.rem(t + step, nt_axis))

    upper = lax.div(t, nt_axis // 2)
    inward = (f, c, t + 1 - 2 * upper)
    outward = (f, c, lax.rem(t - 1 + 2 * upper + nt_axis, nt_axis))
    at_end = (t == 0) | (t == nt_axis - 1)
    not_end = (t != 0) & (t != nt_axis - 1)
    in_middle = (t == nt_axis // 2 - 1) | (t == nt_axis // 2)
    not_middle = (t != nt_axis // 2 - 1) & (t != nt_axis // 2)

    loads = [
        (x_prompt, xv.at[pl.ds(0, length)]),
        (x_cont, xv.at[pl.ds(length, rows_all - length)]),
        (dy_prompt, dyv.at[pl.ds(0, length)]),
        (dy_cont, dyv.at[pl.ds(length, rows_all - length)]),
        (w_q.at[0], wall.at[own_rows, pl.ds(0, cols)]),
        (w_q.at[1], wall.at[own_rows, pl.ds(cols, cols)]),
        (w_q.at[2], wall.at[own_rows, pl.ds(2 * cols, cols)]),
        (w_u, wall.at[own_rows, pl.ds(first, ff)]),
    ]
    if turned_in:
        loads += [
            (w_d, wall.at[own_rows, pl.ds(edge, cols)]),
            (w_o, wall.at[own_rows, pl.ds(edge + cols, ff)]),
        ]
    else:
        loads += [
            (w_d, p_all.at[1, pl.ds(0, cols), pl.ds(0, own)]),
            (w_o, p_all.at[0, pl.ds(0, ff), pl.ds(0, own)]),
        ]
    loads = [pltpu.make_async_copy(src, dst, in_sem.at[i]) for i, (src, dst) in enumerate(loads)]
    for i in (4, 5, 6, 0, 8):
        loads[i].start()

    barrier = pltpu.get_barrier_semaphore()
    greeted = [ctx_to(k) for k in range(1, nc)]
    greeted += [mate_to(g) for g in range(1, nf)]
    greeted += [tp_to(k) for k in range(1, nt_axis)]
    for device in greeted:
        pl.semaphore_signal(barrier, inc=1, device_id=device, device_id_type=MESH)
    pl.semaphore_wait(barrier, len(greeted))

    spans = (
        (0, first),
        (edge, cols),
        (first, ff // 2),
        (first + ff // 2, ff // 2),
        (edge + cols, ff),
    )

    half_own = own // 2

    def block(owner, side, size):
        base = owner * size
        if side is None:
            return pl.ds(pl.multiple_of(base, size), size)
        return pl.ds(pl.multiple_of(base + side * (size // 2), size // 2), size // 2)

    routes = ((0, 0, 1), (0, 1, 2), (0, 1, 1), (0, 0, 2), (1, 0, 2), (2, 1, 1))
    lands = ((1, 0), (2, 1), (1, 1), (2, 0), (3, 0), (3, 1))

    def ctx_copy(route, source, target, size, send_sem, recv_sem):
        owner, side, to = routes[route]
        rows = block(peers[owner], side, size)
        src = source(owner, side, rows)
        return remote(src, target(rows), send_sem, recv_sem, (f, peers[to], t))

    def lanes_of(p):
        return pl.ds(spans[p][0], spans[p][1])

    def gather_copy(p, route):
        def place(rows):
            return wall.at[pl.ds(rows.start + f * nc * own, half_own), lanes_of(p)]

        return ctx_copy(
            route, lambda owner, side, rows: place(rows), place, own, ws.at[p, route], wr.at[p, route]
        )

    def mate_copy(p, peer, g):
        place = wall.at[block(f * nc + peers[peer], None, own), lanes_of(p)]
        return remote(
            place, place, fs.at[p, peer, g - 1], fr.at[p, peer, g - 1], mate_to(g)
        )

    def gather_start(p):
        for route in range(4):
            gather_copy(p, route).start()
        for g in range(1, nf):
            mate_copy(p, 0, g).start()

    def gather_relay(p):
        for arrived, route in ((0, 4), (1, 5)):
            gather_copy(p, arrived).wait_recv()
            gather_copy(p, route).start()

    def gather_pass(p):
        for peer, rest in ((1, (2,)), (2, (3,)), (3, (4, 5))):
            for route in rest:
                gather_copy(p, route).wait_recv()
            for g in range(1, nf):
                mate_copy(p, peer, g).start()

    def gather_finish(p):
        for peer in range(nc):
            for g in range(1, nf):
                mate_copy(p, peer, g).wait_recv()

    def gather_sent(p):
        for route in range(6):
            gather_copy(p, route).wait_send()
        for peer in range(nc):
            for g in range(1, nf):
                mate_copy(p, peer, g).wait_send()

    def small_copy(step, g):
        if g == 0:
            return remote(
                small, smallg.at[shard], small_sem.at[0, step, 0], small_sem.at[1, step, 0], ctx_to(step)
            )
        held = f * nc + ctx_from(step)
        src = small if step == 0 else smallg.at[held]
        return remote(
            src, smallg.at[held], small_sem.at[0, step, g], small_sem.at[1, step, g], mate_to(g)
        )

    if turned_in:
        small[...] = vectors[0][...]
    else:
        small[...] = jnp.zeros_like(small)
        for i, vector in enumerate(vectors):
            small[i : i + 1, :] = vector[...].astype(F32).reshape(1, own)
    bias_u[...] = bias_up[...].astype(F32).reshape(1, ff)
    for step in range(1, nc):
        small_copy(step, 0).start()
    for g in range(1, nf):
        small_copy(0, g).start()
    for i in (4, 5, 6):
        loads[i].wait()
    gather_start(0)
    for i in (7, 1):
        loads[i].start()
    loads[8].wait()
    if not turned_in:
        wall[own_rows, edge : edge + cols] = p_all[1, 0:cols, 0:own].astype(F32).T.astype(BF16)
    smallg[shard] = small[...]
    loads[7].wait()
    gather_relay(0)
    gather_start(1)
    gather_start(2)
    for i in (9, 2, 3):
        loads[i].start()

    loads[0].wait()
    loads[1].wait()

    def statistics(slot):
        rows = pl.ds(pl.multiple_of(slot * length, length), length)
        block_x = xv[rows, :].astype(F32)
        mean = jnp.mean(block_x, axis=1, keepdims=True)
        block_x = block_x - mean
        scale = lax.rsqrt(jnp.mean(block_x * block_x, axis=1, keepdims=True) + EPS)
        stat_s[rows, 0:1] = mean
        stat_s[rows, 1:2] = scale
        n_t[:, rows] = (block_x * scale).T.astype(BF16)
        before = starts[0, jnp.maximum(slot - 1, 0)]
        base = jnp.where(slot == 0, c * length, before)
        place = base + lax.broadcasted_iota(jnp.int32, (length, 128), 0)
        phase = place.astype(F32) * freq[0:1, :]
        cos_s[rows, :] = jnp.cos(phase)
        sin_s[rows, :] = jnp.sin(phase) * freq[1:2, :]

    def loop(low, high, body):
        lax.fori_loop(low, high, lambda i, carry: (body(i), carry)[1], 0)

    statistics(0)
    for step in range(1, nc):
        small_copy(step, 0).wait_recv()
        for g in range(1, nf):
            small_copy(step, g).start()
    gather_relay(1)
    statistics(1)
    gather_relay(2)
    gather_pass(0)
    loop(2, slots - 1, statistics)
    for step in range(nc):
        for g in range(1, nf):
            small_copy(step, g).wait_recv()
    parts = [smallg[i] for i in range(nf * nc)]
    small_out[...] = jnp.concatenate(parts, axis=1)
    gain_one, shift_one = small_out[2:3, :], small_out[3:4, :]
    gain_two, shift_two = small_out[4:5, :], small_out[5:6, :]

    def normed(rows, gain, shift):
        block = (xv[rows, :].astype(F32) - stat_s[rows, 0:1]) * stat_s[rows, 1:2]
        return (block * gain + shift).astype(BF16)

    gather_finish(0)

    def project(slot):
        rows = pl.ds(pl.multiple_of(slot * length, length), length)
        both = nn(normed(rows, gain_one, shift_one), wall[:, 0:first])
        cos_t, sin_t = cos_s[rows, :], sin_s[rows, :]
        query = both[:, 0:cols] + bias_q[0:1, :].astype(F32)
        key = both[:, cols : 2 * cols] + bias_q[1:2, :].astype(F32)
        value = both[:, 2 * cols : first] + bias_q[2:3, :].astype(F32)
        gd[rows, 0:cols] = (turn(query, cos_t, sin_t) * 0.125).astype(BF16)
        gd[rows, cols : 2 * cols] = turn(key, cos_t, sin_t).astype(BF16)
        gd[rows, 2 * cols : first] = value.astype(BF16)

    project(0)
    mine = pl.ds(pl.multiple_of(c * length, length), length)
    kvp[mine, :] = gd[0:length, cols:first]

    def kv_copy(route):
        def source(owner, side, rows):
            if owner == 0:
                return gd.at[pl.ds(side * (length // 2), length // 2), pl.ds(cols, 2 * cols)]
            return kvp.at[rows]

        return ctx_copy(
            route, source, lambda rows: kvp.at[rows], length, kvs.at[route], kvr.at[route]
        )

    for route in range(4):
        kv_copy(route).start()
    gather_pass(1)
    loads[9].wait()
    if not turned_in:
        wall[own_rows, edge + cols : total] = p_all[0, 0:ff, 0:own].astype(F32).T.astype(BF16)
    statistics(slots - 1)
    for arrived, route in ((0, 4), (1, 5)):
        kv_copy(arrived).wait_recv()
        kv_copy(route).start()
    gather_start(3)
    gather_start(4)
    loop(1, slots, project)
    gather_relay(3)
    gather_finish(1)
    gather_pass(2)
    loads[2].wait()
    loads[3].wait()

    def back_dense(slot):
        rows = pl.ds(pl.multiple_of(slot * length, length), length)
        block_dy = dyv[rows, :]
        oa[rows, 0:cols] = nn(block_dy, wall[:, edge : edge + cols]).astype(BF16)

    loop(0, slots, back_dense)

    for route in range(2, 6):
        kv_copy(route).wait_recv()
    k_t[:, 0:prompt] = kvp[0:prompt, 0:cols].astype(F32).T.astype(BF16)
    v_t[:, 0:prompt] = kvp[0:prompt, cols : 2 * cols].astype(F32).T.astype(BF16)

    def fold(block_of, combine):
        return combine(block_of.reshape(-1, 8, block_of.shape[1]), axis=0)

    def attend(slot, is_prompt, between=()):
        rows = pl.ds(pl.multiple_of(slot * length, length), length)
        span = prompt if is_prompt else prompt + length
        stacked = heads * length
        head_row = lax.div(lax.broadcasted_iota(jnp.int32, (cols, length), 0), HD)
        query = gd[rows, 0:cols].astype(F32).T.astype(BF16)
        grad = oa[rows, 0:cols].astype(F32).T.astype(BF16)
        zero = jnp.zeros_like(query)
        for h in range(heads):
            q_t[:, h * length : (h + 1) * length] = jnp.where(head_row == h, query, zero)
            g_t[:, h * length : (h + 1) * length] = jnp.where(head_row == h, grad, zero)
        key_at = lax.broadcasted_iota(jnp.int32, (length, length), 0)
        query_at = lax.broadcasted_iota(jnp.int32, (length, length), 1)
        if is_prompt:
            limit = query_at + (c * length + 1)
        else:
            kvp[prompt:span, :] = gd[rows, cols:first]
            k_t[:, prompt:span] = gd[rows, cols : 2 * cols].astype(F32).T.astype(BF16)
            v_t[:, prompt:span] = gd[rows, 2 * cols : first].astype(F32).T.astype(BF16)
            limit = starts[0, slot - 1]

        def lanes(h):
            return slice(h * length, (h + 1) * length)

        def lines(h):
            return slice(h * HD, (h + 1) * HD)

        def score(h):
            for b in range(0, span, length):
                keys = slice(b, b + length)
                score_s[keys, :] = nn(kvp[keys, 0:cols], q_t[:, lanes(h)])

        def slope(h):
            for b in range(0, span, length):
                keys = slice(b, b + length)
                slope_s[keys, :] = nn(kvp[keys, cols : 2 * cols], g_t[:, lanes(h)])

        def mask():
            highest = jnp.full((8, length), MASKED, F32)
            for b in range(0, span, length):
                seen = key_at + b < limit if b < prompt else key_at <= query_at
                scores = jnp.where(seen, score_s[b : b + length, :], MASKED)
                score_s[b : b + length, :] = scores
                highest = jnp.maximum(highest, fold(scores, jnp.max))
            return jnp.max(highest, axis=0, keepdims=True)

        def raise_up(h, highest):
            norm = jnp.zeros((8, length), F32)
            for b in range(0, span, length):
                raised = jnp.exp(score_s[b : b + length, :] - highest)
                norm = norm + fold(raised, jnp.sum)
                p_all[0, b : b + length, lanes(h)] = raised.astype(BF16)
            share = 1.0 / jnp.sum(norm, axis=0, keepdims=True)
            share_s[h : h + 1, :] = share
            return share

        score(0)
        slope(0)
        share = raise_up(0, mask())
        for h in range(heads):
            out_t = nn(v_t[lines(h), 0:span], p_all[0, 0:span, lanes(h)]) * share
            o_t[lines(h), :] = out_t
            if h + 1 < heads:
                score(h + 1)
            inner = jnp.sum(out_t * g_t[lines(h), lanes(h)].astype(F32), axis=0, keepdims=True)
            for b in range(0, span, length):
                raised = p_all[0, b : b + length, lanes(h)].astype(F32)
                low = (raised * (slope_s[b : b + length, :] - inner)).astype(BF16)
                p_all[1, b : b + length, lanes(h)] = low
            dq_t[lines(h), :] = nn(k_t[lines(h), 0:span], p_all[1, 0:span, lanes(h)]) * share
            if h + 1 < heads:
                slope(h + 1)
                share = raise_up(h + 1, mask())
            for at, action in between:
                if at == h:
                    action()
        for h in range(heads):
            share = share_s[h : h + 1, :]
            q_t[:, lanes(h)] = (q_t[:, lanes(h)].astype(F32) * share).astype(BF16)
            g_t[:, lanes(h)] = (g_t[:, lanes(h)].astype(F32) * share).astype(BF16)
        cos_t, sin_t = cos_s[rows, :], -sin_s[rows, :]
        oa[rows, 0:cols] = o_t[...].T.astype(BF16)
        gd[rows, 0:cols] = turn(dq_t[...].T * 0.125, cos_t, sin_t).astype(BF16)
        acc[:, 0:cols] += nt(p_all[1, 0:prompt, 0:stacked], q_t[...])
        acc[:, cols : 2 * cols] += nt(p_all[0, 0:prompt, 0:stacked], g_t[...])
        if not is_prompt:
            back_k = nt(p_all[1, prompt:span, 0:stacked], q_t[...])
            gd[rows, cols : 2 * cols] = turn(back_k, cos_t, sin_t).astype(BF16)
            gd[rows, 2 * cols : first] = nt(p_all[0, prompt:span, 0:stacked], g_t[...]).astype(BF16)

    def kv_send(step):
        return p_all.at[1, pl.ds((step - 1) * length, length), pl.ds(0, 2 * cols)]

    def back_kv_copy(step):
        return remote(
            kv_send(step), kv_recv.at[step - 1], gks.at[step - 1], gkr.at[step - 1], ctx_to(step)
        )

    chunks = rows_all // CHUNK
    per_slot = length // CHUNK

    def line(q):
        which, place = lax.div(q, chunks), lax.rem(q, chunks)
        slot = lax.rem(lax.div(place, per_slot) + 1, slots)
        inner = lax.rem(place, per_slot)
        return which, pl.ds(pl.multiple_of((slot * per_slot + inner) * CHUNK, CHUNK), CHUNK)

    def line_out(q, middle):
        which, rows = line(q)
        target = from_in if middle else from_out
        landed = zb if middle else za
        return remote(
            part_sum.at[which, rows], target.at[which, rows], zs.at[q], landed.at[q], inward
        )

    def line_home(q, middle):
        which, rows = line(q)
        src = from_out if middle else from_in
        return remote(
            src.at[which, rows], from_in.at[which, rows], zbs.at[q], zb.at[q], outward
        )

    def line_store(q):
        which, rows = line(q)
        return pltpu.make_async_copy(part_sum.at[which, rows], tot_out.at[which, rows], zo.at[q])

    def line_close(q, total_ref):
        which, rows = line(q)
        line_out(q, True).wait_send()
        got = total_ref[which, rows, :].astype(F32)

        @pl.when(which == 0)
        def _():
            whole = xv[rows, :].astype(F32) + got + (small_out[0:1, :] + small_out[1:2, :])
            part_sum[0, rows, :] = whole.astype(BF16)

        @pl.when(which == 1)
        def _():
            scale = stat_s[rows, 1:2]
            unit = (xv[rows, :].astype(F32) - stat_s[rows, 0:1]) * scale
            along = jnp.mean(got * unit, axis=1, keepdims=True)
            rest = got - jnp.mean(got, axis=1, keepdims=True) - unit * along
            part_sum[1, rows, :] = (dyv[rows, :].astype(F32) + scale * rest).astype(BF16)

        line_store(q).start()

    def line_send(q):
        @pl.when(in_middle)
        def _():
            line_out(q, True).start()

        @pl.when(not_middle)
        def _():
            line_out(q, False).start()

    def line_first(q):
        @pl.when(at_end)
        def _():
            line_send(q)

    def line_add(q):
        which, rows = line(q)

        @pl.when(not_end)
        def _():
            line_out(q, False).wait_recv()
            part_sum[which, rows, :] = (
                part_sum[which, rows, :].astype(F32) + from_out[which, rows, :].astype(F32)
            ).astype(BF16)
            line_send(q)

    def line_back(q):
        which, rows = line(q)

        @pl.when(in_middle)
        def _():
            line_out(q, True).wait_recv()
            from_out[which, rows, :] = (
                part_sum[which, rows, :].astype(F32) + from_in[which, rows, :].astype(F32)
            ).astype(BF16)

            @pl.when(not_end)
            def _():
                line_home(q, True).start()

            line_close(q, from_out)

        @pl.when(not_middle)
        def _():
            line_home(q, False).wait_recv()

            @pl.when(not_end)
            def _():
                line_home(q, False).start()

            line_close(q, from_in)

    def line_done(q):
        line_store(q).wait()

        @pl.when(not_end)
        def _():
            line_home(q, True).wait_send()

    def step_line(q):
        @pl.when(q < 2 * chunks)
        def _():
            line_add(q)

        @pl.when((q >= LAG) & not_end)
        def _():
            line_back(q - LAG)

    def tick(k):
        for i in range(PACE):
            step_line(k * PACE + i)

    def feed(position, halfway=None):
        slot = lax.rem(position + 1, slots)
        rows = pl.ds(pl.multiple_of(slot * length, length), length)
        inputs = normed(rows, gain_two, shift_two)
        for at in range(0, ff, ff // 2):
            units = slice(at, at + ff // 2)
            up = slice(first + at, first + at + ff // 2)
            hidden = nn(inputs, wall[:, up]) + bias_u[:, units]
            depth = jnp.abs(hidden) * np.float32(0.5**0.5)
            step = 1.0 / (1.0 + np.float32(0.3275911) * depth)
            poly = np.float32(ERF[4])
            for factor in ERF[3::-1]:
                poly = poly * step + np.float32(factor)
            bell = jnp.exp(-(depth * depth))
            tail = 0.5 * (poly * step) * bell
            below = jnp.where(hidden >= 0.0, 1.0 - tail, tail)
            oa[rows, cols + at : cols + at + ff // 2] = (hidden * below).astype(BF16)
            slope = below + hidden * (bell * np.float32((2.0 * np.pi) ** -0.5))
            for b in range(0, ff // 2, length):
                lines = slice(at + b, at + b + length)
                score_s[lines, :] = slope[:, b : b + length]
        part_sum[0, rows, :] = nt(oa[rows, :], wall[:, edge:total]).astype(BF16)
        for i in range(per_slot):
            line_first(position * per_slot + i)
        if halfway is not None:
            halfway()
        for at in range(0, ff, length):
            down = slice(edge + cols + at, edge + cols + at + length)
            back = nn(dyv[rows, :], wall[:, down])
            gd[rows, first + at : first + at + length] = (
                back * score_s[at : at + length, :]
            ).astype(BF16)

    def back_norms(position):
        slot = lax.rem(position + 1, slots)
        rows = pl.ds(pl.multiple_of(slot * length, length), length)
        toward_x = nt(gd[rows, 0:first], wall[:, 0:first]) * gain_one
        toward_x = toward_x + nt(gd[rows, first:edge], wall[:, first:edge]) * gain_two
        part_sum[1, rows, :] = toward_x.astype(BF16)
        for i in range(per_slot):
            line_first(chunks + position * per_slot + i)

    acc[...] = jnp.zeros_like(acc)

    def at_slot(slot, wanted, *steps):
        def action():
            @pl.when(slot == wanted)
            def _():
                for step in steps:
                    step()

        return action

    def attend_cont(slot):
        attend(
            slot,
            False,
            (
                (heads // 2, at_slot(slot, 1, lambda: gather_relay(4))),
                (heads // 2, at_slot(slot, pair, lambda: gather_pass(3))),
            ),
        )

    loop(1, pair + 1, attend_cont)
    gather_pass(4)
    for p in (2, 3, 4):
        gather_finish(p)
    loop(0, pair, feed)
    for slot in range(pair + 1, slots):
        attend(slot, False, ((1, lambda: tick(0)), (heads - 1, lambda: tick(1))))
        feed(slot - 1, lambda: tick(2))
    attend(0, True, ((0, lambda: tick(3)), (heads // 2, lambda: tick(4))))
    for step in range(1, nc):
        there = pl.ds(pl.multiple_of(lax.rem(c + step, nc) * length, length), length)
        kv_send(step)[...] = acc[there, :].astype(BF16)
        back_kv_copy(step).start()
    feed(slots - 1, lambda: tick(5))
    tick(6)
    loop(0, pair, back_norms)
    tick(7)
    loop(pair, slots - 1, back_norms)
    tick(8)

    def turn_dy(slot):
        rows = pl.ds(pl.multiple_of(slot * length, length), length)
        p_all[0, 0:width, rows] = dyv[rows, :].astype(F32).T.astype(BF16)

    loop(0, slots, turn_dy)
    tick(9)

    group = nc * own
    split = pieces_one + pieces_two

    def product(p, rows, second):
        lanes = pl.ds(pl.multiple_of(p * part, part), part)
        if second:
            return nn(p_all[0, rows, 0:rows_all], oa[:, lanes])
        return nn(n_t[rows, :], gd[:, lanes])

    def half_copy(p, g):
        return remote(
            half_send.at[g - 1, p], half_recv.at[g - 1, p], hs.at[g - 1, p], hr.at[g - 1, p], mate_to(g)
        )

    def piece_copy(p, step):
        rows = pl.ds(pl.multiple_of(lax.rem(c + step, nc) * own, own), own)
        return remote(
            half_recv.at[0, p, rows],
            piece_recv.at[step - 1, p],
            ps.at[step - 1, p],
            pr.at[step - 1, p],
            ctx_to(step),
        )

    def give_half(p, base, second):
        for g in range(1, nf):
            rows = pl.ds(pl.multiple_of(lax.rem(f + g, nf) * group, group), group)
            half_send[g - 1, p] = product(p - base, rows, second).astype(BF16)
            half_copy(p, g).start()

    def keep_half(p, base, second):
        rows = pl.ds(pl.multiple_of(f * group, group), group)
        kept = product(p - base, rows, second)
        for g in range(1, nf):
            half_copy(p, g).wait_recv()
            kept = kept + half_recv[g - 1, p].astype(F32)
        half_recv[0, p] = kept.astype(BF16)
        for step in range(1, nc):
            piece_copy(p, step).start()

    early = first // part

    def with_tick(body, start, lowest=0):
        def step(p):
            body(p)

            @pl.when((lax.rem(p, 3) == 2) & (p >= lowest))
            def _():
                tick(start + lax.div(p, 3))

        return step

    give_start, keep_start, lowest = 8, 10, 2 * early
    for start, body in ((give_start, give_half), (keep_start, keep_half)):
        one = with_tick(lambda p, body=body: body(p, 0, False), start, lowest)
        two = with_tick(lambda p, body=body: body(p, pieces_one, True), start, lowest)
        loop(early, pieces_one, one)
        loop(pieces_one, split, two)
    ticked = keep_start + split // 3

    for route in range(6):
        kv_copy(route).wait_send()
    grad_kv = acc[mine, :]
    for step in range(1, nc):
        back_kv_copy(step).wait_recv()
        grad_kv = grad_kv + kv_recv[step - 1].astype(F32)
    gd[0:length, cols : 2 * cols] = turn(
        grad_kv[:, 0:cols], cos_s[0:length, :], -sin_s[0:length, :]
    ).astype(BF16)
    gd[0:length, 2 * cols : first] = grad_kv[:, cols : 2 * cols].astype(BF16)
    back_norms(slots - 1)
    tick(ticked)
    loop(0, early, lambda p: give_half(p, 0, False))
    tick(ticked + 1)
    loop(0, early, lambda p: keep_half(p, 0, False))
    tick(ticked + 2)
    ticked += 3

    ones = jnp.ones((16, rows_all), BF16)
    sum_own[:, 0:edge] = nn(ones, gd[...])[0:8, :]
    sum_own[:, edge : edge + width] = nn(ones, dyv[...])[0:8, :]

    def sum_copy(step, g):
        if g:
            return remote(
                sum_own, sum_f.at[f], ss.at[0, g - 1], sr.at[0, g - 1], mate_to(g)
            )
        return remote(
            sum_own, sum_c.at[c], ss.at[1, step - 1], sr.at[1, step - 1], ctx_to(step)
        )

    sum_f[f] = sum_own[...]
    for g in range(1, nf):
        sum_copy(0, g).start()

    tick(ticked)
    tick(ticked + 1)
    for g in range(1, nf):
        sum_copy(0, g).wait_recv()
        sum_copy(0, g).wait_send()
    held = sum_f[0]
    for i in range(1, nf):
        held = held + sum_f[i]
    sum_own[...] = held
    sum_c[c] = held
    for step in range(1, nc):
        sum_copy(step, 0).start()
    loop(ticked + 2, ticked + 8, tick)
    ticked += 8
    for step in range(1, nc):
        sum_copy(step, 0).wait_recv()
        sum_copy(step, 0).wait_send()
    held = sum_c[0]
    for i in range(1, nc):
        held = held + sum_c[i]
    sums_out[...] = held

    lane = lax.broadcasted_iota(jnp.int32, (own, 128), 1)
    norm_own[...] = jnp.zeros_like(norm_own)

    columns = small_t[...] if turned_in else small[...].T

    def stored(p, out, base, across):
        slot = lax.rem(p, 2)
        at = pl.ds(pl.multiple_of((p - base) * part, part), part)
        if across:
            return pltpu.make_async_copy(stage.at[slot], out.at[:, at], os.at[slot])
        return pltpu.make_async_copy(stage_t.at[slot], out.at[at], os.at[slot])

    def stage_done(p):
        slot = lax.rem(p, 2)
        pltpu.make_async_copy(stage.at[slot], du_out.at[:, pl.ds(0, part)], os.at[slot]).wait()

    def q_stored(p):
        per = cols // part
        slot = lax.rem(p, 2)
        at = pl.ds(pl.multiple_of(lax.rem(p, per) * part, part), part)
        return pltpu.make_async_copy(stage.at[slot], dq_out.at[lax.div(p, per), :, at], os.at[slot])

    def settle(p, copy_of, group_at):
        rows = pl.ds(pl.multiple_of(c * own, own), own)
        lanes = pl.ds(pl.multiple_of(p * part, part), part)
        kept = half_recv[0, p, rows, :].astype(F32)
        for step in range(1, nc):
            piece_copy(p, step).wait_recv()
            kept = kept + piece_recv[step - 1, p].astype(F32)

        @pl.when((p != early) & (p != early + 1))
        def _():
            stage_done(p)

        if group_at is None:
            if turned_in:
                stage[lax.rem(p, 2)] = kept
            else:
                stage_t[lax.rem(p, 2)] = kept.T
        else:
            weights = wall[own_rows, lanes].astype(F32)
            column = sums_out[0:1, lanes]
            moment = jnp.sum(kept * weights, axis=1, keepdims=True)
            against = jnp.sum(weights * column, axis=1, keepdims=True)
            norm_own[...] += jnp.where(
                lane == 2 * group_at, moment, jnp.where(lane == 2 * group_at + 1, against, 0.0)
            )
            at = 2 + 2 * group_at
            gain, shift = columns[:, at : at + 1], columns[:, at + 1 : at + 2]
            stage[lax.rem(p, 2)] = kept * gain + shift * column
        copy_of(p).start()

    dense_end = pieces_one + cols // part
    orders = (
        (early, pieces_one, lambda q: stored(q, du_out, early, True), 1),
        (pieces_one, dense_end, lambda q: stored(q, dd_out, pieces_one, turned_in), None),
        (dense_end, split, lambda q: stored(q, do_out, dense_end, turned_in), None),
        (0, early, q_stored, 0),
    )
    settled = ticked - early // 3
    for low, high, copy_of, group_at in orders:
        start = settled if low else settled + split // 3
        loop(
            low,
            high,
            with_tick(functools.partial(settle, copy_of=copy_of, group_at=group_at), start),
        )
    ticked += split // 3
    norm_in[t] = norm_own[...]

    def norm_copy(k):
        return remote(norm_own, norm_in.at[t], ns.at[k - 1], nr.at[k - 1], tp_to(k))

    for k in range(1, nt_axis):
        norm_copy(k).start()

    for p in range(5):
        gather_sent(p)
    for step in range(1, nc):
        small_copy(step, 0).wait_send()
        back_kv_copy(step).wait_send()
    for step in range(nc):
        for g in range(1, nf):
            small_copy(step, g).wait_send()

    def sent(p):
        for g in range(1, nf):
            half_copy(p, g).wait_send()
        for step in range(1, nc):
            piece_copy(p, step).wait_send()

    loop(0, split, sent)

    def finish_line(q):
        step_line(q)

        @pl.when(at_end)
        def _():
            line_back(q - LAG)

        line_done(q - BEHIND - LAG)

    @pl.when(at_end)
    def _():
        loop(0, ticked * PACE - LAG, line_back)

    loop(0, ticked * PACE - BEHIND - LAG, line_done)
    loop(ticked * PACE, 2 * chunks + LAG, finish_line)

    for k in range(1, nt_axis):
        norm_copy(k).wait_recv()
        norm_copy(k).wait_send()
    held = norm_in[0]
    for i in range(1, nt_axis):
        held = held + norm_in[i]
    norms_out[...] = held if turned_in else held.T[0:8, :]

    loop(2 * chunks - BEHIND, 2 * chunks, line_done)
    stage_done(split - 2)
    stage_done(split - 1)


def run_layer(sizes, *operands):
    nf, nc, tp = sizes["nf"], sizes["nc"], sizes["tp"]
    own, cols, ff, width = sizes["own"], sizes["cols"], sizes["ff"], sizes["width"]
    length, slots, total = sizes["length"], sizes["slots"], sizes["total"]
    part, split = sizes["part"], sizes["pieces_one"] + sizes["pieces_two"]
    rows = slots * length
    prompt = nc * length
    stacked = cols // HD * length
    edge = 3 * cols + ff
    chunks = rows // CHUNK
    sums = edge + width
    anywhere = pl.BlockSpec(memory_space=pl.ANY)
    vmem = pl.BlockSpec(memory_space=pltpu.VMEM)
    smem = pl.BlockSpec(memory_space=pltpu.SMEM)
    dma = pltpu.SemaphoreType.DMA
    shapes = (
        jax.ShapeDtypeStruct((2, rows, width), BF16),
        jax.ShapeDtypeStruct((3, own, cols), F32),
        jax.ShapeDtypeStruct((own, cols) if sizes["turned"] else (cols, own), F32),
        jax.ShapeDtypeStruct((own, ff), F32),
        jax.ShapeDtypeStruct((own, ff) if sizes["turned"] else (ff, own), F32),
        jax.ShapeDtypeStruct((8, sums), F32),
        jax.ShapeDtypeStruct((own, 128) if sizes["turned"] else (8, own), F32),
        jax.ShapeDtypeStruct((8, width), F32),
    )
    half = nf - 1
    keys = prompt + length
    scratch = [
        pltpu.VMEM((rows, width), BF16),
        pltpu.VMEM((rows, width), BF16),
        pltpu.VMEM((width, rows), BF16),
        pltpu.VMEM((width, total), BF16),
        pltpu.VMEM((rows, 2), F32),
        pltpu.VMEM((rows, 128), F32),
        pltpu.VMEM((rows, 128), F32),
        pltpu.VMEM((8, own), F32),
        pltpu.VMEM((nf * nc, 8, own), F32),
        pltpu.VMEM((1, ff), F32),
        pltpu.VMEM((keys, 2 * cols), BF16),
        pltpu.VMEM((cols, keys), BF16),
        pltpu.VMEM((cols, keys), BF16),
        pltpu.VMEM((cols, stacked), BF16),
        pltpu.VMEM((cols, stacked), BF16),
        pltpu.VMEM((cols, length), F32),
        pltpu.VMEM((cols, length), F32),
        pltpu.VMEM((2, max(keys, width), max(stacked, rows)), BF16),
        pltpu.VMEM((keys, length), F32),
        pltpu.VMEM((keys, length), F32),
        pltpu.VMEM((8, length), F32),
        pltpu.VMEM((rows, cols + ff), BF16),
        pltpu.VMEM((rows, edge), BF16),
        pltpu.VMEM((prompt, 2 * cols), F32),
        pltpu.VMEM((nc - 1, length, 2 * cols), BF16),
    ]
    scratch += [pltpu.VMEM((2, rows, width), BF16)] * 3
    scratch += [
        pltpu.VMEM((half, split, nc * own, part), BF16),
        pltpu.VMEM((half, split, nc * own, part), BF16),
        pltpu.VMEM((nc - 1, split, own, part), BF16),
        pltpu.VMEM((2, own, part), F32),
        pltpu.VMEM((2, part, own), F32),
        pltpu.VMEM((8, sums), F32),
        pltpu.VMEM((nf, 8, sums), F32),
        pltpu.VMEM((nc, 8, sums), F32),
        pltpu.VMEM((own, 128), F32),
        pltpu.VMEM((tp, own, 128), F32),
        dma((10,)),
        dma((2, nc, nf)),
        dma((5, 6)),
        dma((5, 6)),
        dma((5, nc, half)),
        dma((5, nc, half)),
        dma((6,)),
        dma((6,)),
        dma((nc - 1,)),
        dma((nc - 1,)),
        dma((2 * chunks,)),
        dma((2 * chunks,)),
        dma((2 * chunks,)),
        dma((2 * chunks,)),
        dma((2 * chunks,)),
        dma((half, split)),
        dma((half, split)),
        dma((nc - 1, split)),
        dma((nc - 1, split)),
        dma((2, max(half, nc - 1))),
        dma((2, max(half, nc - 1))),
        dma((tp - 1,)),
        dma((tp - 1,)),
        dma((2,)),
    ]
    return pl.pallas_call(
        functools.partial(layer_kernel, sizes),
        out_shape=shapes,
        in_specs=[smem, vmem] + [anywhere] * 8 + [vmem] * (len(operands) - 10),
        out_specs=(anywhere,) * 5 + (vmem,) * 3,
        scratch_shapes=scratch,
        compiler_params=pltpu.CompilerParams(
            collective_id=0, has_side_effects=True, vmem_limit_bytes=MEMORY
        ),
        name="layer",
    )(*operands)


def close_kernel(sizes, *refs):
    nc, own, cols, ff = sizes["nc"], sizes["own"], sizes["cols"], sizes["ff"]
    length, rows_all = sizes["length"], sizes["slots"] * sizes["length"]
    first, turned = 3 * cols, sizes["turned"]
    edge = first + ff
    refs = list(refs)

    def take(count):
        taken = refs[:count]
        del refs[:count]
        return taken

    totals, sums, norms = take(3)
    given = take(4)
    y_prompt, y_cont, dx_prompt, dx_cont, b_qkv, b_u = take(6)
    singles = take(0 if turned else 6)
    taken = take(4)
    tot_v, y_v, dx_v = take(3)
    held = take(4)
    in_sem, out_sem, held_sem = refs

    def at_rows(start, prompt, cont):
        if start < length:
            return prompt.at[pl.ds(start, BLOCK)]
        return cont.at[pl.ds(start - length, BLOCK)]

    loads, stores = [], []
    for i, start in enumerate(range(0, rows_all, BLOCK)):
        rows = pl.ds(start, BLOCK)
        pairs = tuple((totals.at[k, rows], tot_v.at[k, rows]) for k in range(2))
        loads.append(
            [pltpu.make_async_copy(a, b, in_sem.at[i, k]) for k, (a, b) in enumerate(pairs)]
        )
        pairs = (
            (y_v.at[rows], at_rows(start, y_prompt, y_cont)),
            (dx_v.at[rows], at_rows(start, dx_prompt, dx_cont)),
        )
        stores.append(
            [pltpu.make_async_copy(a, b, out_sem.at[i, k]) for k, (a, b) in enumerate(pairs)]
        )
    brought = [pltpu.make_async_copy(a, b, held_sem.at[0, i]) for i, (a, b) in enumerate(zip(given, held))]
    handed = [pltpu.make_async_copy(a, b, held_sem.at[1, i]) for i, (a, b) in enumerate(zip(held, taken))]
    for copies in loads[:2] + [brought] + loads[2:]:
        for copy in copies:
            copy.start()

    for i in range(3):
        b_qkv[i : i + 1, :] = sums[0:1, i * cols : (i + 1) * cols]
    b_u[...] = sums[0:1, first:edge]
    if not turned:
        for i in range(4):
            singles[i][...] = norms[i : i + 1, :]
        shard = lax.axis_index("fsdp") * nc + lax.axis_index("ctx")
        lanes = pl.ds(pl.multiple_of(edge + shard * own, own), own)
        singles[4][...] = sums[0:1, lanes]
        singles[5][...] = sums[0:1, lanes]

    for i, start in enumerate(range(0, rows_all, BLOCK)):
        rows = slice(start, start + BLOCK)
        for k, target in enumerate((y_v, dx_v)):
            loads[i][k].wait()
            target[rows, :] = tot_v[k, rows, :].astype(F32)
            stores[i][k].start()
        if i == 2:
            for back, on in zip(brought, handed):
                back.wait()
                on.start()
    for copies in stores + [handed]:
        for copy in copies:
            copy.wait()


def close_layer(sizes, *operands):
    own, ff, width, cols = sizes["own"], sizes["ff"], sizes["width"], sizes["cols"]
    length, rows = sizes["length"], sizes["slots"] * sizes["length"]
    blocks = rows // BLOCK

    def array(shape):
        return jax.ShapeDtypeStruct(shape, F32)

    kept = [(3, cols), (1, ff)] + ([] if sizes["turned"] else [(1, own)] * 6)
    given = [tuple(o.shape) for o in operands[3:]]
    anywhere = pl.BlockSpec(memory_space=pl.ANY)
    vmem = pl.BlockSpec(memory_space=pltpu.VMEM)
    large = [(length, width), (rows - length, width)] * 2
    return pl.pallas_call(
        functools.partial(close_kernel, sizes),
        in_specs=[anywhere] + [vmem] * 2 + [anywhere] * 4,
        out_specs=[anywhere] * 4 + [vmem] * len(kept) + [anywhere] * 4,
        out_shape=[array(shape) for shape in large + kept + given],
        scratch_shapes=[
            pltpu.VMEM((2, rows, width), BF16),
            pltpu.VMEM((rows, width), F32),
            pltpu.VMEM((rows, width), F32),
        ]
        + [pltpu.VMEM(shape, F32) for shape in given]
        + [
            pltpu.SemaphoreType.DMA((blocks, 2)),
            pltpu.SemaphoreType.DMA((blocks, 2)),
            pltpu.SemaphoreType.DMA((2, 4)),
        ],
        compiler_params=pltpu.CompilerParams(vmem_limit_bytes=62 * 1024 * 1024),
        name="close",
    )(*operands)


def on_device(
    x_prompt,
    x_cont,
    cont_start,
    w_qkv,
    qkv_bias,
    w_dense,
    dense_bias,
    w_fc1,
    fc1_bias,
    w_fc2,
    fc2_bias,
    ln1_gain,
    ln1_bias,
    ln2_gain,
    ln2_bias,
    dy_prompt,
    dy_cont,
):
    length = x_prompt.shape[1]
    conts, cont_len, width = x_cont.shape[1:]
    own, _, cols = w_qkv.shape
    ff = w_fc1.shape[1]
    nf, nc, tp = (lax.axis_size(name) for name in ("fsdp", "ctx", "tp"))
    edge = 3 * cols + ff
    part = 256 if edge % 256 == 0 and (cols + ff) % 256 == 0 else 128
    sizes = {
        "nf": nf,
        "nc": nc,
        "tp": tp,
        "own": own,
        "cols": cols,
        "ff": ff,
        "width": width,
        "length": length,
        "slots": 1 + conts,
        "total": 4 * cols + 2 * ff,
        "part": part,
        "pieces_one": edge // part,
        "pieces_two": (cols + ff) // part,
        "turned": own % 128 != 0,
    }
    turned = [w_dense.T, w_fc2.T] if sizes["turned"] else [w_dense, w_fc2]
    lane = np.arange(128) % HD
    inverse = 10000.0 ** (-2.0 * (lane % (ROT // 2)) / ROT)
    freq = np.zeros((8, 128), np.float32)
    freq[0] = np.where(lane < ROT, inverse, 0.0)
    freq[1] = np.where(lane < ROT // 2, -1.0, 1.0)
    vectors = [dense_bias, fc2_bias, ln1_gain, ln1_bias, ln2_gain, ln2_bias]
    if sizes["turned"]:
        stacked = jnp.pad(jnp.stack(vectors).astype(F32), ((0, 2), (0, 0)))
        vectors = [stacked, stacked.T]
    totals, d_q, d_d, d_u, d_o, sums, norms, _ = run_layer(
        sizes,
        cont_start,
        jnp.asarray(freq),
        x_prompt[0],
        x_cont.reshape(conts * cont_len, width),
        dy_prompt[0],
        dy_cont.reshape(conts * cont_len, width),
        w_qkv.transpose(1, 0, 2),
        turned[0],
        w_fc1,
        turned[1],
        *vectors,
        qkv_bias,
        fc1_bias,
    )
    closed = close_layer(
        sizes,
        totals,
        sums,
        norms,
        d_q,
        d_d,
        d_u,
        d_o,
    )
    y_prompt, y_cont, dx_prompt, dx_cont, b_qkv, b_u = closed[:6]
    d_qkv, d_dense, d_u, d_o = closed[-4:]
    if sizes["turned"]:
        d_dense, d_o = d_dense.T, d_o.T
        four = [norms[:, i] for i in range(4)]
        place = (lax.axis_index("fsdp") * nc + lax.axis_index("ctx")) * own
        shifts = [lax.dynamic_slice_in_dim(sums[0, edge:], place, own)] * 2
    else:
        *four, shift_one, shift_two = (row.reshape(own) for row in closed[6:12])
        shifts = [shift_one, shift_two]
    shape = x_cont.shape
    return (
        y_prompt[None],
        y_cont.reshape(shape),
        dx_prompt[None],
        dx_cont.reshape(shape),
        d_qkv.transpose(1, 0, 2),
        b_qkv,
        d_dense,
        shifts[0],
        d_u,
        b_u.reshape(ff),
        d_o,
        shifts[1],
        four[0],
        four[1],
        four[2],
        four[3],
    )


def solution(mesh):
    both = ("fsdp", "ctx")
    rows = P("fsdp", "ctx", None)
    conts = P("fsdp", "ctx", None, None)
    vector = P(both)
    return jax.shard_map(
        on_device,
        mesh=mesh,
        in_specs=(
            rows,
            conts,
            P("fsdp", "ctx"),
            P(both, None, "tp"),
            P(None, "tp"),
            P("tp", both),
            vector,
            P(both, "tp"),
            P("tp"),
            P("tp", both),
            vector,
            vector,
            vector,
            vector,
            vector,
            rows,
            conts,
        ),
        out_specs=(
            rows,
            conts,
            rows,
            conts,
            P(both, None, "tp"),
            P(None, "tp"),
            P("tp", both),
            vector,
            P(both, "tp"),
            P("tp"),
            P("tp", both),
            vector,
            vector,
            vector,
            vector,
            vector,
        ),
        check_vma=False,
    )
```

```python
import functools

import jax
import jax.numpy as jnp
import numpy as np
from jax import lax
from jax.experimental import pallas as pl
from jax.experimental.pallas import tpu as pltpu
from jax.sharding import PartitionSpec as P

HD = 64
ROT = 16
EPS = 1e-05
MASKED = -1e30
F32 = jnp.float32
BF16 = jnp.bfloat16
MESH = pl.DeviceIdType.MESH
CHUNK = 64
BLOCK = 256
MEMORY = 63 * 1024 * 1024
LAG = 2
PACE = 1
BEHIND = 3
ERF = (0.254829592, -0.284496736, 1.421413741, -1.453152027, 1.061405429)


def nn(left, right):
    return jnp.dot(left, right, preferred_element_type=F32)


def nt(left, right):
    return lax.dot_general(left, right, (((1,), (1,)), ((), ())), preferred_element_type=F32)


def remote(src, dst, send_sem, recv_sem, device):
    return pltpu.make_async_remote_copy(
        src_ref=src,
        dst_ref=dst,
        send_sem=send_sem,
        recv_sem=recv_sem,
        device_id=device,
        device_id_type=MESH,
    )


def turn(values, cos_t, sin_t):
    lane = lax.broadcasted_iota(jnp.int32, cos_t.shape, 1)
    low_half = lax.rem(lane, HD) < ROT // 2
    pieces = []
    for start in range(0, values.shape[1], 128):
        piece = values[:, start : start + 128]
        up = pltpu.roll(piece, 128 - ROT // 2, 1)
        down = pltpu.roll(piece, ROT // 2, 1)
        pieces.append(piece * cos_t + jnp.where(low_half, up, down) * sin_t)
    return jnp.concatenate(pieces, axis=1) if len(pieces) > 1 else pieces[0]


def layer_kernel(sizes, *refs):
    nf, nc, nt_axis = sizes["nf"], sizes["nc"], sizes["tp"]
    own, cols, ff, width = sizes["own"], sizes["cols"], sizes["ff"], sizes["width"]
    length, slots, total = sizes["length"], sizes["slots"], sizes["total"]
    part, pieces_one, pieces_two = sizes["part"], sizes["pieces_one"], sizes["pieces_two"]
    turned_in = sizes["turned"]
    refs = list(refs)

    def take(count):
        taken = refs[:count]
        del refs[:count]
        return taken

    starts, freq, x_prompt, x_cont, dy_prompt, dy_cont, w_q, w_d, w_u, w_o = take(10)
    vectors = take(1 if turned_in else 6)
    small_t = take(1)[0] if turned_in else None
    bias_q, bias_up = take(2)
    tot_out, dq_out, dd_out, du_out, do_out, sums_out, norms_out, small_out = take(8)
    xv, dyv, n_t, wall = take(4)
    stat_s, cos_s, sin_s, small, smallg, bias_u = take(6)
    kvp, k_t, v_t, q_t, g_t, o_t, dq_t, p_all, score_s, slope_s, share_s = take(11)
    oa, gd, acc, kv_recv = take(4)
    part_sum, from_out, from_in, half_send, half_recv, piece_recv, stage, stage_t = take(8)
    sum_own, sum_f, sum_c, norm_own, norm_in = take(5)
    in_sem, small_sem, ws, wr, fs, fr, kvs, kvr, gks, gkr = take(10)
    zs, za, zbs, zb, zo, hs, hr, ps, pr, ss, sr, ns, nr, os = take(14)
    f, c, t = lax.axis_index("fsdp"), lax.axis_index("ctx"), lax.axis_index("tp")
    heads = cols // HD
    rows_all = slots * length
    pair = slots // 2
    prompt = nc * length
    first = 3 * cols
    edge = first + ff
    shard = f * nc + c
    own_rows = pl.ds(pl.multiple_of(shard * own, own), own)

    def ctx_to(step):
        return (f, lax.rem(c + step, nc), t)

    def ctx_from(step):
        return lax.rem(c + nc - step, nc)

    across_x = c + 1 - 2 * lax.rem(c, 2)
    across_y = lax.rem(c + 2, nc)
    corner = lax.rem(across_x + 2, nc)
    peers = (c, across_x, across_y, corner)

    def mate_to(step):
        return (lax.rem(f + step, nf), c, t)

    def mate_from(step):
        return lax.rem(f + nf - step, nf)

    def tp_to(step):
        return (f, c, lax.rem(t + step, nt_axis))

    upper = lax.div(t, nt_axis // 2)
    inward = (f, c, t + 1 - 2 * upper)
    outward = (f, c, lax.rem(t - 1 + 2 * upper + nt_axis, nt_axis))
    at_end = (t == 0) | (t == nt_axis - 1)
    not_end = (t != 0) & (t != nt_axis - 1)
    in_middle = (t == nt_axis // 2 - 1) | (t == nt_axis // 2)
    not_middle = (t != nt_axis // 2 - 1) & (t != nt_axis // 2)

    loads = [
        (x_prompt, xv.at[pl.ds(0, length)]),
        (x_cont, xv.at[pl.ds(length, rows_all - length)]),
        (dy_prompt, dyv.at[pl.ds(0, length)]),
        (dy_cont, dyv.at[pl.ds(length, rows_all - length)]),
        (w_q.at[0], wall.at[own_rows, pl.ds(0, cols)]),
        (w_q.at[1], wall.at[own_rows, pl.ds(cols, cols)]),
        (w_q.at[2], wall.at[own_rows, pl.ds(2 * cols, cols)]),
        (w_u, wall.at[own_rows, pl.ds(first, ff)]),
    ]
    if turned_in:
        loads += [
            (w_d, wall.at[own_rows, pl.ds(edge, cols)]),
            (w_o, wall.at[own_rows, pl.ds(edge + cols, ff)]),
        ]
    else:
        loads += [
            (w_d, p_all.at[1, pl.ds(0, cols), pl.ds(0, own)]),
            (w_o, p_all.at[0, pl.ds(0, ff), pl.ds(0, own)]),
        ]
    loads = [pltpu.make_async_copy(src, dst, in_sem.at[i]) for i, (src, dst) in enumerate(loads)]
    for i in (4, 5, 6, 0, 8):
        loads[i].start()

    barrier = pltpu.get_barrier_semaphore()
    greeted = [ctx_to(k) for k in range(1, nc)]
    greeted += [mate_to(g) for g in range(1, nf)]
    greeted += [tp_to(k) for k in range(1, nt_axis)]
    for device in greeted:
        pl.semaphore_signal(barrier, inc=1, device_id=device, device_id_type=MESH)
    pl.semaphore_wait(barrier, len(greeted))

    spans = (
        (0, first),
        (edge, cols),
        (first, ff // 2),
        (first + ff // 2, ff // 2),
        (edge + cols, ff),
    )

    half_own = own // 2

    def block(owner, side, size):
        base = owner * size
        if side is None:
            return pl.ds(pl.multiple_of(base, size), size)
        return pl.ds(pl.multiple_of(base + side * (size // 2), size // 2), size // 2)

    routes = ((0, 0, 1), (0, 1, 2), (0, 1, 1), (0, 0, 2), (1, 0, 2), (2, 1, 1))
    lands = ((1, 0), (2, 1), (1, 1), (2, 0), (3, 0), (3, 1))

    def ctx_copy(route, source, target, size, send_sem, recv_sem):
        owner, side, to = routes[route]
        rows = block(peers[owner], side, size)
        src = source(owner, side, rows)
        return remote(src, target(rows), send_sem, recv_sem, (f, peers[to], t))

    def lanes_of(p):
        return pl.ds(spans[p][0], spans[p][1])

    def gather_copy(p, route):
        def place(rows):
            return wall.at[pl.ds(rows.start + f * nc * own, half_own), lanes_of(p)]

        return ctx_copy(
            route, lambda owner, side, rows: place(rows), place, own, ws.at[p, route], wr.at[p, route]
        )

    def mate_copy(p, peer, g):
        place = wall.at[block(f * nc + peers[peer], None, own), lanes_of(p)]
        return remote(
            place, place, fs.at[p, peer, g - 1], fr.at[p, peer, g - 1], mate_to(g)
        )

    def gather_start(p):
        for route in range(4):
            gather_copy(p, route).start()
        for g in range(1, nf):
            mate_copy(p, 0, g).start()

    def gather_relay(p):
        for arrived, route in ((0, 4), (1, 5)):
            gather_copy(p, arrived).wait_recv()
            gather_copy(p, route).start()

    def gather_pass(p):
        for peer, rest in ((1, (2,)), (2, (3,)), (3, (4, 5))):
            for route in rest:
                gather_copy(p, route).wait_recv()
            for g in range(1, nf):
                mate_copy(p, peer, g).start()

    def gather_finish(p):
        for peer in range(nc):
            for g in range(1, nf):
                mate_copy(p, peer, g).wait_recv()

    def gather_sent(p):
        for route in range(6):
            gather_copy(p, route).wait_send()
        for peer in range(nc):
            for g in range(1, nf):
                mate_copy(p, peer, g).wait_send()

    def small_copy(step, g):
        if g == 0:
            return remote(
                small, smallg.at[shard], small_sem.at[0, step, 0], small_sem.at[1, step, 0], ctx_to(step)
            )
        held = f * nc + ctx_from(step)
        src = small if step == 0 else smallg.at[held]
        return remote(
            src, smallg.at[held], small_sem.at[0, step, g], small_sem.at[1, step, g], mate_to(g)
        )

    if turned_in:
        small[...] = vectors[0][...]
    else:
        small[...] = jnp.zeros_like(small)
        for i, vector in enumerate(vectors):
            small[i : i + 1, :] = vector[...].astype(F32).reshape(1, own)
    bias_u[...] = bias_up[...].astype(F32).reshape(1, ff)
    for step in range(1, nc):
        small_copy(step, 0).start()
    for g in range(1, nf):
        small_copy(0, g).start()
    for i in (4, 5, 6):
        loads[i].wait()
    gather_start(0)
    for i in (7, 1):
        loads[i].start()
    loads[8].wait()
    if not turned_in:
        wall[own_rows, edge : edge + cols] = p_all[1, 0:cols, 0:own].astype(F32).T.astype(BF16)
    smallg[shard] = small[...]
    loads[7].wait()
    gather_relay(0)
    gather_start(1)
    gather_start(2)
    for i in (9, 2, 3):
        loads[i].start()

    loads[0].wait()
    loads[1].wait()

    def statistics(slot):
        rows = pl.ds(pl.multiple_of(slot * length, length), length)
        block_x = xv[rows, :].astype(F32)
        mean = jnp.mean(block_x, axis=1, keepdims=True)
        block_x = block_x - mean
        scale = lax.rsqrt(jnp.mean(block_x * block_x, axis=1, keepdims=True) + EPS)
        stat_s[rows, 0:1] = mean
        stat_s[rows, 1:2] = scale
        n_t[:, rows] = (block_x * scale).T.astype(BF16)
        before = starts[0, jnp.maximum(slot - 1, 0)]
        base = jnp.where(slot == 0, c * length, before)
        place = base + lax.broadcasted_iota(jnp.int32, (length, 128), 0)
        phase = place.astype(F32) * freq[0:1, :]
        cos_s[rows, :] = jnp.cos(phase)
        sin_s[rows, :] = jnp.sin(phase) * freq[1:2, :]

    def loop(low, high, body):
        lax.fori_loop(low, high, lambda i, carry: (body(i), carry)[1], 0)

    statistics(0)
    for step in range(1, nc):
        small_copy(step, 0).wait_recv()
        for g in range(1, nf):
            small_copy(step, g).start()
    gather_relay(1)
    statistics(1)
    gather_relay(2)
    gather_pass(0)
    loop(2, slots - 1, statistics)
    for step in range(nc):
        for g in range(1, nf):
            small_copy(step, g).wait_recv()
    parts = [smallg[i] for i in range(nf * nc)]
    small_out[...] = jnp.concatenate(parts, axis=1)
    gain_one, shift_one = small_out[2:3, :], small_out[3:4, :]
    gain_two, shift_two = small_out[4:5, :], small_out[5:6, :]

    def normed(rows, gain, shift):
        block = (xv[rows, :].astype(F32) - stat_s[rows, 0:1]) * stat_s[rows, 1:2]
        return (block * gain + shift).astype(BF16)

    gather_finish(0)

    def project(slot):
        rows = pl.ds(pl.multiple_of(slot * length, length), length)
        both = nn(normed(rows, gain_one, shift_one), wall[:, 0:first])
        cos_t, sin_t = cos_s[rows, :], sin_s[rows, :]
        query = both[:, 0:cols] + bias_q[0:1, :].astype(F32)
        key = both[:, cols : 2 * cols] + bias_q[1:2, :].astype(F32)
        value = both[:, 2 * cols : first] + bias_q[2:3, :].astype(F32)
        gd[rows, 0:cols] = (turn(query, cos_t, sin_t) * 0.125).astype(BF16)
        gd[rows, cols : 2 * cols] = turn(key, cos_t, sin_t).astype(BF16)
        gd[rows, 2 * cols : first] = value.astype(BF16)

    project(0)
    mine = pl.ds(pl.multiple_of(c * length, length), length)
    kvp[mine, :] = gd[0:length, cols:first]

    def kv_copy(route):
        def source(owner, side, rows):
            if owner == 0:
                return gd.at[pl.ds(side * (length // 2), length // 2), pl.ds(cols, 2 * cols)]
            return kvp.at[rows]

        return ctx_copy(
            route, source, lambda rows: kvp.at[rows], length, kvs.at[route], kvr.at[route]
        )

    for route in range(4):
        kv_copy(route).start()
    gather_pass(1)
    loads[9].wait()
    if not turned_in:
        wall[own_rows, edge + cols : total] = p_all[0, 0:ff, 0:own].astype(F32).T.astype(BF16)
    statistics(slots - 1)
    for arrived, route in ((0, 4), (1, 5)):
        kv_copy(arrived).wait_recv()
        kv_copy(route).start()
    gather_start(3)
    gather_start(4)
    loop(1, slots, project)
    gather_relay(3)
    gather_finish(1)
    gather_pass(2)
    loads[2].wait()
    loads[3].wait()

    def back_dense(slot):
        rows = pl.ds(pl.multiple_of(slot * length, length), length)
        block_dy = dyv[rows, :]
        oa[rows, 0:cols] = nn(block_dy, wall[:, edge : edge + cols]).astype(BF16)

    loop(0, slots, back_dense)

    for route in range(2, 6):
        kv_copy(route).wait_recv()
    k_t[:, 0:prompt] = kvp[0:prompt, 0:cols].astype(F32).T.astype(BF16)
    v_t[:, 0:prompt] = kvp[0:prompt, cols : 2 * cols].astype(F32).T.astype(BF16)

    def fold(block_of, combine):
        return combine(block_of.reshape(-1, 8, block_of.shape[1]), axis=0)

    def attend(slot, is_prompt, between=()):
        rows = pl.ds(pl.multiple_of(slot * length, length), length)
        span = prompt if is_prompt else prompt + length
        stacked = heads * length
        head_row = lax.div(lax.broadcasted_iota(jnp.int32, (cols, length), 0), HD)
        query = gd[rows, 0:cols].astype(F32).T.astype(BF16)
        grad = oa[rows, 0:cols].astype(F32).T.astype(BF16)
        zero = jnp.zeros_like(query)
        for h in range(heads):
            q_t[:, h * length : (h + 1) * length] = jnp.where(head_row == h, query, zero)
            g_t[:, h * length : (h + 1) * length] = jnp.where(head_row == h, grad, zero)
        key_at = lax.broadcasted_iota(jnp.int32, (length, length), 0)
        query_at = lax.broadcasted_iota(jnp.int32, (length, length), 1)
        if is_prompt:
            limit = query_at + (c * length + 1)
        else:
            kvp[prompt:span, :] = gd[rows, cols:first]
            k_t[:, prompt:span] = gd[rows, cols : 2 * cols].astype(F32).T.astype(BF16)
            v_t[:, prompt:span] = gd[rows, 2 * cols : first].astype(F32).T.astype(BF16)
            limit = starts[0, slot - 1]

        def lanes(h):
            return slice(h * length, (h + 1) * length)

        def lines(h):
            return slice(h * HD, (h + 1) * HD)

        def score(h):
            for b in range(0, span, length):
                keys = slice(b, b + length)
                score_s[keys, :] = nn(kvp[keys, 0:cols], q_t[:, lanes(h)])

        def slope(h):
            for b in range(0, span, length):
                keys = slice(b, b + length)
                slope_s[keys, :] = nn(kvp[keys, cols : 2 * cols], g_t[:, lanes(h)])

        def mask():
            highest = jnp.full((8, length), MASKED, F32)
            for b in range(0, span, length):
                seen = key_at + b < limit if b < prompt else key_at <= query_at
                scores = jnp.where(seen, score_s[b : b + length, :], MASKED)
                score_s[b : b + length, :] = scores
                highest = jnp.maximum(highest, fold(scores, jnp.max))
            return jnp.max(highest, axis=0, keepdims=True)

        def raise_up(h, highest):
            norm = jnp.zeros((8, length), F32)
            for b in range(0, span, length):
                raised = jnp.exp(score_s[b : b + length, :] - highest)
                norm = norm + fold(raised, jnp.sum)
                p_all[0, b : b + length, lanes(h)] = raised.astype(BF16)
            share = 1.0 / jnp.sum(norm, axis=0, keepdims=True)
            share_s[h : h + 1, :] = share
            return share

        score(0)
        slope(0)
        share = raise_up(0, mask())
        for h in range(heads):
            out_t = nn(v_t[lines(h), 0:span], p_all[0, 0:span, lanes(h)]) * share
            o_t[lines(h), :] = out_t
            if h + 1 < heads:
                score(h + 1)
            inner = jnp.sum(out_t * g_t[lines(h), lanes(h)].astype(F32), axis=0, keepdims=True)
            for b in range(0, span, length):
                raised = p_all[0, b : b + length, lanes(h)].astype(F32)
                low = (raised * (slope_s[b : b + length, :] - inner)).astype(BF16)
                p_all[1, b : b + length, lanes(h)] = low
            dq_t[lines(h), :] = nn(k_t[lines(h), 0:span], p_all[1, 0:span, lanes(h)]) * share
            if h + 1 < heads:
                slope(h + 1)
                share = raise_up(h + 1, mask())
            for at, action in between:
                if at == h:
                    action()
        for h in range(heads):
            share = share_s[h : h + 1, :]
            q_t[:, lanes(h)] = (q_t[:, lanes(h)].astype(F32) * share).astype(BF16)
            g_t[:, lanes(h)] = (g_t[:, lanes(h)].astype(F32) * share).astype(BF16)
        cos_t, sin_t = cos_s[rows, :], -sin_s[rows, :]
        oa[rows, 0:cols] = o_t[...].T.astype(BF16)
        gd[rows, 0:cols] = turn(dq_t[...].T * 0.125, cos_t, sin_t).astype(BF16)
        acc[:, 0:cols] += nt(p_all[1, 0:prompt, 0:stacked], q_t[...])
        acc[:, cols : 2 * cols] += nt(p_all[0, 0:prompt, 0:stacked], g_t[...])
        if not is_prompt:
            back_k = nt(p_all[1, prompt:span, 0:stacked], q_t[...])
            gd[rows, cols : 2 * cols] = turn(back_k, cos_t, sin_t).astype(BF16)
            gd[rows, 2 * cols : first] = nt(p_all[0, prompt:span, 0:stacked], g_t[...]).astype(BF16)

    def kv_send(step):
        return p_all.at[1, pl.ds((step - 1) * length, length), pl.ds(0, 2 * cols)]

    def back_kv_copy(step):
        return remote(
            kv_send(step), kv_recv.at[step - 1], gks.at[step - 1], gkr.at[step - 1], ctx_to(step)
        )

    chunks = rows_all // CHUNK
    per_slot = length // CHUNK

    def line(q):
        which, place = lax.div(q, chunks), lax.rem(q, chunks)
        slot = lax.rem(lax.div(place, per_slot) + 1, slots)
        inner = lax.rem(place, per_slot)
        return which, pl.ds(pl.multiple_of((slot * per_slot + inner) * CHUNK, CHUNK), CHUNK)

    def line_out(q, middle):
        which, rows = line(q)
        target = from_in if middle else from_out
        landed = zb if middle else za
        return remote(
            part_sum.at[which, rows], target.at[which, rows], zs.at[q], landed.at[q], inward
        )

    def line_home(q, middle):
        which, rows = line(q)
        src = from_out if middle else from_in
        return remote(
            src.at[which, rows], from_in.at[which, rows], zbs.at[q], zb.at[q], outward
        )

    def line_store(q):
        which, rows = line(q)
        return pltpu.make_async_copy(part_sum.at[which, rows], tot_out.at[which, rows], zo.at[q])

    def line_close(q, total_ref):
        which, rows = line(q)
        line_out(q, True).wait_send()
        got = total_ref[which, rows, :].astype(F32)

        @pl.when(which == 0)
        def _():
            whole = xv[rows, :].astype(F32) + got + (small_out[0:1, :] + small_out[1:2, :])
            part_sum[0, rows, :] = whole.astype(BF16)

        @pl.when(which == 1)
        def _():
            scale = stat_s[rows, 1:2]
            unit = (xv[rows, :].astype(F32) - stat_s[rows, 0:1]) * scale
            along = jnp.mean(got * unit, axis=1, keepdims=True)
            rest = got - jnp.mean(got, axis=1, keepdims=True) - unit * along
            part_sum[1, rows, :] = (dyv[rows, :].astype(F32) + scale * rest).astype(BF16)

        line_store(q).start()

    def line_send(q):
        @pl.when(in_middle)
        def _():
            line_out(q, True).start()

        @pl.when(not_middle)
        def _():
            line_out(q, False).start()

    def line_first(q):
        @pl.when(at_end)
        def _():
            line_send(q)

    def line_add(q):
        which, rows = line(q)

        @pl.when(not_end)
        def _():
            line_out(q, False).wait_recv()
            part_sum[which, rows, :] = (
                part_sum[which, rows, :].astype(F32) + from_out[which, rows, :].astype(F32)
            ).astype(BF16)
            line_send(q)

    def line_back(q):
        which, rows = line(q)

        @pl.when(in_middle)
        def _():
            line_out(q, True).wait_recv()
            from_out[which, rows, :] = (
                part_sum[which, rows, :].astype(F32) + from_in[which, rows, :].astype(F32)
            ).astype(BF16)

            @pl.when(not_end)
            def _():
                line_home(q, True).start()

            line_close(q, from_out)

        @pl.when(not_middle)
        def _():
            line_home(q, False).wait_recv()

            @pl.when(not_end)
            def _():
                line_home(q, False).start()

            line_close(q, from_in)

    def line_done(q):
        line_store(q).wait()

        @pl.when(not_end)
        def _():
            line_home(q, True).wait_send()

    def step_line(q):
        @pl.when(q < 2 * chunks)
        def _():
            line_add(q)

        @pl.when((q >= LAG) & not_end)
        def _():
            line_back(q - LAG)

    def tick(k):
        for i in range(PACE):
            step_line(k * PACE + i)

    def feed(position, halfway=None):
        slot = lax.rem(position + 1, slots)
        rows = pl.ds(pl.multiple_of(slot * length, length), length)
        inputs = normed(rows, gain_two, shift_two)
        for at in range(0, ff, ff // 2):
            units = slice(at, at + ff // 2)
            up = slice(first + at, first + at + ff // 2)
            hidden = nn(inputs, wall[:, up]) + bias_u[:, units]
            depth = jnp.abs(hidden) * np.float32(0.5**0.5)
            step = 1.0 / (1.0 + np.float32(0.3275911) * depth)
            poly = np.float32(ERF[4])
            for factor in ERF[3::-1]:
                poly = poly * step + np.float32(factor)
            bell = jnp.exp(-(depth * depth))
            tail = 0.5 * (poly * step) * bell
            below = jnp.where(hidden >= 0.0, 1.0 - tail, tail)
            oa[rows, cols + at : cols + at + ff // 2] = (hidden * below).astype(BF16)
            slope = below + hidden * (bell * np.float32((2.0 * np.pi) ** -0.5))
            for b in range(0, ff // 2, length):
                lines = slice(at + b, at + b + length)
                score_s[lines, :] = slope[:, b : b + length]
        part_sum[0, rows, :] = nt(oa[rows, :], wall[:, edge:total]).astype(BF16)
        for i in range(per_slot):
            line_first(position * per_slot + i)
        if halfway is not None:
            halfway()
        for at in range(0, ff, length):
            down = slice(edge + cols + at, edge + cols + at + length)
            back = nn(dyv[rows, :], wall[:, down])
            gd[rows, first + at : first + at + length] = (
                back * score_s[at : at + length, :]
            ).astype(BF16)

    def back_norms(position):
        slot = lax.rem(position + 1, slots)
        rows = pl.ds(pl.multiple_of(slot * length, length), length)
        toward_x = nt(gd[rows, 0:first], wall[:, 0:first]) * gain_one
        toward_x = toward_x + nt(gd[rows, first:edge], wall[:, first:edge]) * gain_two
        part_sum[1, rows, :] = toward_x.astype(BF16)
        for i in range(per_slot):
            line_first(chunks + position * per_slot + i)

    acc[...] = jnp.zeros_like(acc)

    def at_slot(slot, wanted, *steps):
        def action():
            @pl.when(slot == wanted)
            def _():
                for step in steps:
                    step()

        return action

    def attend_cont(slot):
        attend(
            slot,
            False,
            (
                (heads // 2, at_slot(slot, 1, lambda: gather_relay(4))),
                (heads // 2, at_slot(slot, pair, lambda: gather_pass(3))),
            ),
        )

    loop(1, pair + 1, attend_cont)
    gather_pass(4)
    for p in (2, 3, 4):
        gather_finish(p)
    loop(0, pair, feed)
    for slot in range(pair + 1, slots):
        attend(slot, False, ((1, lambda: tick(0)), (heads - 1, lambda: tick(1))))
        feed(slot - 1, lambda: tick(2))
    attend(0, True, ((0, lambda: tick(3)), (heads // 2, lambda: tick(4))))
    for step in range(1, nc):
        there = pl.ds(pl.multiple_of(lax.rem(c + step, nc) * length, length), length)
        kv_send(step)[...] = acc[there, :].astype(BF16)
        back_kv_copy(step).start()
    feed(slots - 1, lambda: tick(5))
    tick(6)
    loop(0, pair, back_norms)
    tick(7)
    loop(pair, slots - 1, back_norms)
    tick(8)

    def turn_dy(slot):
        rows = pl.ds(pl.multiple_of(slot * length, length), length)
        p_all[0, 0:width, rows] = dyv[rows, :].astype(F32).T.astype(BF16)

    loop(0, slots, turn_dy)
    tick(9)

    group = nc * own
    split = pieces_one + pieces_two

    def product(p, rows, second):
        lanes = pl.ds(pl.multiple_of(p * part, part), part)
        if second:
            return nn(p_all[0, rows, 0:rows_all], oa[:, lanes])
        return nn(n_t[rows, :], gd[:, lanes])

    def half_copy(p, g):
        return remote(
            half_send.at[g - 1, p], half_recv.at[g - 1, p], hs.at[g - 1, p], hr.at[g - 1, p], mate_to(g)
        )

    def piece_copy(p, step):
        rows = pl.ds(pl.multiple_of(lax.rem(c + step, nc) * own, own), own)
        return remote(
            half_recv.at[0, p, rows],
            piece_recv.at[step - 1, p],
            ps.at[step - 1, p],
            pr.at[step - 1, p],
            ctx_to(step),
        )

    def give_half(p, base, second):
        for g in range(1, nf):
            rows = pl.ds(pl.multiple_of(lax.rem(f + g, nf) * group, group), group)
            half_send[g - 1, p] = product(p - base, rows, second).astype(BF16)
            half_copy(p, g).start()

    def keep_half(p, base, second):
        rows = pl.ds(pl.multiple_of(f * group, group), group)
        kept = product(p - base, rows, second)
        for g in range(1, nf):
            half_copy(p, g).wait_recv()
            kept = kept + half_recv[g - 1, p].astype(F32)
        half_recv[0, p] = kept.astype(BF16)
        for step in range(1, nc):
            piece_copy(p, step).start()

    early = first // part

    def with_tick(body, start, lowest=0):
        def step(p):
            body(p)

            @pl.when((lax.rem(p, 3) == 2) & (p >= lowest))
            def _():
                tick(start + lax.div(p, 3))

        return step

    give_start, keep_start, lowest = 8, 10, 2 * early
    for start, body in ((give_start, give_half), (keep_start, keep_half)):
        one = with_tick(lambda p, body=body: body(p, 0, False), start, lowest)
        two = with_tick(lambda p, body=body: body(p, pieces_one, True), start, lowest)
        loop(early, pieces_one, one)
        loop(pieces_one, split, two)
    ticked = keep_start + split // 3

    for route in range(6):
        kv_copy(route).wait_send()
    grad_kv = acc[mine, :]
    for step in range(1, nc):
        back_kv_copy(step).wait_recv()
        grad_kv = grad_kv + kv_recv[step - 1].astype(F32)
    gd[0:length, cols : 2 * cols] = turn(
        grad_kv[:, 0:cols], cos_s[0:length, :], -sin_s[0:length, :]
    ).astype(BF16)
    gd[0:length, 2 * cols : first] = grad_kv[:, cols : 2 * cols].astype(BF16)
    back_norms(slots - 1)
    tick(ticked)
    loop(0, early, lambda p: give_half(p, 0, False))
    tick(ticked + 1)
    loop(0, early, lambda p: keep_half(p, 0, False))
    tick(ticked + 2)
    ticked += 3

    ones = jnp.ones((16, rows_all), BF16)
    sum_own[:, 0:edge] = nn(ones, gd[...])[0:8, :]
    sum_own[:, edge : edge + width] = nn(ones, dyv[...])[0:8, :]

    def sum_copy(step, g):
        if g:
            return remote(
                sum_own, sum_f.at[f], ss.at[0, g - 1], sr.at[0, g - 1], mate_to(g)
            )
        return remote(
            sum_own, sum_c.at[c], ss.at[1, step - 1], sr.at[1, step - 1], ctx_to(step)
        )

    sum_f[f] = sum_own[...]
    for g in range(1, nf):
        sum_copy(0, g).start()

    tick(ticked)
    tick(ticked + 1)
    for g in range(1, nf):
        sum_copy(0, g).wait_recv()
        sum_copy(0, g).wait_send()
    held = sum_f[0]
    for i in range(1, nf):
        held = held + sum_f[i]
    sum_own[...] = held
    sum_c[c] = held
    for step in range(1, nc):
        sum_copy(step, 0).start()
    loop(ticked + 2, ticked + 8, tick)
    ticked += 8
    for step in range(1, nc):
        sum_copy(step, 0).wait_recv()
        sum_copy(step, 0).wait_send()
    held = sum_c[0]
    for i in range(1, nc):
        held = held + sum_c[i]
    sums_out[...] = held

    lane = lax.broadcasted_iota(jnp.int32, (own, 128), 1)
    norm_own[...] = jnp.zeros_like(norm_own)

    columns = small_t[...] if turned_in else small[...].T

    def stored(p, out, base, across):
        slot = lax.rem(p, 2)
        at = pl.ds(pl.multiple_of((p - base) * part, part), part)
        if across:
            return pltpu.make_async_copy(stage.at[slot], out.at[:, at], os.at[slot])
        return pltpu.make_async_copy(stage_t.at[slot], out.at[at], os.at[slot])

    def stage_done(p):
        slot = lax.rem(p, 2)
        pltpu.make_async_copy(stage.at[slot], du_out.at[:, pl.ds(0, part)], os.at[slot]).wait()

    def q_stored(p):
        per = cols // part
        slot = lax.rem(p, 2)
        at = pl.ds(pl.multiple_of(lax.rem(p, per) * part, part), part)
        return pltpu.make_async_copy(stage.at[slot], dq_out.at[lax.div(p, per), :, at], os.at[slot])

    def settle(p, copy_of, group_at):
        rows = pl.ds(pl.multiple_of(c * own, own), own)
        lanes = pl.ds(pl.multiple_of(p * part, part), part)
        kept = half_recv[0, p, rows, :].astype(F32)
        for step in range(1, nc):
            piece_copy(p, step).wait_recv()
            kept = kept + piece_recv[step - 1, p].astype(F32)

        @pl.when((p != early) & (p != early + 1))
        def _():
            stage_done(p)

        if group_at is None:
            if turned_in:
                stage[lax.rem(p, 2)] = kept
            else:
                stage_t[lax.rem(p, 2)] = kept.T
        else:
            weights = wall[own_rows, lanes].astype(F32)
            column = sums_out[0:1, lanes]
            moment = jnp.sum(kept * weights, axis=1, keepdims=True)
            against = jnp.sum(weights * column, axis=1, keepdims=True)
            norm_own[...] += jnp.where(
                lane == 2 * group_at, moment, jnp.where(lane == 2 * group_at + 1, against, 0.0)
            )
            at = 2 + 2 * group_at
            gain, shift = columns[:, at : at + 1], columns[:, at + 1 : at + 2]
            stage[lax.rem(p, 2)] = kept * gain + shift * column
        copy_of(p).start()

    dense_end = pieces_one + cols // part
    orders = (
        (early, pieces_one, lambda q: stored(q, du_out, early, True), 1),
        (pieces_one, dense_end, lambda q: stored(q, dd_out, pieces_one, turned_in), None),
        (dense_end, split, lambda q: stored(q, do_out, dense_end, turned_in), None),
        (0, early, q_stored, 0),
    )
    settled = ticked - early // 3
    for low, high, copy_of, group_at in orders:
        start = settled if low else settled + split // 3
        loop(
            low,
            high,
            with_tick(functools.partial(settle, copy_of=copy_of, group_at=group_at), start),
        )
    ticked += split // 3
    norm_in[t] = norm_own[...]

    def norm_copy(k):
        return remote(norm_own, norm_in.at[t], ns.at[k - 1], nr.at[k - 1], tp_to(k))

    for k in range(1, nt_axis):
        norm_copy(k).start()

    for p in range(5):
        gather_sent(p)
    for step in range(1, nc):
        small_copy(step, 0).wait_send()
        back_kv_copy(step).wait_send()
    for step in range(nc):
        for g in range(1, nf):
            small_copy(step, g).wait_send()

    def sent(p):
        for g in range(1, nf):
            half_copy(p, g).wait_send()
        for step in range(1, nc):
            piece_copy(p, step).wait_send()

    loop(0, split, sent)

    def finish_line(q):
        step_line(q)

        @pl.when(at_end)
        def _():
            line_back(q - LAG)

        line_done(q - BEHIND - LAG)

    @pl.when(at_end)
    def _():
        loop(0, ticked * PACE - LAG, line_back)

    loop(0, ticked * PACE - BEHIND - LAG, line_done)
    loop(ticked * PACE, 2 * chunks + LAG, finish_line)

    for k in range(1, nt_axis):
        norm_copy(k).wait_recv()
        norm_copy(k).wait_send()
    held = norm_in[0]
    for i in range(1, nt_axis):
        held = held + norm_in[i]
    norms_out[...] = held if turned_in else held.T[0:8, :]

    loop(2 * chunks - BEHIND, 2 * chunks, line_done)
    stage_done(split - 2)
    stage_done(split - 1)


def run_layer(sizes, *operands):
    nf, nc, tp = sizes["nf"], sizes["nc"], sizes["tp"]
    own, cols, ff, width = sizes["own"], sizes["cols"], sizes["ff"], sizes["width"]
    length, slots, total = sizes["length"], sizes["slots"], sizes["total"]
    part, split = sizes["part"], sizes["pieces_one"] + sizes["pieces_two"]
    rows = slots * length
    prompt = nc * length
    stacked = cols // HD * length
    edge = 3 * cols + ff
    chunks = rows // CHUNK
    sums = edge + width
    anywhere = pl.BlockSpec(memory_space=pl.ANY)
    vmem = pl.BlockSpec(memory_space=pltpu.VMEM)
    smem = pl.BlockSpec(memory_space=pltpu.SMEM)
    dma = pltpu.SemaphoreType.DMA
    shapes = (
        jax.ShapeDtypeStruct((2, rows, width), BF16),
        jax.ShapeDtypeStruct((3, own, cols), F32),
        jax.ShapeDtypeStruct((own, cols) if sizes["turned"] else (cols, own), F32),
        jax.ShapeDtypeStruct((own, ff), F32),
        jax.ShapeDtypeStruct((own, ff) if sizes["turned"] else (ff, own), F32),
        jax.ShapeDtypeStruct((8, sums), F32),
        jax.ShapeDtypeStruct((own, 128) if sizes["turned"] else (8, own), F32),
        jax.ShapeDtypeStruct((8, width), F32),
    )
    half = nf - 1
    keys = prompt + length
    scratch = [
        pltpu.VMEM((rows, width), BF16),
        pltpu.VMEM((rows, width), BF16),
        pltpu.VMEM((width, rows), BF16),
        pltpu.VMEM((width, total), BF16),
        pltpu.VMEM((rows, 2), F32),
        pltpu.VMEM((rows, 128), F32),
        pltpu.VMEM((rows, 128), F32),
        pltpu.VMEM((8, own), F32),
        pltpu.VMEM((nf * nc, 8, own), F32),
        pltpu.VMEM((1, ff), F32),
        pltpu.VMEM((keys, 2 * cols), BF16),
        pltpu.VMEM((cols, keys), BF16),
        pltpu.VMEM((cols, keys), BF16),
        pltpu.VMEM((cols, stacked), BF16),
        pltpu.VMEM((cols, stacked), BF16),
        pltpu.VMEM((cols, length), F32),
        pltpu.VMEM((cols, length), F32),
        pltpu.VMEM((2, max(keys, width), max(stacked, rows)), BF16),
        pltpu.VMEM((keys, length), F32),
        pltpu.VMEM((keys, length), F32),
        pltpu.VMEM((8, length), F32),
        pltpu.VMEM((rows, cols + ff), BF16),
        pltpu.VMEM((rows, edge), BF16),
        pltpu.VMEM((prompt, 2 * cols), F32),
        pltpu.VMEM((nc - 1, length, 2 * cols), BF16),
    ]
    scratch += [pltpu.VMEM((2, rows, width), BF16)] * 3
    scratch += [
        pltpu.VMEM((half, split, nc * own, part), BF16),
        pltpu.VMEM((half, split, nc * own, part), BF16),
        pltpu.VMEM((nc - 1, split, own, part), BF16),
        pltpu.VMEM((2, own, part), F32),
        pltpu.VMEM((2, part, own), F32),
        pltpu.VMEM((8, sums), F32),
        pltpu.VMEM((nf, 8, sums), F32),
        pltpu.VMEM((nc, 8, sums), F32),
        pltpu.VMEM((own, 128), F32),
        pltpu.VMEM((tp, own, 128), F32),
        dma((10,)),
        dma((2, nc, nf)),
        dma((5, 6)),
        dma((5, 6)),
        dma((5, nc, half)),
        dma((5, nc, half)),
        dma((6,)),
        dma((6,)),
        dma((nc - 1,)),
        dma((nc - 1,)),
        dma((2 * chunks,)),
        dma((2 * chunks,)),
        dma((2 * chunks,)),
        dma((2 * chunks,)),
        dma((2 * chunks,)),
        dma((half, split)),
        dma((half, split)),
        dma((nc - 1, split)),
        dma((nc - 1, split)),
        dma((2, max(half, nc - 1))),
        dma((2, max(half, nc - 1))),
        dma((tp - 1,)),
        dma((tp - 1,)),
        dma((2,)),
    ]
    return pl.pallas_call(
        functools.partial(layer_kernel, sizes),
        out_shape=shapes,
        in_specs=[smem, vmem] + [anywhere] * 8 + [vmem] * (len(operands) - 10),
        out_specs=(anywhere,) * 5 + (vmem,) * 3,
        scratch_shapes=scratch,
        compiler_params=pltpu.CompilerParams(
            collective_id=0, has_side_effects=True, vmem_limit_bytes=MEMORY
        ),
        name="layer",
    )(*operands)


def close_kernel(sizes, *refs):
    nc, own, cols, ff = sizes["nc"], sizes["own"], sizes["cols"], sizes["ff"]
    length, rows_all = sizes["length"], sizes["slots"] * sizes["length"]
    first, turned = 3 * cols, sizes["turned"]
    edge = first + ff
    refs = list(refs)

    def take(count):
        taken = refs[:count]
        del refs[:count]
        return taken

    totals, sums, norms = take(3)
    given = take(4)
    y_prompt, y_cont, dx_prompt, dx_cont, b_qkv, b_u = take(6)
    singles = take(0 if turned else 6)
    taken = take(4)
    tot_v, y_v, dx_v = take(3)
    held = take(4)
    in_sem, out_sem, held_sem = refs

    def at_rows(start, prompt, cont):
        if start < length:
            return prompt.at[pl.ds(start, BLOCK)]
        return cont.at[pl.ds(start - length, BLOCK)]

    loads, stores = [], []
    for i, start in enumerate(range(0, rows_all, BLOCK)):
        rows = pl.ds(start, BLOCK)
        pairs = tuple((totals.at[k, rows], tot_v.at[k, rows]) for k in range(2))
        loads.append(
            [pltpu.make_async_copy(a, b, in_sem.at[i, k]) for k, (a, b) in enumerate(pairs)]
        )
        pairs = (
            (y_v.at[rows], at_rows(start, y_prompt, y_cont)),
            (dx_v.at[rows], at_rows(start, dx_prompt, dx_cont)),
        )
        stores.append(
            [pltpu.make_async_copy(a, b, out_sem.at[i, k]) for k, (a, b) in enumerate(pairs)]
        )
    brought = [pltpu.make_async_copy(a, b, held_sem.at[0, i]) for i, (a, b) in enumerate(zip(given, held))]
    handed = [pltpu.make_async_copy(a, b, held_sem.at[1, i]) for i, (a, b) in enumerate(zip(held, taken))]
    for copies in loads[:2] + [brought] + loads[2:]:
        for copy in copies:
            copy.start()

    for i in range(3):
        b_qkv[i : i + 1, :] = sums[0:1, i * cols : (i + 1) * cols]
    b_u[...] = sums[0:1, first:edge]
    if not turned:
        for i in range(4):
            singles[i][...] = norms[i : i + 1, :]
        shard = lax.axis_index("fsdp") * nc + lax.axis_index("ctx")
        lanes = pl.ds(pl.multiple_of(edge + shard * own, own), own)
        singles[4][...] = sums[0:1, lanes]
        singles[5][...] = sums[0:1, lanes]

    for i, start in enumerate(range(0, rows_all, BLOCK)):
        rows = slice(start, start + BLOCK)
        for k, target in enumerate((y_v, dx_v)):
            loads[i][k].wait()
            target[rows, :] = tot_v[k, rows, :].astype(F32)
            stores[i][k].start()
        if i == 2:
            for back, on in zip(brought, handed):
                back.wait()
                on.start()
    for copies in stores + [handed]:
        for copy in copies:
            copy.wait()


def close_layer(sizes, *operands):
    own, ff, width, cols = sizes["own"], sizes["ff"], sizes["width"], sizes["cols"]
    length, rows = sizes["length"], sizes["slots"] * sizes["length"]
    blocks = rows // BLOCK

    def array(shape):
        return jax.ShapeDtypeStruct(shape, F32)

    kept = [(3, cols), (1, ff)] + ([] if sizes["turned"] else [(1, own)] * 6)
    given = [tuple(o.shape) for o in operands[3:]]
    anywhere = pl.BlockSpec(memory_space=pl.ANY)
    vmem = pl.BlockSpec(memory_space=pltpu.VMEM)
    large = [(length, width), (rows - length, width)] * 2
    return pl.pallas_call(
        functools.partial(close_kernel, sizes),
        in_specs=[anywhere] + [vmem] * 2 + [anywhere] * 4,
        out_specs=[anywhere] * 4 + [vmem] * len(kept) + [anywhere] * 4,
        out_shape=[array(shape) for shape in large + kept + given],
        scratch_shapes=[
            pltpu.VMEM((2, rows, width), BF16),
            pltpu.VMEM((rows, width), F32),
            pltpu.VMEM((rows, width), F32),
        ]
        + [pltpu.VMEM(shape, F32) for shape in given]
        + [
            pltpu.SemaphoreType.DMA((blocks, 2)),
            pltpu.SemaphoreType.DMA((blocks, 2)),
            pltpu.SemaphoreType.DMA((2, 4)),
        ],
        compiler_params=pltpu.CompilerParams(vmem_limit_bytes=62 * 1024 * 1024),
        name="close",
    )(*operands)


def on_device(
    x_prompt,
    x_cont,
    cont_start,
    w_qkv,
    qkv_bias,
    w_dense,
    dense_bias,
    w_fc1,
    fc1_bias,
    w_fc2,
    fc2_bias,
    ln1_gain,
    ln1_bias,
    ln2_gain,
    ln2_bias,
    dy_prompt,
    dy_cont,
):
    length = x_prompt.shape[1]
    conts, cont_len, width = x_cont.shape[1:]
    own, _, cols = w_qkv.shape
    ff = w_fc1.shape[1]
    nf, nc, tp = (lax.axis_size(name) for name in ("fsdp", "ctx", "tp"))
    edge = 3 * cols + ff
    part = 256 if edge % 256 == 0 and (cols + ff) % 256 == 0 else 128
    sizes = {
        "nf": nf,
        "nc": nc,
        "tp": tp,
        "own": own,
        "cols": cols,
        "ff": ff,
        "width": width,
        "length": length,
        "slots": 1 + conts,
        "total": 4 * cols + 2 * ff,
        "part": part,
        "pieces_one": edge // part,
        "pieces_two": (cols + ff) // part,
        "turned": own % 128 != 0,
    }
    turned = [w_dense.T, w_fc2.T] if sizes["turned"] else [w_dense, w_fc2]
    lane = np.arange(128) % HD
    inverse = 10000.0 ** (-2.0 * (lane % (ROT // 2)) / ROT)
    freq = np.zeros((8, 128), np.float32)
    freq[0] = np.where(lane < ROT, inverse, 0.0)
    freq[1] = np.where(lane < ROT // 2, -1.0, 1.0)
    vectors = [dense_bias, fc2_bias, ln1_gain, ln1_bias, ln2_gain, ln2_bias]
    if sizes["turned"]:
        stacked = jnp.pad(jnp.stack(vectors).astype(F32), ((0, 2), (0, 0)))
        vectors = [stacked, stacked.T]
    totals, d_q, d_d, d_u, d_o, sums, norms, _ = run_layer(
        sizes,
        cont_start,
        jnp.asarray(freq),
        x_prompt[0],
        x_cont.reshape(conts * cont_len, width),
        dy_prompt[0],
        dy_cont.reshape(conts * cont_len, width),
        w_qkv.transpose(1, 0, 2),
        turned[0],
        w_fc1,
        turned[1],
        *vectors,
        qkv_bias,
        fc1_bias,
    )
    closed = close_layer(
        sizes,
        totals,
        sums,
        norms,
        d_q,
        d_d,
        d_u,
        d_o,
    )
    y_prompt, y_cont, dx_prompt, dx_cont, b_qkv, b_u = closed[:6]
    d_qkv, d_dense, d_u, d_o = closed[-4:]
    if sizes["turned"]:
        d_dense, d_o = d_dense.T, d_o.T
        four = [norms[:, i] for i in range(4)]
        place = (lax.axis_index("fsdp") * nc + lax.axis_index("ctx")) * own
        shifts = [lax.dynamic_slice_in_dim(sums[0, edge:], place, own)] * 2
    else:
        *four, shift_one, shift_two = (row.reshape(own) for row in closed[6:12])
        shifts = [shift_one, shift_two]
    shape = x_cont.shape
    return (
        y_prompt[None],
        y_cont.reshape(shape),
        dx_prompt[None],
        dx_cont.reshape(shape),
        d_qkv.transpose(1, 0, 2),
        b_qkv,
        d_dense,
        shifts[0],
        d_u,
        b_u.reshape(ff),
        d_o,
        shifts[1],
        four[0],
        four[1],
        four[2],
        four[3],
    )


def solution(mesh):
    both = ("fsdp", "ctx")
    rows = P("fsdp", "ctx", None)
    conts = P("fsdp", "ctx", None, None)
    vector = P(both)
    return jax.shard_map(
        on_device,
        mesh=mesh,
        in_specs=(
            rows,
            conts,
            P("fsdp", "ctx"),
            P(both, None, "tp"),
            P(None, "tp"),
            P("tp", both),
            vector,
            P(both, "tp"),
            P("tp"),
            P("tp", both),
            vector,
            vector,
            vector,
            vector,
            vector,
            rows,
            conts,
        ),
        out_specs=(
            rows,
            conts,
            rows,
            conts,
            P(both, None, "tp"),
            P(None, "tp"),
            P("tp", both),
            vector,
            P(both, "tp"),
            P("tp"),
            P("tp", both),
            vector,
            vector,
            vector,
            vector,
            vector,
        ),
        check_vma=False,
    )
```
